32 devices in a mesh: grid: 8 (over y, x, core), ao: 4 (over z).
Axes of the slice: x: 2, y: 2, z: 4, core: 2. Of those that a mesh axis runs over, the one named last changes fastest.
Arguments:
- trial: bfloat16 [12288, 16, 2, 128], P('ao'), may hold values from -0.15625 to 0.15625
- occupied: bfloat16 [12288, 2, 128], P('ao'), may hold values from -0.15625 to 0.15625
- colloc: bfloat16 [32, 128, 1536], P('grid'), may hold values from -3 to 3
- blocks: int32 [32, 12], P('grid'), may hold values from 0 to 95, as said below
- coords: float32 [32, 3, 128], P('grid'), may hold values from 0 to 4
- weights: float32 [32, 128], P('grid'), may hold values from 0.02 to 0.2
Outputs:
- exchange: float32 [16, 12288, 2, 128], P('ao', 'grid')
The draws below stay inside these ranges and needn't reach their ends.
Inputs may be any that keep to these rules, and one draw needn't show every extreme that they name: The 12 blocks of a batch are distinct and lie among 24 cyclically consecutive shell blocks.
All inputs are finite; a program needn't handle non-finite values.
Results may differ from the reference program's by a relative error of at most 0.0053.
Values may be sent and summed in bfloat16 or wider, within the bound.
No kernel may reach another device: no remote copies, remote signals or barrier semaphores. Data moves between devices by JAX's collectives and lax.ppermute only.
A program may use at most 192 MiB of HBM per device.

```python
import math
import jax
import jax.numpy as jnp
from jax import lax

BLK = 128
NBLK = 96
NVEC = 16
NOCC = 128
P_SIZE = 128
SIG = 12
NBATCH = 32
NAO = 12288


def draw_blocks(key, part):
    centers = jax.random.randint(key, (NBATCH,), 0, NBLK)
    batch_keys = jax.random.split(jax.random.fold_in(key, 7), NBATCH)
    offsets = jax.vmap(lambda one_key: jax.random.permutation(one_key, 2 * SIG)[:SIG])(batch_keys)
    return ((centers[:, None] + offsets) % NBLK).astype(jnp.int32)


def block_levels(rng, dims, pieces, low, largest):
    def one(position, parts):
        steps = jax.random.uniform(jax.random.fold_in(jax.random.fold_in(rng, 6), position), (parts,), jnp.float32, low / len(pieces), largest / len(pieces))
        return jnp.repeat(jnp.exp(steps), dims[position] // parts).reshape((-1,) + (1,) * (len(dims) - position - 1))

    gain = one(*pieces[0])
    for cut in pieces[1:]:
        gain = gain * one(*cut)
    return gain


def normal_values(own_key, dims, deviation, bound, shards=(), held_as=jnp.bfloat16):
    gain = block_levels(own_key, dims, shards, -0.22, 0.18) if shards else 1.0
    values = jax.random.normal(own_key, dims, jnp.float32) * deviation * gain
    return jnp.minimum(jnp.maximum(values, -bound), bound).astype(held_as)


def setup_inputs(seed: int = 0) -> dict:
    streams_of = jax.random.split(jax.random.key(seed), 7)
    return {
        "trial": normal_values(streams_of[0], (NAO, NVEC, 2, NOCC), (SIG * BLK) ** -0.5, 0.15625, ((0, 4),)),
        "occupied": normal_values(streams_of[1], (NAO, 2, NOCC), (SIG * BLK) ** -0.5, 0.15625, ((0, 4),)),
        "colloc": normal_values(streams_of[2], (NBATCH, P_SIZE, SIG * BLK), 0.5, 3.0, ((0, 8),)),
        "blocks": draw_blocks(jax.random.fold_in(streams_of[6], 71), 0),
        "coords": jnp.clip(4.0 * jax.random.uniform(streams_of[4], (NBATCH, 3, P_SIZE), jnp.float32) ** block_levels(streams_of[4], (NBATCH, 3, P_SIZE), ((0, 8),), -0.2, 0.2), 0.0, 4.0),
        "weights": jnp.clip(jnp.exp(math.log(0.2) - 2.3025851 * jax.random.uniform(streams_of[5], (NBATCH, P_SIZE), jnp.float32) ** block_levels(streams_of[5], (NBATCH, P_SIZE), ((0, 8),), -0.2, 0.2)), 0.02, 0.2),
    }


def kernel_matrix(points, quad):
    differ = points[:, :, None] - points[:, None, :]
    square = lax.optimization_barrier(jnp.sum(differ * differ, axis=0))
    return quad[:, None] * quad[None, :] / jnp.sqrt(square + 0.25)

def pair_exchange(lg_half, og_half, kernel):
    lreal = lg_half[:, :, 0].astype(jnp.float32)
    limag = lg_half[:, :, 1].astype(jnp.float32)
    oreal = og_half[:, 0].astype(jnp.float32)
    oimag = og_half[:, 1].astype(jnp.float32)
    rho_real = jnp.einsum('gvi,hi->vgh', lreal, oreal) + jnp.einsum('gvi,hi->vgh', limag, oimag)
    rho_imag = jnp.einsum('gvi,hi->vgh', limag, oreal) - jnp.einsum('gvi,hi->vgh', lreal, oimag)
    m_real = (rho_real * kernel[None]).astype(jnp.bfloat16).astype(jnp.float32)
    m_imag = (rho_imag * kernel[None]).astype(jnp.bfloat16).astype(jnp.float32)
    e_real = jnp.einsum('vgh,hj->gvj', m_real, oreal) - jnp.einsum('vgh,hj->gvj', m_imag, oimag)
    e_imag = jnp.einsum('vgh,hj->gvj', m_real, oimag) + jnp.einsum('vgh,hj->gvj', m_imag, oreal)
    return jnp.stack([e_real, e_imag], axis=2).astype(jnp.bfloat16)

def reference(trial, occupied, colloc, blocks, coords, weights):
    width = NVEC * 2 * NOCC
    combined = jnp.concatenate([trial.reshape(NAO, width), occupied.reshape(NAO, 2 * NOCC)], axis=1)
    combined = combined.reshape(NBLK, BLK, width + 2 * NOCC)

    def one_batch(running, batch_items):
        values, block_ids, points, quad = batch_items
        picked = combined[block_ids].reshape(SIG * BLK, width + 2 * NOCC)
        dens = jnp.dot(values, picked, preferred_element_type=jnp.float32)
        lg_half = dens[:, :width].reshape(P_SIZE, NVEC, 2, NOCC).astype(jnp.bfloat16)
        og_half = dens[:, width:].reshape(P_SIZE, 2, NOCC).astype(jnp.bfloat16)
        potential = pair_exchange(lg_half, og_half, kernel_matrix(points, quad))
        contrib = jnp.dot(values.T, potential.reshape(P_SIZE, width), preferred_element_type=jnp.float32)
        running = running.at[block_ids].add(contrib.reshape(SIG, BLK, width))
        return (running, None)
    panel, _ = lax.scan(one_batch, jnp.zeros((NBLK, BLK, width), jnp.float32), (colloc, blocks, coords, weights))
    return panel.reshape(NAO, NVEC, 2, NOCC).transpose(1, 0, 2, 3)
```

```python
import functools

import jax
import jax.numpy as jnp
from jax import lax
from jax.experimental import pallas as pl
from jax.experimental.pallas import tpu as pltpu
from jax.sharding import PartitionSpec as P

F32 = jnp.float32
BF16 = jnp.bfloat16
ID_ROWS = 16
NBUF = 3
VMEM_LIMIT = 56 * 1024 * 1024


def kernel_matrix(points, quad):
    differ = points[:, :, None, :] - points[:, :, :, None]
    square = jnp.sum(differ * differ, axis=1)
    return quad[:, :, None] * quad[:, None, :] / jnp.sqrt(square + 0.25)


def spec(space):
    return pl.BlockSpec(memory_space=space)


def density_kernel(sizes, ids, meta, trial, occupied, values, keep, send, todo, rows, acc, acc_occ, sems):
    first, count, sig, blk, nvec, nv, nlocal = sizes
    npts = values.shape[1]
    nocc = rows.shape[-1]
    base = meta[0]
    parity = meta[1]
    n = jnp.int32(0)
    for b in range(count):
        for s in range(sig):
            local = ids[first + b, s] - base
            todo[0, n] = local
            todo[1, n] = b
            todo[2, n] = s
            n = n + ((local >= 0) & (local < nlocal)).astype(jnp.int32)

    def copies(j):
        slot = lax.rem(j, NBUF)
        start = todo[0, j] * blk
        out = [
            pltpu.make_async_copy(trial.at[pl.ds(start, blk), v], rows.at[slot, v], sems.at[slot, v])
            for v in range(nvec)
        ]
        out.append(pltpu.make_async_copy(occupied.at[pl.ds(start, blk)], rows.at[slot, nvec], sems.at[slot, nvec]))
        return out

    def fetch(j):
        @pl.when(j < n)
        def _():
            for c in copies(j):
                c.start()

    for j in range(NBUF - 1):
        fetch(jnp.int32(j))
    acc[...] = jnp.zeros_like(acc)
    acc_occ[...] = jnp.zeros_like(acc_occ)
    ao = lax.broadcasted_iota(jnp.int32, (blk, 2 * blk), 0)
    col = lax.broadcasted_iota(jnp.int32, (blk, 2 * blk), 1)
    spread = [(col == 2 * ao + c).astype(F32).astype(BF16) for c in range(2)]

    def step(j, carry):
        slot = lax.rem(j, NBUF)
        b = todo[1, j]
        start = pl.multiple_of(todo[2, j] * blk, blk)
        x = values[b, :, pl.ds(start, blk)]
        both = jnp.concatenate(
            [jnp.dot(x, spread[c], preferred_element_type=F32).astype(BF16) for c in range(2)], axis=0
        )
        fetch(j + NBUF - 1)
        waits = copies(j)
        for pair in range(nvec // 2):
            waits[2 * pair].wait()
            waits[2 * pair + 1].wait()
            two = jnp.concatenate([rows[slot, 2 * pair + k].reshape(2 * blk, nocc) for k in range(2)], axis=1)
            acc[b, pair] += jnp.dot(both, two, preferred_element_type=F32)
        waits[nvec].wait()
        acc_occ[b] += jnp.dot(both, rows[slot, nvec].reshape(2 * blk, nocc), preferred_element_type=F32)
        return carry

    lax.fori_loop(0, n, step, 0)
    nkeep = nvec // nv // 2
    for b in range(count):
        for q in range(nkeep):
            for half in range(nv // 2):
                for ref, bit in ((keep, parity), (send, 1 - parity)):
                    part = acc[b, (2 * q + bit) * (nv // 2) + half]
                    for k in range(2):
                        for c in range(2):
                            piece = part[c * npts : (c + 1) * npts, k * nocc : (k + 1) * nocc]
                            ref[b, q * nv + 2 * half + k, c] = piece.astype(ref.dtype)
        for ref in (keep, send):
            for c in range(2):
                ref[b, nkeep * nv, c] = acc_occ[b, c * npts : (c + 1) * npts].astype(ref.dtype)


def density(trial, occupied, colloc, blocks, meta, chunk, count, nv):
    sig = blocks.shape[1]
    npts = colloc.shape[1]
    blk = colloc.shape[2] // sig
    nvec, nocc = trial.shape[1], trial.shape[3]
    sizes = (chunk * count, count, sig, blk, nvec, nv, trial.shape[0] // blk)
    shape = (count, nvec // 2 + 1, 2, npts, nocc)
    return pl.pallas_call(
        functools.partial(density_kernel, sizes),
        grid=(1,),
        out_shape=(jax.ShapeDtypeStruct(shape, F32), jax.ShapeDtypeStruct(shape, BF16)),
        in_specs=[
            spec(pltpu.SMEM),
            spec(pltpu.SMEM),
            spec(pl.ANY),
            spec(pl.ANY),
            pl.BlockSpec((count, npts, colloc.shape[2]), lambda i: (chunk, 0, 0)),
        ],
        out_specs=(
            pl.BlockSpec(shape, lambda i: (0, 0, 0, 0, 0)),
            pl.BlockSpec(shape, lambda i: (0, 0, 0, 0, 0)),
        ),
        scratch_shapes=[
            pltpu.SMEM((3, count * sig + 1), jnp.int32),
            pltpu.VMEM((NBUF, nvec + 1, blk, 2, nocc), BF16),
            pltpu.VMEM((count, nvec // 2, 2 * npts, 2 * nocc), F32),
            pltpu.VMEM((count, 2 * npts, nocc), F32),
            pltpu.SemaphoreType.DMA((NBUF, nvec + 1)),
        ],
        compiler_params=pltpu.CompilerParams(vmem_limit_bytes=VMEM_LIMIT),
        name="density",
    )(blocks, meta, trial, occupied, colloc)


def merge_kernel(nv, bit, held, received, keep, send):
    nkeep = (keep.shape[1] - 1) // nv
    mine = bit[0]
    for b in range(keep.shape[0]):
        for q in range(nkeep):
            for v in range(nv):
                for ref, which in ((keep, mine), (send, 1 - mine)):
                    at = (2 * q + which) * nv + v
                    ref[b, q * nv + v] = (held[b, at] + received[b, at].astype(F32)).astype(ref.dtype)
        total = held[b, 2 * nkeep * nv] + received[b, 2 * nkeep * nv].astype(F32)
        keep[b, nkeep * nv] = total
        send[b, nkeep * nv] = total.astype(BF16)


def merge(held, received, bit, nv):
    shape = (held.shape[0], (held.shape[1] - 1) // 2 + 1) + held.shape[2:]
    return pl.pallas_call(
        functools.partial(merge_kernel, nv),
        out_shape=(jax.ShapeDtypeStruct(shape, F32), jax.ShapeDtypeStruct(shape, BF16)),
        in_specs=[spec(pltpu.SMEM), spec(pltpu.VMEM), spec(pltpu.VMEM)],
        out_specs=(spec(pltpu.VMEM), spec(pltpu.VMEM)),
        compiler_params=pltpu.CompilerParams(vmem_limit_bytes=VMEM_LIMIT),
        name="merge",
    )(bit, held, received)


def exchange_kernel(first, held, received, kern, *refs):
    outs, (left, stack) = refs[:-2], refs[-2:]
    nv = held.shape[1] - 1
    npts, nocc = held.shape[3], held.shape[4]
    per_out = outs[0].shape[0]
    dims = (((1,), (1,)), ((), ()))
    for b in range(held.shape[0]):
        total = lambda u, c: (held[b, u, c] + received[b, u, c].astype(F32)).astype(BF16)
        oreal, oimag = total(nv, 0), total(nv, 1)
        turn = jnp.concatenate(
            [
                jnp.concatenate([oreal, oimag], axis=1),
                jnp.concatenate([-oimag, oreal], axis=1),
            ],
            axis=0,
        )
        for v in range(nv):
            for c in range(2):
                left[v * npts : (v + 1) * npts, c * nocc : (c + 1) * nocc] = total(v, c)
        rho = lax.dot_general(left[...], turn, dims, preferred_element_type=F32)
        weight = kern[first + b]
        weight = jnp.concatenate([weight, weight], axis=1)
        for v in range(nv):
            stack[v * npts : (v + 1) * npts] = (rho[v * npts : (v + 1) * npts] * weight).astype(BF16)
        result = jnp.dot(stack[...], turn, preferred_element_type=F32).astype(BF16)
        for v in range(nv):
            outs[b // per_out][b % per_out, :, v * 2 * nocc : (v + 1) * 2 * nocc] = result[v * npts : (v + 1) * npts]


def exchange(held, received, kern, chunk):
    count, nv, npts, nocc = held.shape[0], held.shape[1] - 1, held.shape[3], held.shape[4]
    out = jax.ShapeDtypeStruct((count // 2, npts, nv * 2 * nocc), BF16)
    return pl.pallas_call(
        functools.partial(exchange_kernel, chunk * count),
        out_shape=(out, out),
        in_specs=[spec(pltpu.VMEM)] * 3,
        out_specs=(spec(pltpu.VMEM),) * 2,
        scratch_shapes=[pltpu.VMEM((nv * npts, 2 * nocc), BF16), pltpu.VMEM((nv * npts, 2 * npts), BF16)],
        compiler_params=pltpu.CompilerParams(vmem_limit_bytes=VMEM_LIMIT),
        name="exchange",
    )(held, received, kern)


def project_kernel(sizes, ids, meta, *refs):
    npieces, nown, sig, blk, npts, has_acc, last = sizes
    at = 2 * npieces
    values, potentials = refs[:npieces], refs[npieces:at]
    before = refs[at] if has_acc else None
    out = refs[at + has_acc]
    x, e, acc, sems = refs[at + has_acc + 1 :]
    base = meta[2]
    copies = []
    place = 0
    for i in range(npieces):
        size = values[i].shape[0]
        copies.append(
            pltpu.make_async_copy(values[i].at[:, pl.ds(0, npts)], x.at[pl.ds(place, size)], sems.at[2 * i])
        )
        copies.append(pltpu.make_async_copy(potentials[i], e.at[pl.ds(place, size)], sems.at[2 * i + 1]))
        place += size
    if has_acc:
        copies.append(pltpu.make_async_copy(before, acc, sems.at[2 * npieces]))
    for c in copies:
        c.start()
    if not has_acc:
        acc[...] = jnp.zeros_like(acc)
    for c in copies:
        c.wait()

    def one(i, carry):
        for s in range(sig):
            own = ids[i, s] - base

            @pl.when((own >= 0) & (own < nown))
            def _():
                acc[own] += lax.dot_general(
                    x[i, :, s * blk : (s + 1) * blk], e[i], (((0,), (0,)), ((), ())), preferred_element_type=F32
                )

        return carry

    lax.fori_loop(0, place, one, 0)
    if last:
        nocc = out.shape[2]
        for o in range(nown):
            for v in range(out.shape[0]):
                for c in range(2):
                    col = (2 * v + c) * nocc
                    out[v, pl.ds(o * 2 * blk + c, blk, stride=2), :] = acc[o, :, col : col + nocc]
    else:
        out[...] = acc[...]


def project(values, potentials, ids, meta, before, last, nown, nv, blk, npts, nocc):
    width = nv * 2 * nocc
    total = ids.shape[0]
    sig = ids.shape[1]
    n = len(values)
    has_acc = before is not None
    sizes = (n, nown, sig, blk, npts, int(has_acc), last)
    shape = (nv, nown * blk * 2, nocc) if last else (nown, blk, width)
    args = [ids, meta, *values, *potentials] + ([before] if has_acc else [])
    return pl.pallas_call(
        functools.partial(project_kernel, sizes),
        out_shape=jax.ShapeDtypeStruct(shape, F32),
        in_specs=[spec(pltpu.SMEM)] * 2 + [spec(pl.ANY)] * (2 * n + int(has_acc)),
        out_specs=spec(pltpu.VMEM),
        scratch_shapes=[
            pltpu.VMEM((total, npts, sig * blk), BF16),
            pltpu.VMEM((total, npts, width), BF16),
            pltpu.VMEM((nown, blk, width), F32),
            pltpu.SemaphoreType.DMA((2 * n + 1,)),
        ],
        compiler_params=pltpu.CompilerParams(vmem_limit_bytes=VMEM_LIMIT),
        name="project",
    )(*args)


def swap(array, axis, bit):
    size = lax.axis_size(axis)
    return lax.ppermute(array, axis, [(i, i ^ bit) for i in range(size)])


def gather_all(part, reverse):
    bits = [1 << b for b in range(1, lax.axis_size("grid").bit_length() - 1)]
    if reverse:
        bits = bits[::-1]
    held = part
    for i, bit in enumerate(bits):
        got = swap(held, "grid", bit)
        if i + 1 < len(bits):
            held = jnp.concatenate([held, got], axis=0)
    pieces = [held, got]
    return pieces + [swap(p, "grid", 1) for p in pieces]


def on_device(trial, occupied, colloc, blocks, coords, weights):
    n_ao, n_grid = lax.axis_size("ao"), lax.axis_size("grid")
    batches, npts, _ = colloc.shape
    sig = blocks.shape[1]
    blk = colloc.shape[2] // sig
    nvec, nocc = trial.shape[1], trial.shape[3]
    nv = nvec // n_ao
    nlocal = trial.shape[0] // blk
    nown = nlocal * n_ao // n_grid
    count = batches // 2
    ao, grid = lax.axis_index("ao"), lax.axis_index("grid")
    meta = jnp.stack([ao * nlocal, ao & 1, grid * nown]).astype(jnp.int32)
    steps = n_ao.bit_length() - 1

    numbers = jnp.stack([blocks % 128, blocks // 128], axis=1).astype(BF16)
    numbers = jnp.pad(numbers, ((0, 0), (0, ID_ROWS - 2), (0, colloc.shape[2] - sig)))
    payload = jnp.concatenate([colloc, numbers], axis=1)
    half = count // 2
    values = []
    for chunk in range(2):
        pieces = []
        for h in range(2):
            at = chunk * count + h * half
            pieces += gather_all(payload[at : at + half], h == 1)
        values.append(pieces)
    kern = kernel_matrix(coords, weights)

    total = None
    for chunk in range(2):
        keep, send = density(trial, occupied, colloc, blocks, meta, chunk, count, nv)
        for s in range(steps):
            got = swap(send, "ao", 1 << s)
            if s + 1 < steps:
                bit = ((ao >> (s + 1)) & 1).astype(jnp.int32).reshape(1)
                keep, send = merge(keep, got, bit, nv)
        parts = exchange(keep, got, kern, chunk)
        potentials = []
        for h in range(2):
            potentials += gather_all(parts[h], h == 1)
        numbers = jnp.concatenate([p[:, npts : npts + 2, :sig] for p in values[chunk]], axis=0).astype(jnp.int32)
        ids = numbers[:, 0] + 128 * numbers[:, 1]
        total = project(
            values[chunk], potentials, ids, meta, total, chunk == 1, nown, nv, blk, npts, nocc
        )
    return total.reshape(nv, nown * blk, 2, nocc)


def solution(mesh):
    in_specs = (
        P("ao", None, None, None),
        P("ao", None, None),
        P("grid", None, None),
        P("grid", None),
        P("grid", None, None),
        P("grid", None),
    )
    out_specs = P("ao", "grid", None, None)
    return jax.shard_map(on_device, mesh=mesh, in_specs=in_specs, out_specs=out_specs, check_vma=False)
```

```python
import functools

import jax
import jax.numpy as jnp
from jax import lax
from jax.experimental import pallas as pl
from jax.experimental.pallas import tpu as pltpu
from jax.sharding import PartitionSpec as P

F32 = jnp.float32
BF16 = jnp.bfloat16
EXTRA = 16
NBUF = 4
PARAMS = pltpu.CompilerParams(vmem_limit_bytes=58 * 1024 * 1024)
SMEM = pl.BlockSpec(memory_space=pltpu.SMEM)
VMEM = pl.BlockSpec(memory_space=pltpu.VMEM)
ANY = pl.BlockSpec(memory_space=pl.ANY)


def kernel_matrix(points, quad):
    differ = points[..., :, None, :] - points[..., :, :, None]
    square = jnp.sum(differ * differ, axis=-3)
    return quad[..., :, None] * quad[..., None, :] / jnp.sqrt(square + 0.25)


def selectors(blk):
    ao = lax.broadcasted_iota(jnp.int32, (blk, 2 * blk), 0)
    col = lax.broadcasted_iota(jnp.int32, (blk, 2 * blk), 1)
    return [(col == 2 * ao + c).astype(F32).astype(BF16) for c in range(2)]


def pack_kernel(where, trial, out, rows, sem):
    nb, blk, width = out.shape
    nocc = width // 2
    copies = []
    for j in range(nb):
        at = (where[0] + j) * blk
        copies.append(pltpu.make_async_copy(trial.at[pl.ds(at, blk), where[1]], rows.at[j], sem.at[j]))
    for c in copies:
        c.start()
    pick = selectors(blk)
    for j in range(nb):
        copies[j].wait()
        both = rows[j].reshape(2 * blk, nocc)
        for c in range(2):
            out[j, :, c * nocc : (c + 1) * nocc] = jnp.dot(pick[c], both, preferred_element_type=F32).astype(BF16)


def pack(trial, where, nb, blk):
    nocc = trial.shape[3]
    return pl.pallas_call(
        pack_kernel,
        out_shape=jax.ShapeDtypeStruct((nb, blk, 2 * nocc), BF16),
        in_specs=[SMEM, ANY],
        out_specs=VMEM,
        scratch_shapes=[pltpu.VMEM((nb, blk, 2, nocc), BF16), pltpu.SemaphoreType.DMA((nb,))],
        compiler_params=PARAMS,
        name="pack",
    )(where, trial)


def occupied_kernel(nlocal, ids, meta, occupied, values, keep, send, todo, rows, acc, sems):
    batches, sig = ids.shape
    blk, nocc = rows.shape[1], rows.shape[3]
    npts = values.shape[1]
    n = jnp.int32(0)
    for b in range(batches):
        for s in range(sig):
            local = ids[b, s] - meta[0]
            todo[0, n] = local
            todo[1, n] = b
            todo[2, n] = s
            n = n + ((local >= 0) & (local < nlocal)).astype(jnp.int32)

    def copy(j):
        slot = lax.rem(j, NBUF)
        return pltpu.make_async_copy(occupied.at[pl.ds(todo[0, j] * blk, blk)], rows.at[slot], sems.at[slot])

    def fetch(j):
        @pl.when(j < n)
        def _():
            copy(j).start()

    for j in range(NBUF - 1):
        fetch(jnp.int32(j))
    acc[...] = jnp.zeros_like(acc)
    pick = selectors(blk)

    def step(j, carry):
        b = todo[1, j]
        x = values[b, :, pl.ds(pl.multiple_of(todo[2, j] * blk, blk), blk)]
        fetch(j + NBUF - 1)
        copy(j).wait()
        both = rows[lax.rem(j, NBUF)].reshape(2 * blk, nocc)
        for c in range(2):
            split = jnp.dot(pick[c], both, preferred_element_type=F32).astype(BF16)
            acc[b, :, c * nocc : (c + 1) * nocc] += jnp.dot(x, split, preferred_element_type=F32)
        return carry

    lax.fori_loop(0, n, step, 0)
    keep[...] = acc[...]
    send[...] = acc[...].astype(BF16)


def occupied_part(occupied, colloc, blocks, meta, blk):
    batches, npts, _ = colloc.shape
    nocc = occupied.shape[2]
    shape = (batches, npts, 2 * nocc)
    return pl.pallas_call(
        functools.partial(occupied_kernel, occupied.shape[0] // blk),
        out_shape=(jax.ShapeDtypeStruct(shape, F32), jax.ShapeDtypeStruct(shape, BF16)),
        in_specs=[SMEM, SMEM, ANY, VMEM],
        out_specs=(VMEM, VMEM),
        scratch_shapes=[
            pltpu.SMEM((3, blocks.size + 1), jnp.int32),
            pltpu.VMEM((NBUF, blk, 2, nocc), BF16),
            pltpu.VMEM(shape, F32),
            pltpu.SemaphoreType.DMA((NBUF,)),
        ],
        compiler_params=PARAMS,
        name="occupied",
    )(blocks, meta, occupied, colloc)


def potential_kernel(sizes, ids, meta, *refs):
    nt, tmasks, npiece, xmasks, no, omasks, first, count, nlocal, rank = sizes
    panels, refs = refs[:nt], refs[nt:]
    values, refs = refs[:npiece], refs[npiece:]
    occ, refs = refs[:no], refs[no:]
    kern, out, table, x, sems = refs
    nb, blk, width = panels[0].shape
    nocc = width // 2
    npts = x.shape[2]
    sig = ids.shape[2]
    copies = []
    for i in range(nt):
        over, side = tmasks[i]
        at = (meta[3] ^ over) * nlocal + (meta[4] ^ side) * nb
        copies.append(pltpu.make_async_copy(panels[i], table.at[pl.ds(at, nb)], sems.at[i]))
    place = 0
    for i in range(npiece):
        size = values[i].shape[0]
        copies.append(
            pltpu.make_async_copy(values[i].at[:, :, pl.ds(0, npts)], x.at[pl.ds(place, size)], sems.at[nt + i])
        )
        place += size
    for c in copies:
        c.start()
    for c in copies:
        c.wait()
    sources = [m for masks in xmasks for m in masks]
    where = {m: (i, j) for i, masks in enumerate(omasks) for j, m in enumerate(masks)}
    dims = (((1,), (1,)), ((), ()))
    for p, mask in enumerate(sources):
        piece, row = where[mask]
        for b in range(count):
            dens = jnp.zeros((npts, width), F32)
            for s in range(0, sig, 2):
                panel = jnp.concatenate([table[ids[p, b, s]], table[ids[p, b, s + 1]]], axis=0)
                dens += jnp.dot(x[p, b, :, s * blk : (s + 2) * blk], panel, preferred_element_type=F32)
            left = dens.astype(BF16)
            og = occ[piece][row, first + b]
            oreal, oimag = og[:, :nocc], og[:, nocc:]
            turn = jnp.concatenate([og, jnp.concatenate([-oimag, oreal], axis=1)], axis=0)
            rho = lax.dot_general(left, turn, dims, preferred_element_type=F32)
            weight = kern[p, b]
            m = (rho * jnp.concatenate([weight, weight], axis=1)).astype(BF16)
            out[meta[5] ^ (mask // rank), b] = jnp.dot(m, turn, preferred_element_type=F32).astype(BF16)


def potential(panels, values, occ, kern, ids, meta, first, nlocal, rank):
    tmasks = tuple(m for _, m in panels)
    xmasks = tuple(tuple(m) for _, m in values)
    omasks = tuple(tuple(m) for _, m in occ)
    nsrc, count, sig = ids.shape
    npts = kern.shape[-1]
    blk, width = panels[0][0].shape[1:]
    nt, npiece, no = len(panels), len(values), len(occ)
    total = nlocal * (nt * panels[0][0].shape[0] // nlocal)
    sizes = (nt, tmasks, npiece, xmasks, no, omasks, first, count, nlocal, rank)
    return pl.pallas_call(
        functools.partial(potential_kernel, sizes),
        out_shape=jax.ShapeDtypeStruct((nsrc, count, npts, width), BF16),
        in_specs=[SMEM, SMEM] + [ANY] * (nt + npiece) + [VMEM] * (no + 1),
        out_specs=VMEM,
        scratch_shapes=[
            pltpu.VMEM((total, blk, width), BF16),
            pltpu.VMEM((nsrc, count, npts, sig * blk), BF16),
            pltpu.SemaphoreType.DMA((nt + npiece,)),
        ],
        compiler_params=PARAMS,
        name="potential",
    )(ids, meta, *[a for a, _ in panels], *[a for a, _ in values], *[a for a, _ in occ], kern)


def project_kernel(sizes, ids, meta, *refs):
    nx, xmasks, ne, emasks, rank, nown, last = sizes
    has_acc = last
    values, refs = refs[:nx], refs[nx:]
    potentials, refs = refs[:ne], refs[ne:]
    before = refs[0] if has_acc else None
    out, x, e, acc, sems = refs[has_acc:]
    sig = ids.shape[2]
    count = x.shape[1]
    npts = x.shape[2]
    blk = x.shape[3] // sig
    width = potentials[0].shape[-1]
    copies = []
    place = 0
    for i in range(nx):
        size = values[i].shape[0]
        copies.append(
            pltpu.make_async_copy(values[i].at[:, :, pl.ds(0, npts)], x.at[pl.ds(place, size)], sems.at[len(copies)])
        )
        place += size
    for i in range(ne):
        for j, mask in enumerate(emasks[i]):
            col = pl.multiple_of((meta[5] ^ (mask // rank)) * width, width)
            copies.append(
                pltpu.make_async_copy(
                    potentials[i].at[j], e.at[mask % rank, :, :, :, pl.ds(col, width)], sems.at[len(copies)]
                )
            )
    if has_acc:
        copies.append(pltpu.make_async_copy(before, acc, sems.at[len(copies)]))
    for c in copies:
        c.start()
    if not has_acc:
        acc[...] = jnp.zeros_like(acc)
    for c in copies:
        c.wait()
    sources = [m for masks in xmasks for m in masks]
    for p, mask in enumerate(sources):
        for b in range(count):

            def one(s, carry):
                own = ids[p, b, s] - meta[2]

                @pl.when((own >= 0) & (own < nown))
                def _():
                    at = pl.multiple_of(s * blk, blk)
                    acc[own] += lax.dot_general(
                        x[p, b, :, pl.ds(at, blk)],
                        e[mask % rank, meta[5] ^ (mask // rank), b],
                        (((0,), (0,)), ((), ())),
                        preferred_element_type=F32,
                    )

                return carry

            lax.fori_loop(0, sig, one, 0)
    if last:
        nocc = out.shape[2]
        for o in range(nown):
            for v in range(out.shape[0]):
                for c in range(2):
                    col = (2 * v + c) * nocc
                    out[v, pl.ds(o * 2 * blk + c, blk, stride=2), :] = acc[o, :, col : col + nocc]
    else:
        out[...] = acc[...]


def project(values, potentials, ids, meta, before, rank, nown, npts):
    xmasks = tuple(tuple(m) for _, m in values)
    emasks = tuple(tuple(m) for _, m in potentials)
    nsrc, count, sig = ids.shape
    nv, width = potentials[0][0].shape[1], potentials[0][0].shape[-1]
    blk = values[0][0].shape[-1] // sig
    nx, ne = len(values), len(potentials)
    last = before is not None
    shape = (nv, nown * blk * 2, width // 2) if last else (nown, blk, nv * width)
    args = [ids, meta, *[a for a, _ in values], *[a for a, _ in potentials]] + ([before] if last else [])
    return pl.pallas_call(
        functools.partial(project_kernel, (nx, xmasks, ne, emasks, rank, nown, int(last))),
        out_shape=jax.ShapeDtypeStruct(shape, F32),
        in_specs=[SMEM] * 2 + [ANY] * (nx + ne + int(last)),
        out_specs=VMEM,
        scratch_shapes=[
            pltpu.VMEM((nsrc, count, npts, sig * blk), BF16),
            pltpu.VMEM((rank, nv, count, npts, nv * width), BF16),
            pltpu.VMEM((nown, blk, nv * width), F32),
            pltpu.SemaphoreType.DMA((nx + sum(len(m) for m in emasks) + 1,)),
        ],
        compiler_params=PARAMS,
        name="project",
    )(*args)


def swap(array, axis, bit):
    size = lax.axis_size(axis)
    return lax.ppermute(array, axis, [(i, i ^ bit) for i in range(size)])


def across(pieces, bits):
    for i, bit in enumerate(bits):
        got = [(swap(a, "grid", bit), [m ^ bit for m in masks]) for a, masks in pieces]
        if i + 1 < len(bits):
            pieces = [
                (jnp.concatenate([a, b], axis=0), masks + more) for (a, masks), (b, more) in zip(pieces, got, strict=True)
            ]
        else:
            pieces = pieces + got
    return pieces


def within(pieces, bits):
    for bit in bits:
        pieces = pieces + [(swap(a, "grid", bit), [m ^ bit for m in masks]) for a, masks in pieces]
    return pieces


def thirds(x):
    high = lax.reduce_precision(x, 8, 7)
    rest = x - high
    mid = lax.reduce_precision(rest, 8, 7)
    return [high, mid, rest - mid]


def on_device(trial, occupied, colloc, blocks, coords, weights):
    n_ao, n_grid = lax.axis_size("ao"), lax.axis_size("grid")
    batches, npts, span = colloc.shape
    sig = blocks.shape[1]
    blk = span // sig
    nvec, nocc = trial.shape[1], trial.shape[3]
    nv = nvec // n_ao
    rank = n_grid // nv
    nlocal = trial.shape[0] // blk
    nown = nlocal * n_ao // n_grid
    parts = min(rank, nlocal & -nlocal)
    nb = nlocal // parts
    count = batches // 2
    ao, grid = lax.axis_index("ao"), lax.axis_index("grid")
    vector, side = grid // rank, grid % parts
    meta = jnp.stack([ao * nlocal, ao * 0, grid * nown, ao, side, vector]).astype(jnp.int32)
    high_bits = [rank << b for b in range(nv.bit_length() - 1)]
    low_bits = [1 << b for b in range(rank.bit_length() - 1)]
    part_bits = [1 << b for b in range(parts.bit_length() - 1)]

    panels = []
    for over in reversed(range(n_ao)):
        where = jnp.stack([side * nb, (ao ^ over) * nv + vector]).astype(jnp.int32)
        rows = pack(trial, where, nb, blk)
        panels.append((swap(rows, "ao", over) if over else rows, (over, 0)))

    numbers = [blocks % 128, blocks // 128]
    numbers = [jnp.pad(a.astype(F32), ((0, 0), (0, npts - sig))) for a in numbers]
    exact = jnp.concatenate([coords, weights[:, None]], axis=1)
    extra = jnp.concatenate([jnp.stack(numbers, axis=1)] + thirds(exact), axis=1).astype(BF16)
    extra = jnp.pad(extra, ((0, 0), (0, EXTRA - extra.shape[1]), (0, span - npts)))
    payload = jnp.concatenate([colloc, extra], axis=1)
    near = []
    for chunk in range(2):
        part = payload[None, chunk * count : (chunk + 1) * count]
        near.append(across([(part, [0])], high_bits[::-1] if chunk else high_bits))

    held, send = occupied_part(occupied, colloc, blocks, meta, blk)
    for s in range(n_ao.bit_length() - 1):
        held = held + swap(send, "ao", 1 << s).astype(F32)
        send = held.astype(BF16)
    occ = across([(send[None], [0])], high_bits)

    for bit in part_bits:
        panels = panels + [(swap(a, "grid", bit), (over, m ^ bit)) for a, (over, m) in panels]
    far = [within(pieces, low_bits) for pieces in near]

    def facts(pieces):
        rows = jnp.concatenate([a[:, :, npts:, :npts] for a, _ in pieces], axis=0).astype(F32)
        ids = (rows[:, :, 0, :sig] + 128 * rows[:, :, 1, :sig]).astype(jnp.int32)
        return ids, rows[:, :, 2:6] + rows[:, :, 6:10] + rows[:, :, 10:14]

    potentials = []
    for chunk in range(2):
        ids, exact = facts(near[chunk])
        kern = kernel_matrix(exact[:, :, :3], exact[:, :, 3])
        e = potential(panels, near[chunk], occ, kern, ids, meta, chunk * count, nlocal, rank)
        pieces = across([(e[None], [0])], high_bits[::-1] if chunk else high_bits)
        potentials.append(within(pieces, low_bits))
    total = None
    for chunk in range(2):
        ids, _ = facts(far[chunk])
        total = project(far[chunk], potentials[chunk], ids, meta, total, rank, nown, npts)
    return total.reshape(nv, nown * blk, 2, nocc)


def solution(mesh):
    in_specs = (
        P("ao", None, None, None),
        P("ao", None, None),
        P("grid", None, None),
        P("grid", None),
        P("grid", None, None),
        P("grid", None),
    )
    out_specs = P("ao", "grid", None, None)
    return jax.shard_map(on_device, mesh=mesh, in_specs=in_specs, out_specs=out_specs, check_vma=False)
```

```python
import functools

import jax
import jax.numpy as jnp
from jax import lax
from jax.experimental import pallas as pl
from jax.experimental.pallas import tpu as pltpu
from jax.sharding import PartitionSpec as P

F32 = jnp.float32
BF16 = jnp.bfloat16
EXTRA = 16
PARAMS = pltpu.CompilerParams(vmem_limit_bytes=58 * 1024 * 1024)
SMEM = pl.BlockSpec(memory_space=pltpu.SMEM)
VMEM = pl.BlockSpec(memory_space=pltpu.VMEM)
ANY = pl.BlockSpec(memory_space=pl.ANY)


def kernel_matrix(points, quad):
    differ = points[..., :, None, :] - points[..., :, :, None]
    square = jnp.sum(differ * differ, axis=-3)
    return quad[..., :, None] * quad[..., None, :] / jnp.sqrt(square + 0.25)


def selectors(blk):
    ao = lax.broadcasted_iota(jnp.int32, (blk, 2 * blk), 0)
    col = lax.broadcasted_iota(jnp.int32, (blk, 2 * blk), 1)
    return [(col == 2 * ao + c).astype(F32).astype(BF16) for c in range(2)]


def pack_kernel(where, trial, *refs):
    outs, (rows, sem) = refs[:-2], refs[-2:]
    nb, blk, width = outs[0].shape
    nocc = width // 2
    copies = []
    for i in range(len(outs)):
        for j in range(nb):
            at = (where[0] + j) * blk
            copies.append(
                pltpu.make_async_copy(trial.at[pl.ds(at, blk), where[1 + i]], rows.at[i, j], sem.at[i, j])
            )
    for c in copies:
        c.start()
    pick = selectors(blk)
    for i, out in enumerate(outs):
        for j in range(nb):
            copies[i * nb + j].wait()
            both = rows[i, j].reshape(2 * blk, nocc)
            for c in range(2):
                split = jnp.dot(pick[c], both, preferred_element_type=F32)
                out[j, :, c * nocc : (c + 1) * nocc] = split.astype(BF16)


def pack(trial, where, planes, nb, blk):
    nocc = trial.shape[3]
    return pl.pallas_call(
        pack_kernel,
        out_shape=(jax.ShapeDtypeStruct((nb, blk, 2 * nocc), BF16),) * planes,
        in_specs=[SMEM, ANY],
        out_specs=(VMEM,) * planes,
        scratch_shapes=[pltpu.VMEM((planes, nb, blk, 2, nocc), BF16), pltpu.SemaphoreType.DMA((planes, nb))],
        compiler_params=PARAMS,
        name="pack",
    )(where, trial)


def occupied_kernel(ids, meta, occupied, values, keep, send, table):
    batches, sig = ids.shape
    blk, nocc = occupied.shape[0] // (table.shape[0] - 1), occupied.shape[2]
    nlocal = table.shape[0] - 1
    pick = selectors(blk)
    for j in range(nlocal):
        both = occupied[j * blk : (j + 1) * blk].reshape(2 * blk, nocc)
        for c in range(2):
            split = jnp.dot(pick[c], both, preferred_element_type=F32)
            table[j, :, c * nocc : (c + 1) * nocc] = split.astype(BF16)
    table[nlocal] = jnp.zeros(table.shape[1:], BF16)

    def block(b, s):
        local = ids[b, s] - meta[0]
        return table[jnp.where((local >= 0) & (local < nlocal), local, nlocal)]

    for b in range(batches):
        total = jnp.zeros(keep.shape[1:], F32)
        for s in range(0, sig, 2):
            two = jnp.concatenate([block(b, s), block(b, s + 1)], axis=0)
            total += jnp.dot(values[b, :, s * blk : (s + 2) * blk], two, preferred_element_type=F32)
        keep[b] = total
        send[b] = total.astype(BF16)


def occupied_part(occupied, colloc, blocks, meta, blk):
    batches, npts, _ = colloc.shape
    nocc = occupied.shape[2]
    shape = (batches, npts, 2 * nocc)
    return pl.pallas_call(
        occupied_kernel,
        out_shape=(jax.ShapeDtypeStruct(shape, F32), jax.ShapeDtypeStruct(shape, BF16)),
        in_specs=[SMEM, SMEM, VMEM, VMEM],
        out_specs=(VMEM, VMEM),
        scratch_shapes=[pltpu.VMEM((occupied.shape[0] // blk + 1, blk, 2 * nocc), BF16)],
        compiler_params=PARAMS,
        name="occupied",
    )(blocks, meta, occupied, colloc)


def potential_kernel(sizes, ids, meta, *refs):
    nt, tmasks, npiece, xmasks, no, omasks, first, count, nlocal, rank = sizes
    panels, refs = refs[:nt], refs[nt:]
    values, refs = refs[:npiece], refs[npiece:]
    occ, refs = refs[:no], refs[no:]
    kern, out, table, x, sems = refs
    nb, blk, width = panels[0].shape
    nocc = width // 2
    npts = x.shape[2]
    sig = ids.shape[2]
    copies = []
    for i in range(nt):
        over, side = tmasks[i]
        at = (meta[3] ^ over) * nlocal + (meta[4] ^ side) * nb
        copies.append(pltpu.make_async_copy(panels[i], table.at[pl.ds(at, nb)], sems.at[i]))
    place = 0
    for i in range(npiece):
        size = values[i].shape[0]
        copies.append(
            pltpu.make_async_copy(values[i].at[:, :, pl.ds(0, npts)], x.at[pl.ds(place, size)], sems.at[nt + i])
        )
        place += size
    for c in copies:
        c.start()
    for c in copies:
        c.wait()
    sources = [m for masks in xmasks for m in masks]
    where = {m: (i, j) for i, masks in enumerate(omasks) for j, m in enumerate(masks)}
    dims = (((1,), (1,)), ((), ()))
    for p, mask in enumerate(sources):
        piece, row = where[mask]
        for b in range(count):
            dens = jnp.zeros((npts, width), F32)
            for s in range(0, sig, 2):
                panel = jnp.concatenate([table[ids[p, b, s]], table[ids[p, b, s + 1]]], axis=0)
                dens += jnp.dot(x[p, b, :, s * blk : (s + 2) * blk], panel, preferred_element_type=F32)
            left = dens.astype(BF16)
            og = occ[piece][row, first + b]
            oreal, oimag = og[:, :nocc], og[:, nocc:]
            turn = jnp.concatenate([og, jnp.concatenate([-oimag, oreal], axis=1)], axis=0)
            rho = lax.dot_general(left, turn, dims, preferred_element_type=F32)
            weight = kern[p, b]
            m = (rho * jnp.concatenate([weight, weight], axis=1)).astype(BF16)
            out[meta[5] ^ (mask // rank), b] = jnp.dot(m, turn, preferred_element_type=F32).astype(BF16)


def potential(panels, values, occ, kern, ids, meta, first, nlocal, rank):
    tmasks = tuple(m for _, m in panels)
    xmasks = tuple(tuple(m) for _, m in values)
    omasks = tuple(tuple(m) for _, m in occ)
    nsrc, count, sig = ids.shape
    npts = kern.shape[-1]
    blk, width = panels[0][0].shape[1:]
    nt, npiece, no = len(panels), len(values), len(occ)
    total = nlocal * (nt * panels[0][0].shape[0] // nlocal)
    sizes = (nt, tmasks, npiece, xmasks, no, omasks, first, count, nlocal, rank)
    return pl.pallas_call(
        functools.partial(potential_kernel, sizes),
        out_shape=jax.ShapeDtypeStruct((nsrc, count, npts, width), BF16),
        in_specs=[SMEM, SMEM] + [ANY] * (nt + npiece) + [VMEM] * (no + 1),
        out_specs=VMEM,
        scratch_shapes=[
            pltpu.VMEM((total, blk, width), BF16),
            pltpu.VMEM((nsrc, count, npts, sig * blk), BF16),
            pltpu.SemaphoreType.DMA((nt + npiece,)),
        ],
        compiler_params=PARAMS,
        name="potential",
    )(ids, meta, *[a for a, _ in panels], *[a for a, _ in values], *[a for a, _ in occ], kern)


def select_kernel(sizes, *refs):
    ncall, xmasks, rank, nown = sizes
    all_ids, refs = refs[:ncall], refs[ncall:]
    meta, refs = refs[0], refs[1:]
    flat = [m for masks in xmasks for m in masks]
    values, (facts, columns, x, sems) = refs[: len(flat)], refs[len(flat) :]
    ncount = all_ids[0].shape[1]
    sig = all_ids[0].shape[2]
    npts = x.shape[2]
    blk = x.shape[3] // sig
    copies = []
    place = 0
    starts = []
    for i, piece in enumerate(values):
        size = piece.shape[0]
        copies.append(pltpu.make_async_copy(piece.at[:, :, pl.ds(0, npts)], x.at[pl.ds(place, size)], sems.at[i]))
        starts.append(place)
        place += size
    for c in copies:
        c.start()
    for c in copies:
        c.wait()
    n = jnp.int32(0)
    place = 0
    groups = len(values) // ncall
    for chunk in range(ncall):
        p = 0
        for i in range(groups):
            piece = chunk * groups + i
            for j, mask in enumerate(flat[piece]):
                for b in range(ncount):

                    def one(s, n, chunk=chunk, p=p, mask=mask, b=b, row=starts[piece] + j):
                        own = all_ids[chunk][p, b, s] - meta[2]
                        mine = (own >= 0) & (own < nown)

                        @pl.when(mine)
                        def _():
                            facts[0, n] = own
                            facts[1, n] = chunk
                            facts[2, n] = mask % rank
                            facts[3, n] = meta[5] ^ (mask // rank)
                            facts[4, n] = b
                            at = pl.multiple_of(s * blk, blk)
                            columns[n] = x[row, b, :, pl.ds(at, blk)].T

                        return n + mine.astype(jnp.int32)

                    n = lax.fori_loop(0, sig, one, n)
                p += 1
    facts[5, 0] = n


def select(values, all_ids, meta, rank, nown, npts):
    flat = [piece for pieces in values for piece in pieces]
    xmasks = tuple((tuple(m),) for _, m in flat)
    nsrc, count, sig = all_ids[0].shape
    blk = flat[0][0].shape[-1] // sig
    most = len(values) * nsrc * count * sig
    sizes = (len(values), tuple(tuple(m) for m in xmasks), rank, nown)
    return pl.pallas_call(
        functools.partial(select_kernel, sizes),
        out_shape=(jax.ShapeDtypeStruct((6, most), jnp.int32), jax.ShapeDtypeStruct((most, blk, npts), BF16)),
        in_specs=[SMEM] * (len(values) + 1) + [ANY] * len(flat),
        out_specs=(SMEM, VMEM),
        scratch_shapes=[
            pltpu.VMEM((len(values) * nsrc, count, npts, sig * blk), BF16),
            pltpu.SemaphoreType.DMA((len(flat),)),
        ],
        compiler_params=PARAMS,
        name="select",
    )(*all_ids, meta, *[a for a, _ in flat])


def project_kernel(sizes, facts, meta, columns, *refs):
    nchunk, emasks, rank, group, last = sizes
    ne = len(emasks)
    potentials, refs = refs[:ne], refs[ne:]
    before = refs[0] if last else None
    out, x, e, acc, esems, xsems = refs[last:]
    nvs = e.shape[2]
    blk = x.shape[1]
    nown = acc.shape[1]
    n = facts[5, 0]
    ncopy = columns.shape[0] // group
    ecopies = []
    place = {}
    for i in range(ne):
        chunk, masks = emasks[i]
        for j, mask in enumerate(masks):
            k = place.setdefault((chunk, mask % rank), [])
            ecopies.append(
                pltpu.make_async_copy(
                    potentials[i].at[j], e.at[chunk, mask % rank, len(k)], esems.at[len(ecopies)]
                )
            )
            k.append(mask // rank)
    if last:
        ecopies.append(pltpu.make_async_copy(before, acc, esems.at[len(ecopies)]))
    xcopies = [
        pltpu.make_async_copy(columns.at[pl.ds(i * group, group)], x.at[pl.ds(i * group, group)], xsems.at[i])
        for i in range(ncopy)
    ]
    for i, c in enumerate(xcopies):

        @pl.when(i * group < n)
        def _(c=c):
            c.start()

    for c in ecopies:
        c.start()
    if not last:
        acc[...] = jnp.zeros_like(acc)
    for i, c in enumerate(xcopies):

        @pl.when(i * group < n)
        def _(c=c):
            c.wait()

    for c in ecopies:
        c.wait()

    def one(i, carry):
        own, chunk, side, source, b = [facts[f, i] for f in range(5)]
        for k in range(nvs):
            off = jnp.int32(place[(0, 0)][k])
            for other in range(1, nchunk):
                off = jnp.where(chunk == other, place[(other, 0)][k], off)
            vec = meta[5] ^ off
            acc[vec, own] += jnp.dot(x[i], e[chunk, side, k, source, b], preferred_element_type=F32)
        return carry

    lax.fori_loop(0, n, one, 0)
    if last:
        nocc = out.shape[2]
        for v in range(out.shape[0]):
            for o in range(nown):
                for c in range(2):
                    out[v, pl.ds(o * 2 * blk + c, blk, stride=2), :] = acc[v, o, :, c * nocc : (c + 1) * nocc]
    else:
        out[...] = acc[...]


def project(potentials, facts, columns, meta, before, rank, nown, group):
    emasks = tuple((chunk, tuple(m)) for chunk, _, m in potentials)
    nchunk = 1 + max(chunk for chunk, _, _ in potentials)
    nv, count, npts, width = potentials[0][1].shape[1:]
    blk = columns.shape[1]
    ne = len(potentials)
    slots = sum(len(m) for _, m in emasks) // nchunk // rank
    last = before is not None
    shape = (nv, nown * blk * 2, width // 2) if last else (nv, nown, blk, width)
    args = [facts, meta, columns, *[a for _, a, _ in potentials]] + ([before] if last else [])
    return pl.pallas_call(
        functools.partial(project_kernel, (nchunk, emasks, rank, group, int(last))),
        out_shape=jax.ShapeDtypeStruct(shape, F32),
        in_specs=[SMEM] * 2 + [ANY] * (1 + ne + int(last)),
        out_specs=VMEM,
        scratch_shapes=[
            pltpu.VMEM(columns.shape, BF16),
            pltpu.VMEM((nchunk, rank, slots, nv, count, npts, width), BF16),
            pltpu.VMEM((nv, nown, blk, width), F32),
            pltpu.SemaphoreType.DMA((sum(len(m) for _, m in emasks) + 1,)),
            pltpu.SemaphoreType.DMA((columns.shape[0] // group,)),
        ],
        compiler_params=PARAMS,
        name="project",
    )(*args)


def swap(array, axis, bit):
    size = lax.axis_size(axis)
    return lax.ppermute(array, axis, [(i, i ^ bit) for i in range(size)])


def across(pieces, bits):
    for i, bit in enumerate(bits):
        got = [(swap(a, "grid", bit), [m ^ bit for m in masks]) for a, masks in pieces]
        if i + 1 < len(bits):
            pieces = [
                (jnp.concatenate([a, b], axis=0), masks + more) for (a, masks), (b, more) in zip(pieces, got, strict=True)
            ]
        else:
            pieces = pieces + got
    return pieces


def within(pieces, bits):
    for bit in bits:
        pieces = pieces + [(swap(a, "grid", bit), [m ^ bit for m in masks]) for a, masks in pieces]
    return pieces


def thirds(x):
    high = lax.reduce_precision(x, 8, 7)
    rest = x - high
    mid = lax.reduce_precision(rest, 8, 7)
    return [high, mid, rest - mid]


def on_device(trial, occupied, colloc, blocks, coords, weights):
    n_ao, n_grid = lax.axis_size("ao"), lax.axis_size("grid")
    batches, npts, span = colloc.shape
    sig = blocks.shape[1]
    blk = span // sig
    nvec, nocc = trial.shape[1], trial.shape[3]
    nv = nvec // n_ao
    rank = n_grid // nv
    nlocal = trial.shape[0] // blk
    nown = nlocal * n_ao // n_grid
    parts = min(rank, nlocal & -nlocal)
    nb = nlocal // parts
    count = batches // 2
    ao, grid = lax.axis_index("ao"), lax.axis_index("grid")
    vector, side = grid // rank, grid % parts
    meta = jnp.stack([ao * nlocal, ao * 0, grid * nown, ao, side, vector]).astype(jnp.int32)
    high_bits = [rank << b for b in range(nv.bit_length() - 1)]
    low_bits = [1 << b for b in range(rank.bit_length() - 1)]
    part_bits = [1 << b for b in range(parts.bit_length() - 1)]

    planes = list(reversed(range(n_ao)))
    where = jnp.stack([side * nb] + [(ao ^ over) * nv + vector for over in planes]).astype(jnp.int32)
    rows = pack(trial, where, n_ao, nb, blk)
    panels = []
    for over, one in zip(planes, rows, strict=True):
        panels.append((swap(one, "ao", over) if over else one, (over, 0)))
    own = panels[-1][0]

    own, colloc, blocks = lax.optimization_barrier((own, colloc, blocks))
    panels[-1] = (own, panels[-1][1])
    numbers = [blocks % 128, blocks // 128]
    numbers = [jnp.pad(a.astype(F32), ((0, 0), (0, npts - sig))) for a in numbers]
    exact = jnp.concatenate([coords, weights[:, None]], axis=1)
    extra = jnp.concatenate([jnp.stack(numbers, axis=1)] + thirds(exact), axis=1).astype(BF16)
    extra = jnp.pad(extra, ((0, 0), (0, EXTRA - extra.shape[1]), (0, span - npts)))
    payload = jnp.concatenate([colloc, extra], axis=1)
    near = []
    for chunk in range(2):
        part = payload[None, chunk * count : (chunk + 1) * count]
        near.append(across([(part, [0])], high_bits[::-1] if chunk else high_bits))

    payload, occupied = lax.optimization_barrier((payload, occupied))
    held, send = occupied_part(occupied, colloc, blocks, meta, blk)
    for s in range(n_ao.bit_length() - 1):
        held = held + swap(send, "ao", 1 << s).astype(F32)
        send = held.astype(BF16)
    occ = across([(send[None], [0])], high_bits)

    for bit in part_bits:
        panels = panels + [(swap(a, "grid", bit), (over, m ^ bit)) for a, (over, m) in panels]
    far = [within(pieces, low_bits) for pieces in near]

    def facts_of(pieces):
        rows = jnp.concatenate([a[:, :, npts:, :npts] for a, _ in pieces], axis=0).astype(F32)
        ids = (rows[:, :, 0, :sig] + 128 * rows[:, :, 1, :sig]).astype(jnp.int32)
        return ids, rows[:, :, 2:6] + rows[:, :, 6:10] + rows[:, :, 10:14]

    all_ids = [facts_of(pieces)[0] for pieces in far]
    facts, columns = select(far, all_ids, meta, rank, nown, npts)

    early, late = [], []
    for chunk in range(2):
        ids, exact = facts_of(near[chunk])
        kern = kernel_matrix(exact[:, :, :3], exact[:, :, 3])
        e = potential(panels, near[chunk], occ, kern, ids, meta, chunk * count, nlocal, rank)
        pieces = across([(e[None], [0])], high_bits[::-1] if chunk else high_bits)
        early += [(chunk, a, m) for a, m in within(pieces[:1], low_bits)]
        late += [(chunk, a, m) for a, m in within(pieces[1:], low_bits)]
    total = project(early, facts, columns, meta, None, rank, nown, 4 * sig)
    total = project(late, facts, columns, meta, total, rank, nown, 4 * sig)
    return total.reshape(nv, nown * blk, 2, nocc)


def solution(mesh):
    in_specs = (
        P("ao", None, None, None),
        P("ao", None, None),
        P("grid", None, None),
        P("grid", None),
        P("grid", None, None),
        P("grid", None),
    )
    out_specs = P("ao", "grid", None, None)

    return jax.shard_map(on_device, mesh=mesh, in_specs=in_specs, out_specs=out_specs, check_vma=False)
```

```python
import functools

import jax
import jax.numpy as jnp
from jax import lax
from jax.experimental import pallas as pl
from jax.experimental.pallas import tpu as pltpu
from jax.sharding import PartitionSpec as P

F32 = jnp.float32
BF16 = jnp.bfloat16
EXTRA = 16
PARAMS = pltpu.CompilerParams(vmem_limit_bytes=58 * 1024 * 1024)
SMEM = pl.BlockSpec(memory_space=pltpu.SMEM)
VMEM = pl.BlockSpec(memory_space=pltpu.VMEM)
ANY = pl.BlockSpec(memory_space=pl.ANY)


def kernel_matrix(points, quad):
    differ = points[..., :, None, :] - points[..., :, :, None]
    square = jnp.sum(differ * differ, axis=-3)
    return quad[..., :, None] * quad[..., None, :] / jnp.sqrt(square + 0.25)


def selectors(blk):
    ao = lax.broadcasted_iota(jnp.int32, (blk, 2 * blk), 0)
    col = lax.broadcasted_iota(jnp.int32, (blk, 2 * blk), 1)
    return [(col == 2 * ao + c).astype(F32).astype(BF16) for c in range(2)]


def pack_kernel(where, trial, *refs):
    outs, (rows, sem) = refs[:-2], refs[-2:]
    nb, blk, width = outs[0].shape
    nocc = width // 2
    copies = []
    for i in range(len(outs)):
        for j in range(nb):
            at = (where[0] + j) * blk
            copies.append(
                pltpu.make_async_copy(trial.at[pl.ds(at, blk), where[1 + i]], rows.at[i, j], sem.at[i, j])
            )
    for c in copies:
        c.start()
    pick = jnp.concatenate(selectors(blk), axis=0)
    for i, out in enumerate(outs):
        for j in range(0, nb, 2):
            ahead = range(j, min(j + 2, nb))
            for k in ahead:
                copies[i * nb + k].wait()
            both = jnp.concatenate([rows[i, k].reshape(2 * blk, nocc) for k in ahead], axis=1)
            split = jnp.dot(pick, both, preferred_element_type=F32).astype(BF16)
            for k in ahead:
                for c in range(2):
                    piece = split[c * blk : (c + 1) * blk, (k - j) * nocc : (k - j + 1) * nocc]
                    out[k, :, c * nocc : (c + 1) * nocc] = piece


def pack(trial, where, planes, nb, blk):
    nocc = trial.shape[3]
    return pl.pallas_call(
        pack_kernel,
        out_shape=(jax.ShapeDtypeStruct((nb, blk, 2 * nocc), BF16),) * planes,
        in_specs=[SMEM, ANY],
        out_specs=(VMEM,) * planes,
        scratch_shapes=[pltpu.VMEM((planes, nb, blk, 2, nocc), BF16), pltpu.SemaphoreType.DMA((planes, nb))],
        compiler_params=PARAMS,
        name="pack",
    )(where, trial)


def occupied_kernel(ids, meta, occupied, values, keep, send, table):
    batches, sig = ids.shape
    blk, nocc = occupied.shape[0] // (table.shape[0] - 1), occupied.shape[2]
    nlocal = table.shape[0] - 1
    pick = selectors(blk)
    for j in range(nlocal):
        both = occupied[j * blk : (j + 1) * blk].reshape(2 * blk, nocc)
        for c in range(2):
            split = jnp.dot(pick[c], both, preferred_element_type=F32)
            table[j, :, c * nocc : (c + 1) * nocc] = split.astype(BF16)
    table[nlocal] = jnp.zeros(table.shape[1:], BF16)

    def block(b, s):
        local = ids[b, s] - meta[0]
        return table[jnp.where((local >= 0) & (local < nlocal), local, nlocal)]

    for b in range(batches):
        total = jnp.zeros(keep.shape[1:], F32)
        for s in range(0, sig, 2):
            two = jnp.concatenate([block(b, s), block(b, s + 1)], axis=0)
            total += jnp.dot(values[b, :, s * blk : (s + 2) * blk], two, preferred_element_type=F32)
        keep[b] = total
        send[b] = total.astype(BF16)


def occupied_part(occupied, colloc, blocks, meta, blk):
    batches, npts, _ = colloc.shape
    nocc = occupied.shape[2]
    shape = (batches, npts, 2 * nocc)
    return pl.pallas_call(
        occupied_kernel,
        out_shape=(jax.ShapeDtypeStruct(shape, F32), jax.ShapeDtypeStruct(shape, BF16)),
        in_specs=[SMEM, SMEM, VMEM, VMEM],
        out_specs=(VMEM, VMEM),
        scratch_shapes=[pltpu.VMEM((occupied.shape[0] // blk + 1, blk, 2 * nocc), BF16)],
        compiler_params=PARAMS,
        name="occupied",
    )(blocks, meta, occupied, colloc)


def potential_kernel(sizes, ids, meta, *refs):
    nt, tmasks, npiece, xmasks, no, omasks, first, count, nlocal, rank = sizes
    panels, refs = refs[:nt], refs[nt:]
    values, refs = refs[:npiece], refs[npiece:]
    occ, refs = refs[:no], refs[no:]
    kern, out, table, x, left, m, sems = refs
    nb, blk, width = panels[0].shape
    nocc = width // 2
    npts = x.shape[2]
    sig = ids.shape[2]
    copies = []
    for i in range(nt):
        over, side = tmasks[i]
        at = (meta[3] ^ over) * nlocal + (meta[4] ^ side) * nb
        copies.append(pltpu.make_async_copy(panels[i], table.at[pl.ds(at, nb)], sems.at[i]))
    place = 0
    for i in range(npiece):
        size = values[i].shape[0]
        copies.append(
            pltpu.make_async_copy(values[i].at[:, :, pl.ds(0, npts)], x.at[pl.ds(place, size)], sems.at[nt + i])
        )
        place += size
    for c in copies:
        c.start()
    for c in copies:
        c.wait()
    sources = [m for masks in xmasks for m in masks]
    where = {m: (i, j) for i, masks in enumerate(omasks) for j, m in enumerate(masks)}
    dims = (((1,), (1,)), ((), ()))
    todo = [(p, mask, b) for p, mask in enumerate(sources) for b in range(count)]

    def turn_of(mask, b):
        piece, row = where[mask]
        og = occ[piece][row, first + b]
        return jnp.concatenate([og, jnp.concatenate([-og[:, nocc:], og[:, :nocc]], axis=1)], axis=0)

    for i, (p, mask, b) in enumerate(todo):
        dens = jnp.zeros((npts, width), F32)
        for s in range(0, sig, 2):
            panel = jnp.concatenate([table[ids[p, b, s]], table[ids[p, b, s + 1]]], axis=0)
            dens += jnp.dot(x[p, b, :, s * blk : (s + 2) * blk], panel, preferred_element_type=F32)
        left[i] = dens.astype(BF16)
    for i, (p, mask, b) in enumerate(todo):
        rho = lax.dot_general(left[i], turn_of(mask, b), dims, preferred_element_type=F32)
        weight = kern[p, b]
        m[i] = (rho * jnp.concatenate([weight, weight], axis=1)).astype(BF16)
    for i, (p, mask, b) in enumerate(todo):
        e = jnp.dot(m[i], turn_of(mask, b), preferred_element_type=F32)
        out[meta[5] ^ (mask // rank), b] = e.astype(BF16)


def potential(panels, values, occ, kern, ids, meta, first, nlocal, rank):
    tmasks = tuple(m for _, m in panels)
    xmasks = tuple(tuple(m) for _, m in values)
    omasks = tuple(tuple(m) for _, m in occ)
    nsrc, count, sig = ids.shape
    npts = kern.shape[-1]
    blk, width = panels[0][0].shape[1:]
    nt, npiece, no = len(panels), len(values), len(occ)
    total = nlocal * (nt * panels[0][0].shape[0] // nlocal)
    sizes = (nt, tmasks, npiece, xmasks, no, omasks, first, count, nlocal, rank)
    return pl.pallas_call(
        functools.partial(potential_kernel, sizes),
        out_shape=jax.ShapeDtypeStruct((nsrc, count, npts, width), BF16),
        in_specs=[SMEM, SMEM] + [ANY] * (nt + npiece) + [VMEM] * (no + 1),
        out_specs=VMEM,
        scratch_shapes=[
            pltpu.VMEM((total, blk, width), BF16),
            pltpu.VMEM((nsrc, count, npts, sig * blk), BF16),
            pltpu.VMEM((nsrc * count, npts, width), BF16),
            pltpu.VMEM((nsrc * count, npts, 2 * npts), BF16),
            pltpu.SemaphoreType.DMA((nt + npiece,)),
        ],
        compiler_params=PARAMS,
        name="potential",
    )(ids, meta, *[a for a, _ in panels], *[a for a, _ in values], *[a for a, _ in occ], kern)


def select_kernel(sizes, *refs):
    ncall, xmasks, rank, nown, group = sizes
    all_ids, refs = refs[:ncall], refs[ncall:]
    meta, refs = refs[0], refs[1:]
    values, (facts, columns, x, rows, place, xsems, osems) = refs[: len(xmasks)], refs[len(xmasks) :]
    sig = all_ids[0].shape[2]
    npts = x.shape[2]
    blk = x.shape[3] // sig
    copies = []
    at = 0
    entries = []
    groups = len(values) // ncall
    for i, piece in enumerate(values):
        size = piece.shape[0]
        copies.append(pltpu.make_async_copy(piece.at[:, :, pl.ds(0, npts)], x.at[pl.ds(at, size)], xsems.at[i]))
        if i % groups == 0:
            p = 0
        for j, mask in enumerate(xmasks[i]):
            entries += [(i // groups, p, mask, b, at + j) for b in range(x.shape[1])]
            p += 1
        at += size
    for c in copies:
        c.start()
    nlist = nown * ncall
    for o in range(nlist + 1):
        place[o] = 0

    def slot(chunk, p, b, s):
        own = all_ids[chunk][p, b, s] - meta[2]
        return jnp.where((own >= 0) & (own < nown), own * ncall + chunk, nlist)

    def blank(at, own, chunk):
        facts[0, at] = own
        facts[1, at] = chunk
        for f in range(2, 5):
            facts[f, at] = 0
        rows[at] = jnp.zeros(rows.shape[1:], BF16)

    for chunk, p, _, b, _ in entries:
        for s in range(sig):
            own = slot(chunk, p, b, s)
            place[own] = place[own] + 1
    n = jnp.int32(0)
    for o in range(nlist):
        size = place[o]
        place[o] = n
        odd = lax.rem(size, 2)

        @pl.when(odd == 1)
        def _(at=n + size, o=o):
            blank(at, o // ncall, o % ncall)

        n = n + size + odd
    blank(n, 0, 0)
    blank(n + 1, 0, 0)
    n = n + lax.rem(n, 4)
    facts[5, 0] = n
    for c in copies:
        c.wait()
    for chunk, p, mask, b, row in entries:

        def one(s, carry, chunk=chunk, p=p, mask=mask, b=b, row=row):
            own = slot(chunk, p, b, s)

            @pl.when(own < nlist)
            def _():
                to = place[own]
                place[own] = to + 1
                facts[0, to] = lax.div(own, ncall)
                facts[1, to] = chunk
                facts[2, to] = mask % rank
                facts[3, to] = meta[5] ^ (mask // rank)
                facts[4, to] = b
                rows[to] = x[row, b, :, pl.ds(pl.multiple_of(s * blk, blk), blk)].T

            return carry

        lax.fori_loop(0, sig, one, 0)
    outs = [
        pltpu.make_async_copy(rows.at[pl.ds(i * group, group)], columns.at[pl.ds(i * group, group)], osems.at[i])
        for i in range(columns.shape[0] // group)
    ]
    for act in ("start", "wait"):
        for i, c in enumerate(outs):

            @pl.when(i * group < n)
            def _(c=c, act=act):
                getattr(c, act)()


def select(values, all_ids, meta, rank, nown, npts, group):
    flat = [piece for pieces in values for piece in pieces]
    xmasks = tuple(tuple(m) for _, m in flat)
    nsrc, count, sig = all_ids[0].shape
    blk = flat[0][0].shape[-1] // sig
    most = -(-(len(values) * (nsrc * count * sig + nown) + 4) // group) * group
    return pl.pallas_call(
        functools.partial(select_kernel, (len(values), xmasks, rank, nown, group)),
        out_shape=(jax.ShapeDtypeStruct((6, most), jnp.int32), jax.ShapeDtypeStruct((most, blk, npts), BF16)),
        in_specs=[SMEM] * (len(values) + 1) + [ANY] * len(flat),
        out_specs=(SMEM, ANY),
        scratch_shapes=[
            pltpu.VMEM((len(values) * nsrc, count, npts, sig * blk), BF16),
            pltpu.VMEM((most, blk, npts), BF16),
            pltpu.SMEM((nown * len(values) + 1,), jnp.int32),
            pltpu.SemaphoreType.DMA((len(flat),)),
            pltpu.SemaphoreType.DMA((most // group,)),
        ],
        compiler_params=PARAMS,
        name="select",
    )(*all_ids, meta, *[a for a, _ in flat])


def project_kernel(sizes, facts, meta, columns, *refs):
    nchunk, emasks, rank, group, last = sizes
    ne = len(emasks)
    potentials, refs = refs[:ne], refs[ne:]
    before = refs[0] if last else None
    out, x, e, held, esems, xsems = refs[last:]
    nvs = e.shape[2]
    blk = x.shape[1]
    nown = held.shape[1] if last else out.shape[1]
    n = facts[5, 0]
    ecopies = []
    place = {}
    for i in range(ne):
        chunk, masks = emasks[i]
        for j, mask in enumerate(masks):
            k = place.setdefault((chunk, mask % rank), [])
            ecopies.append(
                pltpu.make_async_copy(
                    potentials[i].at[j], e.at[chunk, mask % rank, len(k)], esems.at[len(ecopies)]
                )
            )
            k.append(mask // rank)
    if last:
        ecopies.append(pltpu.make_async_copy(before, held, esems.at[len(ecopies)]))
    xcopies = [
        pltpu.make_async_copy(columns.at[pl.ds(i * group, group)], x.at[pl.ds(i * group, group)], xsems.at[i])
        for i in range(columns.shape[0] // group)
    ]
    for i, c in enumerate(xcopies):

        @pl.when(i * group < n)
        def _(c=c):
            c.start()

    for c in ecopies:
        c.start()
    total = held if last else out
    if not last:
        total[...] = jnp.zeros_like(total)
    for i, c in enumerate(xcopies):

        @pl.when(i * group < n)
        def _(c=c):
            c.wait()

    for c in ecopies:
        c.wait()

    def add(at):
        own, chunk = facts[0, at], facts[1, at]
        here = [[facts[f, at + t] for f in range(2, 5)] for t in range(2)]
        left = jnp.concatenate([x[at], x[at + 1]], axis=1)
        for k in range(nvs):
            off = jnp.int32(place[(0, 0)][k])
            for other in range(1, nchunk):
                off = jnp.where(chunk == other, place[(other, 0)][k], off)
            right = jnp.concatenate([e[chunk, side, k, source, b] for side, source, b in here], axis=0)
            total[meta[5] ^ off, own] += jnp.dot(left, right, preferred_element_type=F32)

    def one(i, carry):
        add(4 * i)
        add(4 * i + 2)
        return carry

    lax.fori_loop(0, lax.div(n, 4), one, 0)
    if last:
        nocc = out.shape[2]
        for v in range(out.shape[0]):
            for o in range(nown):
                for c in range(2):
                    out[v, pl.ds(o * 2 * blk + c, blk, stride=2), :] = total[v, o, :, c * nocc : (c + 1) * nocc]


def project(potentials, facts, columns, meta, before, rank, nown, group):
    emasks = tuple((chunk, tuple(m)) for chunk, _, m in potentials)
    nchunk = 1 + max(chunk for chunk, _, _ in potentials)
    nv, count, npts, width = potentials[0][1].shape[1:]
    blk = columns.shape[1]
    ne = len(potentials)
    slots = sum(len(m) for _, m in emasks) // nchunk // rank
    last = before is not None
    shape = (nv, nown * blk * 2, width // 2) if last else (nv, nown, blk, width)
    args = [facts, meta, columns, *[a for _, a, _ in potentials]] + ([before] if last else [])
    return pl.pallas_call(
        functools.partial(project_kernel, (nchunk, emasks, rank, group, int(last))),
        out_shape=jax.ShapeDtypeStruct(shape, F32),
        in_specs=[SMEM] * 2 + [ANY] * (1 + ne + int(last)),
        out_specs=VMEM,
        scratch_shapes=[
            pltpu.VMEM(columns.shape, BF16),
            pltpu.VMEM((nchunk, rank, slots, nv, count, npts, width), BF16),
            pltpu.VMEM((nv, nown, blk, width) if last else (8, 128), F32),
            pltpu.SemaphoreType.DMA((sum(len(m) for _, m in emasks) + 1,)),
            pltpu.SemaphoreType.DMA((columns.shape[0] // group,)),
        ],
        compiler_params=PARAMS,
        name="project",
    )(*args)


def swap(array, axis, bit):
    size = lax.axis_size(axis)
    return lax.ppermute(array, axis, [(i, i ^ bit) for i in range(size)])


def across(pieces, bits):
    for i, bit in enumerate(bits):
        got = [(swap(a, "grid", bit), [m ^ bit for m in masks]) for a, masks in pieces]
        if i + 1 < len(bits):
            pieces = [
                (jnp.concatenate([a, b], axis=0), masks + more) for (a, masks), (b, more) in zip(pieces, got, strict=True)
            ]
        else:
            pieces = pieces + got
    return pieces


def within(pieces, bits):
    for bit in bits:
        pieces = pieces + [(swap(a, "grid", bit), [m ^ bit for m in masks]) for a, masks in pieces]
    return pieces


def thirds(x):
    high = lax.reduce_precision(x, 8, 7)
    rest = x - high
    mid = lax.reduce_precision(rest, 8, 7)
    return [high, mid, rest - mid]


def on_device(trial, occupied, colloc, blocks, coords, weights):
    n_ao, n_grid = lax.axis_size("ao"), lax.axis_size("grid")
    batches, npts, span = colloc.shape
    sig = blocks.shape[1]
    blk = span // sig
    nvec, nocc = trial.shape[1], trial.shape[3]
    nv = nvec // n_ao
    rank = n_grid // nv
    nlocal = trial.shape[0] // blk
    nown = nlocal * n_ao // n_grid
    parts = min(rank, nlocal & -nlocal)
    nb = nlocal // parts
    count = batches // 2
    ao, grid = lax.axis_index("ao"), lax.axis_index("grid")
    vector, side = grid // rank, grid % parts
    meta = jnp.stack([ao * nlocal, ao * 0, grid * nown, ao, side, vector]).astype(jnp.int32)
    high_bits = [rank << b for b in range(nv.bit_length() - 1)]
    low_bits = [1 << b for b in range(rank.bit_length() - 1)]
    part_bits = [1 << b for b in range(parts.bit_length() - 1)]

    planes = list(reversed(range(n_ao)))
    where = jnp.stack([side * nb] + [(ao ^ over) * nv + vector for over in planes]).astype(jnp.int32)
    rows = pack(trial, where, n_ao, nb, blk)
    panels = []
    for over, one in zip(planes, rows, strict=True):
        panels.append((swap(one, "ao", over) if over else one, (over, 0)))
    own, occupied, colloc, blocks = lax.optimization_barrier((panels[-1][0], occupied, colloc, blocks))
    panels[-1] = (own, panels[-1][1])

    numbers = [blocks % 128, blocks // 128]
    numbers = [jnp.pad(a.astype(F32), ((0, 0), (0, npts - sig))) for a in numbers]
    exact = jnp.concatenate([coords, weights[:, None]], axis=1)
    extra = jnp.concatenate([jnp.stack(numbers, axis=1)] + thirds(exact), axis=1).astype(BF16)
    extra = jnp.pad(extra, ((0, 0), (0, EXTRA - extra.shape[1]), (0, span - npts)))
    payload = jnp.concatenate([colloc, extra], axis=1)
    near = []
    for chunk in range(2):
        part = payload[None, chunk * count : (chunk + 1) * count]
        near.append(across([(part, [0])], high_bits[::-1] if chunk else high_bits))

    held, send = occupied_part(occupied, colloc, blocks, meta, blk)
    for s in range(n_ao.bit_length() - 1):
        held = held + swap(send, "ao", 1 << s).astype(F32)
        send = held.astype(BF16)
    occ = across([(send[None], [0])], high_bits)

    for bit in part_bits:
        panels = panels + [(swap(a, "grid", bit), (over, m ^ bit)) for a, (over, m) in panels]
    far = [within(pieces, low_bits) for pieces in near]

    def facts_of(pieces):
        rows = jnp.concatenate([a[:, :, npts:, :npts] for a, _ in pieces], axis=0).astype(F32)
        ids = (rows[:, :, 0, :sig] + 128 * rows[:, :, 1, :sig]).astype(jnp.int32)
        return ids, rows[:, :, 2:6] + rows[:, :, 6:10] + rows[:, :, 10:14]

    early, late = [], []
    for chunk in range(2):
        ids, exact = facts_of(near[chunk])
        kern = kernel_matrix(exact[:, :, :3], exact[:, :, 3])
        e = potential(panels, near[chunk], occ, kern, ids, meta, chunk * count, nlocal, rank)
        pieces = across([(e[None], [0])], high_bits[::-1] if chunk else high_bits)
        early += [(chunk, a, m) for a, m in within(pieces[:1], low_bits)]
        late += [(chunk, a, m) for a, m in within(pieces[1:], low_bits)]
    group = 4 * sig
    all_ids = [facts_of(pieces)[0] for pieces in far]
    facts, columns = select(far, all_ids, meta, rank, nown, npts, group)
    total = project(early, facts, columns, meta, None, rank, nown, group)
    total = project(late, facts, columns, meta, total, rank, nown, group)
    return total.reshape(nv, nown * blk, 2, nocc)


def solution(mesh):
    in_specs = (
        P("ao", None, None, None),
        P("ao", None, None),
        P("grid", None, None),
        P("grid", None),
        P("grid", None, None),
        P("grid", None),
    )
    out_specs = P("ao", "grid", None, None)

    return jax.shard_map(on_device, mesh=mesh, in_specs=in_specs, out_specs=out_specs, check_vma=False)
```

```python
import functools

import jax
import jax.numpy as jnp
from jax import lax
from jax.experimental import pallas as pl
from jax.experimental.pallas import tpu as pltpu
from jax.sharding import PartitionSpec as P

F32 = jnp.float32
BF16 = jnp.bfloat16
PARAMS = pltpu.CompilerParams(vmem_limit_bytes=58 * 1024 * 1024)
SMEM = pl.BlockSpec(memory_space=pltpu.SMEM)
VMEM = pl.BlockSpec(memory_space=pltpu.VMEM)
ANY = pl.BlockSpec(memory_space=pl.ANY)


def kernel_matrix(points, quad):
    differ = points[..., :, None, :] - points[..., :, :, None]
    square = jnp.sum(differ * differ, axis=-3)
    return quad[..., :, None] * quad[..., None, :] / jnp.sqrt(square + 0.25)


def selectors(blk):
    ao = lax.broadcasted_iota(jnp.int32, (blk, 2 * blk), 0)
    col = lax.broadcasted_iota(jnp.int32, (blk, 2 * blk), 1)
    return [(col == 2 * ao + c).astype(F32).astype(BF16) for c in range(2)]


def pack_kernel(where, trial, *refs):
    outs, (rows, sem) = refs[:-2], refs[-2:]
    nb, blk, width = outs[0].shape
    nocc = width // 2
    copies = []
    for i in range(len(outs)):
        for j in range(nb):
            at = (where[0] + j) * blk
            copies.append(
                pltpu.make_async_copy(trial.at[pl.ds(at, blk), where[1 + i]], rows.at[i, j], sem.at[i, j])
            )
    for c in copies:
        c.start()
    pick = jnp.concatenate(selectors(blk), axis=0)
    for i, out in enumerate(outs):
        for j in range(0, nb, 2):
            ahead = range(j, min(j + 2, nb))
            for k in ahead:
                copies[i * nb + k].wait()
            both = jnp.concatenate([rows[i, k].reshape(2 * blk, nocc) for k in ahead], axis=1)
            split = jnp.dot(pick, both, preferred_element_type=F32).astype(BF16)
            for k in ahead:
                for c in range(2):
                    piece = split[c * blk : (c + 1) * blk, (k - j) * nocc : (k - j + 1) * nocc]
                    out[k, :, c * nocc : (c + 1) * nocc] = piece


def pack(trial, where, planes, nb, blk):
    nocc = trial.shape[3]
    return pl.pallas_call(
        pack_kernel,
        out_shape=(jax.ShapeDtypeStruct((nb, blk, 2 * nocc), BF16),) * planes,
        in_specs=[SMEM, ANY],
        out_specs=(VMEM,) * planes,
        scratch_shapes=[pltpu.VMEM((planes, nb, blk, 2, nocc), BF16), pltpu.SemaphoreType.DMA((planes, nb))],
        compiler_params=PARAMS,
        name="pack",
    )(where, trial)


def occupied_kernel(ids, meta, occupied, values, keep, send, table):
    batches, sig = ids.shape
    blk, nocc = occupied.shape[0] // (table.shape[0] - 1), occupied.shape[2]
    nlocal = table.shape[0] - 1
    pick = selectors(blk)
    for j in range(nlocal):
        both = occupied[j * blk : (j + 1) * blk].reshape(2 * blk, nocc)
        for c in range(2):
            split = jnp.dot(pick[c], both, preferred_element_type=F32)
            table[j, :, c * nocc : (c + 1) * nocc] = split.astype(BF16)
    table[nlocal] = jnp.zeros(table.shape[1:], BF16)

    def block(b, s):
        local = ids[b, s] - meta[0]
        return table[jnp.where((local >= 0) & (local < nlocal), local, nlocal)]

    for b in range(batches):
        total = jnp.zeros(keep.shape[1:], F32)
        for s in range(0, sig, 2):
            two = jnp.concatenate([block(b, s), block(b, s + 1)], axis=0)
            total += jnp.dot(values[b, :, s * blk : (s + 2) * blk], two, preferred_element_type=F32)
        keep[b] = total
        send[b] = total.astype(BF16)


def occupied_part(occupied, colloc, blocks, meta, blk):
    batches, npts, _ = colloc.shape
    nocc = occupied.shape[2]
    shape = (batches, npts, 2 * nocc)
    return pl.pallas_call(
        occupied_kernel,
        out_shape=(jax.ShapeDtypeStruct(shape, F32), jax.ShapeDtypeStruct(shape, BF16)),
        in_specs=[SMEM, SMEM, VMEM, VMEM],
        out_specs=(VMEM, VMEM),
        scratch_shapes=[pltpu.VMEM((occupied.shape[0] // blk + 1, blk, 2 * nocc), BF16)],
        compiler_params=PARAMS,
        name="occupied",
    )(blocks, meta, occupied, colloc)


def potential_kernel(sizes, ids, meta, *refs):
    tmasks, xmasks, omasks, fmasks, nlocal, rank, nchunk = sizes
    panels, refs = refs[: len(tmasks)], refs[len(tmasks) :]
    values, refs = refs[: len(xmasks)], refs[len(xmasks) :]
    occ, refs = refs[: len(omasks)], refs[len(omasks) :]
    kern, refs = refs[0], refs[1:]
    outs, (table, x, left, m, tsems, xsems) = refs[:nchunk], refs[nchunk:]
    nb, blk, width = panels[0].shape
    count, npts = x.shape[1], x.shape[2]
    sig = ids.shape[2]
    copies = []
    for i, (over, side) in enumerate(tmasks):
        at = (meta[3] ^ over) * nlocal + (meta[4] ^ side) * nb
        copies.append(pltpu.make_async_copy(panels[i], table.at[pl.ds(at, nb)], tsems.at[i]))
    loads = []
    todo = []
    at = 0
    groups = len(values) // nchunk
    for i, piece in enumerate(values):
        loads.append(pltpu.make_async_copy(piece, x.at[pl.ds(at, piece.shape[0])], xsems.at[i]))
        for j, mask in enumerate(xmasks[i]):
            todo += [(i, i // groups, at + j, mask, b) for b in range(count)]
        at += piece.shape[0]
    for c in copies + loads:
        c.start()
    where = {mask: (i, j) for i, masks in enumerate(omasks) for j, mask in enumerate(masks)}
    dims = (((1,), (1,)), ((), ()))

    def turn_of(mask, b):
        piece, row = where[mask]
        og = occ[piece][row, b]
        half = width // 2
        return jnp.concatenate([og, jnp.concatenate([-og[:, half:], og[:, :half]], axis=1)], axis=0)

    for c in copies:
        c.wait()
    seen = -1
    for i, (piece, chunk, row, mask, b) in enumerate(todo):
        if piece != seen:
            loads[piece].wait()
            seen = piece
        f = fmasks.index(mask)
        dens = jnp.zeros((npts, width), F32)
        for s in range(0, sig, 2):
            two = [table[ids[f, chunk * count + b, s + t]] for t in range(2)]
            dens += jnp.dot(
                x[row, b, :, s * blk : (s + 2) * blk], jnp.concatenate(two, axis=0), preferred_element_type=F32
            )
        left[i] = dens.astype(BF16)
    for i, (_, chunk, _, mask, b) in enumerate(todo):
        rho = lax.dot_general(left[i], turn_of(mask, chunk * count + b), dims, preferred_element_type=F32)
        weight = kern[fmasks.index(mask), chunk * count + b]
        m[i] = (rho * jnp.concatenate([weight, weight], axis=1)).astype(BF16)
    for i, (_, chunk, _, mask, b) in enumerate(todo):
        e = jnp.dot(m[i], turn_of(mask, chunk * count + b), preferred_element_type=F32)
        outs[chunk][meta[5] ^ (mask // rank), b] = e.astype(BF16)


def potential(panels, values, occ, kern, ids, fmasks, meta, nlocal, rank):
    tmasks = tuple(m for _, m in panels)
    flat = [piece for pieces in values for piece in pieces]
    xmasks = tuple(tuple(m) for _, m in flat)
    omasks = tuple(tuple(m) for _, m in occ)
    nchunk = len(values)
    count, npts, span = flat[0][0].shape[1:]
    nb, blk, width = panels[0][0].shape
    nsrc = sum(len(m) for m in xmasks) // nchunk
    sizes = (tmasks, xmasks, omasks, tuple(fmasks), nlocal, rank, nchunk)
    out = jax.ShapeDtypeStruct((nsrc, count, npts, width), BF16)
    return pl.pallas_call(
        functools.partial(potential_kernel, sizes),
        out_shape=(out,) * nchunk,
        in_specs=[SMEM, SMEM] + [ANY] * (len(panels) + len(flat)) + [VMEM] * (len(occ) + 1),
        out_specs=(VMEM,) * nchunk,
        scratch_shapes=[
            pltpu.VMEM((len(panels) * nb, blk, width), BF16),
            pltpu.VMEM((nchunk * nsrc, count, npts, span), BF16),
            pltpu.VMEM((nchunk * nsrc * count, npts, width), BF16),
            pltpu.VMEM((nchunk * nsrc * count, npts, 2 * npts), BF16),
            pltpu.SemaphoreType.DMA((len(panels),)),
            pltpu.SemaphoreType.DMA((len(flat),)),
        ],
        compiler_params=PARAMS,
        name="potential",
    )(ids, meta, *[a for a, _ in panels], *[a for a, _ in flat], *[a for a, _ in occ], kern)


def list_kernel(sizes, ids, meta, facts, place):
    entries, nchunk, rank, nown = sizes
    sig = ids.shape[2]
    nlist = nown * nchunk
    for o in range(nlist + 1):
        place[o] = 0

    def slot(f, b, chunk, s):
        own = ids[f, b, s] - meta[2]
        return jnp.where((own >= 0) & (own < nown), own * nchunk + chunk, nlist)

    def put(at, *what):
        for f, one in enumerate(what):
            facts[f, at] = jnp.int32(one)

    for f, b, _, chunk, _, _ in entries:
        for s in range(sig):
            own = slot(f, b, chunk, s)
            place[own] = place[own] + 1
    n = jnp.int32(0)
    for o in range(nlist):
        size = place[o]
        place[o] = n
        odd = lax.rem(size, 2)

        @pl.when(odd == 1)
        def _(at=n + size, o=o):
            put(at, o // nchunk, o % nchunk, 0, 0, 0, -1, 0)

        n = n + size + odd
    put(n, 0, 0, 0, 0, 0, -1, 0)
    put(n + 1, 0, 0, 0, 0, 0, -1, 0)
    facts[7, 0] = n + lax.rem(n, 4)
    for f, b, mask, chunk, row, inner in entries:
        for s in range(sig):
            own = slot(f, b, chunk, s)

            @pl.when(own < nlist)
            def _(f=f, b=b, mask=mask, chunk=chunk, row=row, inner=inner, s=s, own=own):
                to = place[own]
                place[own] = to + 1
                put(to, lax.div(own, nchunk), chunk, mask % rank, meta[5] ^ (mask // rank), inner, row, s)


def entries_of(xmasks, fmasks, nchunk, count):
    out = []
    at = 0
    groups = len(xmasks) // nchunk
    for i, masks in enumerate(xmasks):
        chunk = i // groups
        for j, mask in enumerate(masks):
            out += [(fmasks.index(mask), chunk * count + b, mask, chunk, at + j, b) for b in range(count)]
        at += len(masks)
    return tuple(out)


def pair_list(xmasks, ids, fmasks, meta, rank, nown, nchunk, count, group):
    nsrc, _, sig = ids.shape
    most = -(-(nchunk * (nsrc * count * sig + nown) + 4) // group) * group
    sizes = (entries_of(xmasks, fmasks, nchunk, count), nchunk, rank, nown)
    return pl.pallas_call(
        functools.partial(list_kernel, sizes),
        out_shape=jax.ShapeDtypeStruct((8, most), jnp.int32),
        in_specs=[SMEM, SMEM],
        out_specs=SMEM,
        scratch_shapes=[pltpu.SMEM((nown * nchunk + 1,), jnp.int32)],
        compiler_params=PARAMS,
        name="pairs",
    )(ids, meta)


def gather_kernel(group, facts, *refs):
    values, (columns, x, rows, xsems, osems) = refs[:-5], refs[-5:]
    blk = rows.shape[1]
    copies = []
    at = 0
    for i, piece in enumerate(values):
        copies.append(pltpu.make_async_copy(piece, x.at[pl.ds(at, piece.shape[0])], xsems.at[i]))
        at += piece.shape[0]
    for c in copies:
        c.start()
    for c in copies:
        c.wait()
    n = facts[7, 0]

    def one(i, carry):
        for t in range(4):
            row = facts[5, 4 * i + t]
            start = pl.multiple_of(facts[6, 4 * i + t] * blk, blk)
            column = x[jnp.maximum(row, 0), facts[4, 4 * i + t], :, pl.ds(start, blk)]
            rows[4 * i + t] = jnp.where(row >= 0, column, jnp.zeros_like(column)).T
        return carry

    lax.fori_loop(0, lax.div(n, 4), one, 0)
    outs = [
        pltpu.make_async_copy(rows.at[pl.ds(i * group, group)], columns.at[pl.ds(i * group, group)], osems.at[i])
        for i in range(columns.shape[0] // group)
    ]
    for act in ("start", "wait"):
        for i, c in enumerate(outs):

            @pl.when(i * group < n)
            def _(c=c, act=act):
                getattr(c, act)()


def gather(values, facts, blk, group):
    flat = [a for pieces in values for a, _ in pieces]
    count, npts, span = flat[0].shape[1:]
    most = facts.shape[1]
    return pl.pallas_call(
        functools.partial(gather_kernel, group),
        out_shape=jax.ShapeDtypeStruct((most, blk, npts), BF16),
        in_specs=[SMEM] + [ANY] * len(flat),
        out_specs=ANY,
        scratch_shapes=[
            pltpu.VMEM((sum(a.shape[0] for a in flat), count, npts, span), BF16),
            pltpu.VMEM((most, blk, npts), BF16),
            pltpu.SemaphoreType.DMA((len(flat),)),
            pltpu.SemaphoreType.DMA((most // group,)),
        ],
        compiler_params=PARAMS,
        name="gather",
    )(facts, *flat)


def project_kernel(sizes, facts, meta, columns, *refs):
    nchunk, emasks, rank, group, last = sizes
    ne = len(emasks)
    potentials, refs = refs[:ne], refs[ne:]
    before = refs[0] if last else None
    out, x, e, held, staged, esems, xsems, osems = refs[last:]
    nvs = e.shape[2]
    blk = x.shape[1]
    nown = held.shape[1] if last else out.shape[1]
    n = facts[7, 0]
    ecopies = []
    place = {}
    for i in range(ne):
        chunk, masks = emasks[i]
        for j, mask in enumerate(masks):
            k = place.setdefault((chunk, mask % rank), [])
            ecopies.append(
                pltpu.make_async_copy(
                    potentials[i].at[j], e.at[chunk, mask % rank, len(k)], esems.at[len(ecopies)]
                )
            )
            k.append(mask // rank)
    if last:
        ecopies.append(pltpu.make_async_copy(before, held, esems.at[len(ecopies)]))
    xcopies = [
        pltpu.make_async_copy(columns.at[pl.ds(i * group, group)], x.at[pl.ds(i * group, group)], xsems.at[i])
        for i in range(columns.shape[0] // group)
    ]
    for i, c in enumerate(xcopies):

        @pl.when(i * group < n)
        def _(c=c):
            c.start()

    for c in ecopies:
        c.start()
    total = held if last else out
    if not last:
        total[...] = jnp.zeros_like(total)
    for i, c in enumerate(xcopies):

        @pl.when(i * group < n)
        def _(c=c):
            c.wait()

    for c in ecopies:
        c.wait()

    def add(at):
        own, chunk = facts[0, at], facts[1, at]
        here = [[facts[f, at + t] for f in range(2, 5)] for t in range(2)]
        left = jnp.concatenate([x[at], x[at + 1]], axis=1)
        for k in range(nvs):
            off = jnp.int32(place[(0, 0)][k])
            for other in range(1, nchunk):
                off = jnp.where(chunk == other, place[(other, 0)][k], off)
            right = jnp.concatenate([e[chunk, side, k, source, b] for side, source, b in here], axis=0)
            total[meta[5] ^ off, own] += jnp.dot(left, right, preferred_element_type=F32)

    def one(i, carry):
        add(4 * i)
        add(4 * i + 2)
        return carry

    lax.fori_loop(0, lax.div(n, 4), one, 0)
    if last:
        nocc = out.shape[2]
        copies = [pltpu.make_async_copy(staged.at[v], out.at[v], osems.at[v]) for v in range(out.shape[0])]
        for v in range(out.shape[0]):
            for o in range(nown):
                for c in range(2):
                    staged[v, pl.ds(o * 2 * blk + c, blk, stride=2), :] = total[v, o, :, c * nocc : (c + 1) * nocc]
            copies[v].start()
        for c in copies:
            c.wait()


def project(potentials, facts, columns, meta, before, rank, nown, group):
    emasks = tuple((chunk, tuple(m)) for chunk, _, m in potentials)
    nchunk = 1 + max(chunk for chunk, _, _ in potentials)
    nv, count, npts, width = potentials[0][1].shape[1:]
    blk = columns.shape[1]
    ne = len(potentials)
    slots = sum(len(m) for _, m in emasks) // nchunk // rank
    last = before is not None
    shape = (nv, nown * blk * 2, width // 2) if last else (nv, nown, blk, width)
    args = [facts, meta, columns, *[a for _, a, _ in potentials]] + ([before] if last else [])
    return pl.pallas_call(
        functools.partial(project_kernel, (nchunk, emasks, rank, group, int(last))),
        out_shape=jax.ShapeDtypeStruct(shape, F32),
        in_specs=[SMEM] * 2 + [ANY] * (1 + ne + int(last)),
        out_specs=ANY if last else VMEM,
        scratch_shapes=[
            pltpu.VMEM(columns.shape, BF16),
            pltpu.VMEM((nchunk, rank, slots, nv, count, npts, width), BF16),
            pltpu.VMEM((nv, nown, blk, width) if last else (8, 128), F32),
            pltpu.VMEM(shape if last else (8, 128), F32),
            pltpu.SemaphoreType.DMA((sum(len(m) for _, m in emasks) + 1,)),
            pltpu.SemaphoreType.DMA((columns.shape[0] // group,)),
            pltpu.SemaphoreType.DMA((nv,)),
        ],
        compiler_params=PARAMS,
        name="project",
    )(*args)


def swap(array, axis, bit):
    size = lax.axis_size(axis)
    return lax.ppermute(array, axis, [(i, i ^ bit) for i in range(size)])


def across(pieces, bits):
    for i, bit in enumerate(bits):
        got = [(swap(a, "grid", bit), [m ^ bit for m in masks]) for a, masks in pieces]
        if i + 1 < len(bits):
            pieces = [
                (jnp.concatenate([a, b], axis=0), masks + more) for (a, masks), (b, more) in zip(pieces, got, strict=True)
            ]
        else:
            pieces = pieces + got
    return pieces


def within(pieces, bits):
    for bit in bits:
        pieces = pieces + [(swap(a, "grid", bit), [m ^ bit for m in masks]) for a, masks in pieces]
    return pieces


def thirds(x):
    high = lax.reduce_precision(x, 8, 7)
    rest = x - high
    mid = lax.reduce_precision(rest, 8, 7)
    return [high, mid, rest - mid]


def on_device(trial, occupied, colloc, blocks, coords, weights):
    n_ao, n_grid = lax.axis_size("ao"), lax.axis_size("grid")
    batches, npts, span = colloc.shape
    sig = blocks.shape[1]
    blk = span // sig
    nvec, nocc = trial.shape[1], trial.shape[3]
    nv = nvec // n_ao
    rank = n_grid // nv
    nlocal = trial.shape[0] // blk
    nown = nlocal * n_ao // n_grid
    parts = min(rank, nlocal & -nlocal)
    nb = nlocal // parts
    count = batches // 2
    ao, grid = lax.axis_index("ao"), lax.axis_index("grid")
    vector, side = grid // rank, grid % parts
    meta = jnp.stack([ao * nlocal, ao * 0, grid * nown, ao, side, vector]).astype(jnp.int32)
    high_bits = [rank << b for b in range(nv.bit_length() - 1)]
    low_bits = [1 << b for b in range(rank.bit_length() - 1)]
    part_bits = [1 << b for b in range(parts.bit_length() - 1)]

    panels = []
    far_first = list(reversed(range(n_ao)))
    for planes in (far_first[:1], far_first[1:]):
        where = jnp.stack([side * nb] + [(ao ^ over) * nv + vector for over in planes]).astype(jnp.int32)
        if panels:
            where, occupied = lax.optimization_barrier((where, occupied))
        rows = pack(trial, where, len(planes), nb, blk)
        for over, one in zip(planes, rows, strict=True):
            panels.append((swap(one, "ao", over) if over else one, (over, 0)))

    near = []
    for chunk in range(2):
        part = colloc[None, chunk * count : (chunk + 1) * count]
        near.append(across([(part, [0])], high_bits[::-1] if chunk else high_bits))
    far = [within(pieces, low_bits) for pieces in near]

    held, send = occupied_part(occupied, colloc, blocks, meta, blk)
    for s in range(n_ao.bit_length() - 1):
        held = held + swap(send, "ao", 1 << s).astype(F32)
        send = held.astype(BF16)
    occ = across([(send[None], [0])], high_bits)

    numbers = [blocks % 128, blocks // 128]
    numbers = [jnp.pad(a.astype(F32), ((0, 0), (0, npts - sig))) for a in numbers]
    exact = jnp.concatenate([coords, weights[:, None]], axis=1)
    extra = jnp.concatenate([jnp.stack(numbers, axis=1)] + thirds(exact), axis=1).astype(BF16)
    extra = within(across([(extra[None], [0])], high_bits), low_bits)
    fmasks = [m for _, masks in extra for m in masks]
    extra = jnp.concatenate([a for a, _ in extra], axis=0).astype(F32)
    ids = (extra[:, :, 0, :sig] + 128 * extra[:, :, 1, :sig]).astype(jnp.int32)
    exact = (extra[:, :, 2:6] + extra[:, :, 6:10] + extra[:, :, 10:14])[: nv]
    kern = kernel_matrix(exact[:, :, :3], exact[:, :, 3])
    group = 4 * sig
    xmasks = [m for pieces in far for _, m in pieces]
    facts = pair_list(xmasks, ids, fmasks, meta, rank, nown, 2, count, group)

    for bit in part_bits:
        panels = panels + [(swap(a, "grid", bit), (over, m ^ bit)) for a, (over, m) in panels]
    columns = gather(far, facts, blk, group)
    parts = potential(panels, near, occ, kern, ids, fmasks, meta, nlocal, rank)
    early, late = [], []
    for chunk in range(2):
        pieces = across([(parts[chunk][None], [0])], high_bits[::-1] if chunk else high_bits)
        early += [(chunk, a, m) for a, m in within(pieces[:1], low_bits)]
        late += [(chunk, a, m) for a, m in within(pieces[1:], low_bits)]
    total = project(early, facts, columns, meta, None, rank, nown, group)
    total = project(late, facts, columns, meta, total, rank, nown, group)
    return total.reshape(nv, nown * blk, 2, nocc)


def solution(mesh):
    in_specs = (
        P("ao", None, None, None),
        P("ao", None, None),
        P("grid", None, None),
        P("grid", None),
        P("grid", None, None),
        P("grid", None),
    )
    out_specs = P("ao", "grid", None, None)

    return jax.shard_map(on_device, mesh=mesh, in_specs=in_specs, out_specs=out_specs, check_vma=False)
```

```python
import functools

import jax
import jax.numpy as jnp
from jax import lax
from jax.experimental import pallas as pl
from jax.experimental.pallas import tpu as pltpu
from jax.sharding import PartitionSpec as P

F32 = jnp.float32
BF16 = jnp.bfloat16
PARAMS = pltpu.CompilerParams(vmem_limit_bytes=58 * 1024 * 1024)
SMEM = pl.BlockSpec(memory_space=pltpu.SMEM)
VMEM = pl.BlockSpec(memory_space=pltpu.VMEM)
ANY = pl.BlockSpec(memory_space=pl.ANY)


def kernel_matrix(points, quad):
    differ = points[..., :, None, :] - points[..., :, :, None]
    square = jnp.sum(differ * differ, axis=-3)
    return quad[..., :, None] * quad[..., None, :] / jnp.sqrt(square + 0.25)


def selectors(blk):
    ao = lax.broadcasted_iota(jnp.int32, (blk, 2 * blk), 0)
    col = lax.broadcasted_iota(jnp.int32, (blk, 2 * blk), 1)
    return [(col == 2 * ao + c).astype(F32).astype(BF16) for c in range(2)]


def pack_kernel(where, trial, *refs):
    outs, (rows, sem) = refs[:-2], refs[-2:]
    nb, blk, width = outs[0].shape
    nocc = width // 2
    copies = []
    for i in range(len(outs)):
        for j in range(nb):
            at = (where[0] + j) * blk
            copies.append(
                pltpu.make_async_copy(trial.at[pl.ds(at, blk), where[1 + i]], rows.at[i, j], sem.at[i, j])
            )
    for c in copies:
        c.start()
    pick = jnp.concatenate(selectors(blk), axis=0)
    for i, out in enumerate(outs):
        for j in range(0, nb, 2):
            ahead = range(j, min(j + 2, nb))
            for k in ahead:
                copies[i * nb + k].wait()
            both = jnp.concatenate([rows[i, k].reshape(2 * blk, nocc) for k in ahead], axis=1)
            split = jnp.dot(pick, both, preferred_element_type=F32).astype(BF16)
            for k in ahead:
                for c in range(2):
                    piece = split[c * blk : (c + 1) * blk, (k - j) * nocc : (k - j + 1) * nocc]
                    out[k, :, c * nocc : (c + 1) * nocc] = piece


def pack(trial, where, planes, nb, blk):
    nocc = trial.shape[3]
    return pl.pallas_call(
        pack_kernel,
        out_shape=(jax.ShapeDtypeStruct((nb, blk, 2 * nocc), BF16),) * planes,
        in_specs=[SMEM, ANY],
        out_specs=(VMEM,) * planes,
        scratch_shapes=[pltpu.VMEM((planes, nb, blk, 2, nocc), BF16), pltpu.SemaphoreType.DMA((planes, nb))],
        compiler_params=PARAMS,
        name="pack",
    )(where, trial)


def occupied_kernel(ids, meta, occupied, values, keep, send, table):
    batches, sig = ids.shape
    blk, nocc = occupied.shape[0] // (table.shape[0] - 1), occupied.shape[2]
    nlocal = table.shape[0] - 1
    pick = selectors(blk)
    for j in range(nlocal):
        both = occupied[j * blk : (j + 1) * blk].reshape(2 * blk, nocc)
        for c in range(2):
            split = jnp.dot(pick[c], both, preferred_element_type=F32)
            table[j, :, c * nocc : (c + 1) * nocc] = split.astype(BF16)
    table[nlocal] = jnp.zeros(table.shape[1:], BF16)

    def block(b, s):
        local = ids[b, s] - meta[0]
        return table[jnp.where((local >= 0) & (local < nlocal), local, nlocal)]

    for b in range(batches):
        total = jnp.zeros(keep.shape[1:], F32)
        for s in range(0, sig, 2):
            two = jnp.concatenate([block(b, s), block(b, s + 1)], axis=0)
            total += jnp.dot(values[b, :, s * blk : (s + 2) * blk], two, preferred_element_type=F32)
        keep[b] = total
        send[b] = total.astype(BF16)


def occupied_part(occupied, colloc, blocks, meta, blk):
    batches, npts, _ = colloc.shape
    nocc = occupied.shape[2]
    shape = (batches, npts, 2 * nocc)
    return pl.pallas_call(
        occupied_kernel,
        out_shape=(jax.ShapeDtypeStruct(shape, F32), jax.ShapeDtypeStruct(shape, BF16)),
        in_specs=[SMEM, SMEM, VMEM, VMEM],
        out_specs=(VMEM, VMEM),
        scratch_shapes=[pltpu.VMEM((occupied.shape[0] // blk + 1, blk, 2 * nocc), BF16)],
        compiler_params=PARAMS,
        name="occupied",
    )(blocks, meta, occupied, colloc)


def potential_kernel(sizes, ids, meta, *refs):
    tmasks, xmasks, omasks, fmasks, nlocal, rank, nchunk = sizes
    panels, refs = refs[: len(tmasks)], refs[len(tmasks) :]
    values, refs = refs[: len(xmasks)], refs[len(xmasks) :]
    occ, refs = refs[: len(omasks)], refs[len(omasks) :]
    kern, refs = refs[0], refs[1:]
    outs, (table, x, left, m, tsems, xsems) = refs[:nchunk], refs[nchunk:]
    nb, blk, width = panels[0].shape
    count, npts = x.shape[1], x.shape[2]
    sig = ids.shape[2]
    copies = []
    for i, (over, side) in enumerate(tmasks):
        at = (meta[3] ^ over) * nlocal + (meta[4] ^ side) * nb
        copies.append(pltpu.make_async_copy(panels[i], table.at[pl.ds(at, nb)], tsems.at[i]))
    loads = []
    todo = []
    at = 0
    groups = len(values) // nchunk
    for i, piece in enumerate(values):
        loads.append(pltpu.make_async_copy(piece, x.at[pl.ds(at, piece.shape[0])], xsems.at[i]))
        for j, mask in enumerate(xmasks[i]):
            todo += [(i, i // groups, at + j, mask, b) for b in range(count)]
        at += piece.shape[0]
    for c in copies + loads:
        c.start()
    where = {mask: (i, j) for i, masks in enumerate(omasks) for j, mask in enumerate(masks)}
    dims = (((1,), (1,)), ((), ()))

    def turn_of(mask, b):
        piece, row = where[mask]
        og = occ[piece][row, b]
        half = width // 2
        return jnp.concatenate([og, jnp.concatenate([-og[:, half:], og[:, :half]], axis=1)], axis=0)

    for c in copies:
        c.wait()
    seen = -1
    for i, (piece, chunk, row, mask, b) in enumerate(todo):
        if piece != seen:
            loads[piece].wait()
            seen = piece
        f = fmasks.index(mask)
        dens = jnp.zeros((npts, width), F32)
        for s in range(0, sig, 2):
            two = [table[ids[f, chunk * count + b, s + t]] for t in range(2)]
            dens += jnp.dot(
                x[row, b, :, s * blk : (s + 2) * blk], jnp.concatenate(two, axis=0), preferred_element_type=F32
            )
        left[i] = dens.astype(BF16)
    for i, (_, chunk, _, mask, b) in enumerate(todo):
        rho = lax.dot_general(left[i], turn_of(mask, chunk * count + b), dims, preferred_element_type=F32)
        weight = kern[fmasks.index(mask), chunk * count + b]
        m[i] = (rho * jnp.concatenate([weight, weight], axis=1)).astype(BF16)
    for i, (_, chunk, _, mask, b) in enumerate(todo):
        e = jnp.dot(m[i], turn_of(mask, chunk * count + b), preferred_element_type=F32)
        outs[chunk][meta[5] ^ (mask // rank), b] = e.astype(BF16)


def potential(panels, values, occ, kern, ids, fmasks, meta, nlocal, rank):
    tmasks = tuple(m for _, m in panels)
    flat = [piece for pieces in values for piece in pieces]
    xmasks = tuple(tuple(m) for _, m in flat)
    omasks = tuple(tuple(m) for _, m in occ)
    nchunk = len(values)
    count, npts, span = flat[0][0].shape[1:]
    nb, blk, width = panels[0][0].shape
    nsrc = sum(len(m) for m in xmasks) // nchunk
    sizes = (tmasks, xmasks, omasks, tuple(fmasks), nlocal, rank, nchunk)
    out = jax.ShapeDtypeStruct((nsrc, count, npts, width), BF16)
    return pl.pallas_call(
        functools.partial(potential_kernel, sizes),
        out_shape=(out,) * nchunk,
        in_specs=[SMEM, SMEM] + [VMEM] * len(panels) + [ANY] * len(flat) + [VMEM] * (len(occ) + 1),
        out_specs=(VMEM,) * nchunk,
        scratch_shapes=[
            pltpu.VMEM((len(panels) * nb, blk, width), BF16),
            pltpu.VMEM((nchunk * nsrc, count, npts, span), BF16),
            pltpu.VMEM((nchunk * nsrc * count, npts, width), BF16),
            pltpu.VMEM((nchunk * nsrc * count, npts, 2 * npts), BF16),
            pltpu.SemaphoreType.DMA((len(panels),)),
            pltpu.SemaphoreType.DMA((len(flat),)),
        ],
        compiler_params=PARAMS,
        name="potential",
    )(ids, meta, *[a for a, _ in panels], *[a for a, _ in flat], *[a for a, _ in occ], kern)


def list_kernel(sizes, ids, meta, facts, place):
    entries, nchunk, rank, nown = sizes
    sig = ids.shape[2]
    nlist = nchunk * rank
    sizes = []
    for t in range(nlist):
        n = jnp.int32(0)
        for f, b, mask, chunk, _, _ in entries:
            if chunk * rank + mask % rank == t:
                for s in range(sig):
                    own = ids[f, b, s] - meta[2]
                    n = n + ((own >= 0) & (own < nown)).astype(jnp.int32)
        sizes.append(n)
    n = jnp.int32(0)
    for t in range(nlist):
        facts[5, t] = n
        place[t] = n
        end = n + sizes[t]
        for k in range(3):
            for f, one in enumerate((0, 0, 0, -1, 0)):
                facts[f, end + k] = jnp.int32(one)
        n = lax.div(end + 3, 4) * 4
    facts[5, nlist] = n
    for f, b, mask, chunk, row, inner in entries:
        for s in range(sig):
            own = ids[f, b, s] - meta[2]

            @pl.when((own >= 0) & (own < nown))
            def _(mask=mask, t=chunk * rank + mask % rank, row=row, inner=inner, s=s, own=own):
                to = place[t]
                place[t] = to + 1
                what = (own, meta[5] ^ (mask // rank), jnp.int32(inner), jnp.int32(row), jnp.int32(s))
                for f, one in enumerate(what):
                    facts[f, to] = one


def entries_of(xmasks, fmasks, nchunk, count):
    out = []
    at = 0
    groups = len(xmasks) // nchunk
    for i, masks in enumerate(xmasks):
        chunk = i // groups
        for j, mask in enumerate(masks):
            out += [(fmasks.index(mask), chunk * count + b, mask, chunk, at + j, b) for b in range(count)]
        at += len(masks)
    return tuple(out)


def pair_list(xmasks, ids, fmasks, meta, rank, nown, nchunk, count, group):
    nsrc, _, sig = ids.shape
    most = -(-(nchunk * (nsrc * count * sig + 3 * rank) + 4) // group) * group
    sizes = (entries_of(xmasks, fmasks, nchunk, count), nchunk, rank, nown)
    return pl.pallas_call(
        functools.partial(list_kernel, sizes),
        out_shape=jax.ShapeDtypeStruct((8, most), jnp.int32),
        in_specs=[SMEM, SMEM],
        out_specs=SMEM,
        scratch_shapes=[pltpu.SMEM((nchunk * rank,), jnp.int32)],
        compiler_params=PARAMS,
        name="pairs",
    )(ids, meta)


def gather_kernel(group, nlist, facts, *refs):
    values, (columns, x, rows, xsems, osems) = refs[:-5], refs[-5:]
    blk = rows.shape[1]
    copies = []
    at = 0
    for i, piece in enumerate(values):
        copies.append(pltpu.make_async_copy(piece, x.at[pl.ds(at, piece.shape[0])], xsems.at[i]))
        at += piece.shape[0]
    for c in copies:
        c.start()
    for c in copies:
        c.wait()
    n = facts[5, nlist]

    def one(i, carry):
        for t in range(4):
            row = facts[3, 4 * i + t]
            start = pl.multiple_of(facts[4, 4 * i + t] * blk, blk)
            column = x[jnp.maximum(row, 0), facts[2, 4 * i + t], :, pl.ds(start, blk)]
            rows[4 * i + t] = jnp.where(row >= 0, column, jnp.zeros_like(column)).T
        return carry

    lax.fori_loop(0, lax.div(n, 4), one, 0)
    outs = [
        pltpu.make_async_copy(rows.at[pl.ds(i * group, group)], columns.at[pl.ds(i * group, group)], osems.at[i])
        for i in range(columns.shape[0] // group)
    ]
    for act in ("start", "wait"):
        for i, c in enumerate(outs):

            @pl.when(i * group < n)
            def _(c=c, act=act):
                getattr(c, act)()


def gather(values, facts, blk, group, nlist):
    flat = [a for pieces in values for a, _ in pieces]
    count, npts, span = flat[0].shape[1:]
    most = facts.shape[1]
    return pl.pallas_call(
        functools.partial(gather_kernel, group, nlist),
        out_shape=jax.ShapeDtypeStruct((most, blk, npts), BF16),
        in_specs=[SMEM] + [ANY] * len(flat),
        out_specs=ANY,
        scratch_shapes=[
            pltpu.VMEM((sum(a.shape[0] for a in flat), count, npts, span), BF16),
            pltpu.VMEM((most, blk, npts), BF16),
            pltpu.SemaphoreType.DMA((len(flat),)),
            pltpu.SemaphoreType.DMA((most // group,)),
        ],
        compiler_params=PARAMS,
        name="gather",
    )(facts, *flat)


def project_kernel(sizes, facts, meta, columns, *refs):
    nchunk, emasks, rank, group, last = sizes
    ne = len(emasks)
    potentials, refs = refs[:ne], refs[ne:]
    held = refs[0] if last else None
    out, x, staged, acc, xsems, osems = refs[last:]
    total = acc if last else out
    nown, blk = total.shape[1:3]
    n = facts[5, nchunk * rank]
    xcopies = [
        pltpu.make_async_copy(columns.at[pl.ds(i * group, group)], x.at[pl.ds(i * group, group)], xsems.at[i])
        for i in range(columns.shape[0] // group)
    ]
    for i, c in enumerate(xcopies):

        @pl.when(i * group < n)
        def _(c=c):
            c.start()

    total[...] = held[...] if last else jnp.zeros_like(total)
    for i, c in enumerate(xcopies):

        @pl.when(i * group < n)
        def _(c=c):
            c.wait()

    for t in range(nchunk * rank):
        mine = [
            (i, j, meta[5] ^ (mask // rank))
            for i, (chunk, masks) in enumerate(emasks)
            for j, mask in enumerate(masks)
            if chunk * rank + mask % rank == t
        ]

        def one(p, carry, mine=mine):
            for at in range(4):
                own, source, b = [facts[f, 4 * p + at] for f in range(3)]
                for i, j, vec in mine:
                    total[vec, own] += jnp.dot(
                        x[4 * p + at], potentials[i][j, source, b], preferred_element_type=F32
                    )
            return carry

        lax.fori_loop(lax.div(facts[5, t], 4), lax.div(facts[5, t + 1], 4), one, 0)
    if last:
        nocc = out.shape[2]
        copies = [pltpu.make_async_copy(staged.at[v], out.at[v], osems.at[v]) for v in range(out.shape[0])]
        for v in range(out.shape[0]):
            for o in range(nown):
                for c in range(2):
                    staged[v, pl.ds(o * 2 * blk + c, blk, stride=2), :] = total[v, o, :, c * nocc : (c + 1) * nocc]
            copies[v].start()
        for c in copies:
            c.wait()


def project(potentials, facts, columns, meta, before, rank, nown, group):
    emasks = tuple((chunk, tuple(m)) for chunk, _, m in potentials)
    nchunk = 1 + max(chunk for chunk, _, _ in potentials)
    nv, _, _, width = potentials[0][1].shape[1:]
    blk = columns.shape[1]
    ne = len(potentials)
    last = before is not None
    shape = (nv, nown * blk * 2, width // 2) if last else (nv, nown, blk, width)
    args = [facts, meta, columns, *[a for _, a, _ in potentials]] + ([before] if last else [])
    return pl.pallas_call(
        functools.partial(project_kernel, (nchunk, emasks, rank, group, int(last))),
        out_shape=jax.ShapeDtypeStruct(shape, F32),
        in_specs=[SMEM] * 2 + [ANY] + [VMEM] * (ne + int(last)),
        out_specs=ANY if last else VMEM,
        scratch_shapes=[
            pltpu.VMEM(columns.shape, BF16),
            pltpu.VMEM(shape if last else (8, 128), F32),
            pltpu.VMEM((nv, nown, blk, width) if last else (8, 128), F32),
            pltpu.SemaphoreType.DMA((columns.shape[0] // group,)),
            pltpu.SemaphoreType.DMA((nv,)),
        ],
        compiler_params=PARAMS,
        name="project",
    )(*args)


def swap(array, axis, bit):
    size = lax.axis_size(axis)
    return lax.ppermute(array, axis, [(i, i ^ bit) for i in range(size)])


def across(pieces, bits):
    for i, bit in enumerate(bits):
        got = [(swap(a, "grid", bit), [m ^ bit for m in masks]) for a, masks in pieces]
        if i + 1 < len(bits):
            pieces = [
                (jnp.concatenate([a, b], axis=0), masks + more)
                for (a, masks), (b, more) in zip(pieces, got, strict=True)
            ]
        else:
            pieces = pieces + got
    return pieces


def within(pieces, bits):
    for bit in bits:
        pieces = pieces + [(swap(a, "grid", bit), [m ^ bit for m in masks]) for a, masks in pieces]
    return pieces


def on_device(trial, occupied, colloc, blocks, coords, weights):
    n_ao, n_grid = lax.axis_size("ao"), lax.axis_size("grid")
    batches, npts, span = colloc.shape
    sig = blocks.shape[1]
    blk = span // sig
    nvec, nocc = trial.shape[1], trial.shape[3]
    nv = nvec // n_ao
    rank = n_grid // nv
    nlocal = trial.shape[0] // blk
    nown = nlocal * n_ao // n_grid
    parts = min(rank, nlocal & -nlocal)
    nb = nlocal // parts
    count = batches // 2
    ao, grid = lax.axis_index("ao"), lax.axis_index("grid")
    vector, side = grid // rank, grid % parts
    meta = jnp.stack([ao * nlocal, ao * 0, grid * nown, ao, side, vector]).astype(jnp.int32)
    high_bits = [rank << b for b in range(nv.bit_length() - 1)]
    low_bits = [1 << b for b in range(rank.bit_length() - 1)]
    part_bits = [1 << b for b in range(parts.bit_length() - 1)]

    panels = []
    far_first = list(reversed(range(n_ao)))
    for planes in (far_first[:1], far_first[1:]):
        where = jnp.stack([side * nb] + [(ao ^ over) * nv + vector for over in planes]).astype(jnp.int32)
        if panels:
            where, occupied = lax.optimization_barrier((where, occupied))
        rows = pack(trial, where, len(planes), nb, blk)
        for over, one in zip(planes, rows, strict=True):
            panels.append((swap(one, "ao", over) if over else one, (over, 0)))

    near = []
    for chunk in range(2):
        part = colloc[None, chunk * count : (chunk + 1) * count]
        near.append(across([(part, [0])], high_bits[::-1] if chunk else high_bits))
    far = [within(pieces, low_bits) for pieces in near]

    held, send = occupied_part(occupied, colloc, blocks, meta, blk)
    for s in range(n_ao.bit_length() - 1):
        got = swap(send, "ao", 1 << s)
        held = held + got.astype(F32)
        send = held.astype(BF16)
        whole = send[None]
    occ = across([(whole, [0])], high_bits)

    numbers = jnp.pad(blocks.astype(F32), ((0, 0), (0, npts - sig)))
    extra = jnp.concatenate([numbers[:, None], coords, weights[:, None]], axis=1)
    extra = within(across([(extra[None], [0])], high_bits), low_bits)
    fmasks = [m for _, masks in extra for m in masks]
    extra = jnp.concatenate([a for a, _ in extra], axis=0)
    ids = extra[:, :, 0, :sig].astype(jnp.int32)
    exact = extra[:nv, :, 1:]
    kern = kernel_matrix(exact[:, :, :3], exact[:, :, 3])
    group = 4 * sig
    xmasks = [m for pieces in far for _, m in pieces]
    facts = pair_list(xmasks, ids, fmasks, meta, rank, nown, 2, count, group)

    for bit in part_bits:
        panels = panels + [(swap(a, "grid", bit), (over, m ^ bit)) for a, (over, m) in panels]
    columns = gather(far, facts, blk, group, 2 * rank)
    parts = potential(panels, near, occ, kern, ids, fmasks, meta, nlocal, rank)
    early, late = [], []
    for chunk in range(2):
        pieces = across([(parts[chunk][None], [0])], high_bits[::-1] if chunk else high_bits)
        early += [(chunk, a, m) for a, m in within(pieces[:1], low_bits)]
        late += [(chunk, a, m) for a, m in within(pieces[1:], low_bits)]
    total = project(early, facts, columns, meta, None, rank, nown, group)
    total = project(late, facts, columns, meta, total, rank, nown, group)
    return total.reshape(nv, nown * blk, 2, nocc)


def solution(mesh):
    in_specs = (
        P("ao", None, None, None),
        P("ao", None, None),
        P("grid", None, None),
        P("grid", None),
        P("grid", None, None),
        P("grid", None),
    )
    out_specs = P("ao", "grid", None, None)

    return jax.shard_map(on_device, mesh=mesh, in_specs=in_specs, out_specs=out_specs, check_vma=False)
```

```python
import functools
import math

import jax
import jax.numpy as jnp
from jax import lax
from jax.experimental import pallas as pl
from jax.experimental.pallas import tpu as pltpu
from jax.sharding import PartitionSpec as P

F32 = jnp.float32
BF16 = jnp.bfloat16
MIB = 1024 * 1024


def params(*arrays):
    total = sum(math.prod(shape) * size for shape, size in arrays)
    return pltpu.CompilerParams(vmem_limit_bytes=min(60 * MIB, total + 6 * MIB))


SMEM = pl.BlockSpec(memory_space=pltpu.SMEM)
VMEM = pl.BlockSpec(memory_space=pltpu.VMEM)
ANY = pl.BlockSpec(memory_space=pl.ANY)
HBM = pl.BlockSpec(memory_space=pltpu.HBM)


def kernel_matrix(points, quad):
    differ = points[..., :, None, :] - points[..., :, :, None]
    square = jnp.sum(differ * differ, axis=-3)
    return quad[..., :, None] * quad[..., None, :] / jnp.sqrt(square + 0.25)


def selectors(blk):
    ao = lax.broadcasted_iota(jnp.int32, (blk, 2 * blk), 0)
    col = lax.broadcasted_iota(jnp.int32, (blk, 2 * blk), 1)
    return [(col == 2 * ao + c).astype(F32).astype(BF16) for c in range(2)]


def pack_kernel(where, trial, *refs):
    outs, (rows, sem) = refs[:-2], refs[-2:]
    nb, blk, width = outs[0].shape
    nocc = width // 2
    copies = []
    for i in range(len(outs)):
        for j in range(nb):
            at = (where[0] + j) * blk
            copies.append(
                pltpu.make_async_copy(trial.at[pl.ds(at, blk), where[1 + i]], rows.at[i, j], sem.at[i, j])
            )
    for c in copies:
        c.start()
    pick = jnp.concatenate(selectors(blk), axis=0)
    for i, out in enumerate(outs):
        for j in range(0, nb, 2):
            ahead = range(j, min(j + 2, nb))
            for k in ahead:
                copies[i * nb + k].wait()
            both = jnp.concatenate([rows[i, k].reshape(2 * blk, nocc) for k in ahead], axis=1)
            split = jnp.dot(pick, both, preferred_element_type=F32).astype(BF16)
            for k in ahead:
                for c in range(2):
                    piece = split[c * blk : (c + 1) * blk, (k - j) * nocc : (k - j + 1) * nocc]
                    out[k, :, c * nocc : (c + 1) * nocc] = piece


def pack(trial, where, planes, nb, blk):
    nocc = trial.shape[3]
    return pl.pallas_call(
        pack_kernel,
        out_shape=(jax.ShapeDtypeStruct((nb, blk, 2 * nocc), BF16),) * planes,
        in_specs=[SMEM, HBM],
        out_specs=(VMEM,) * planes,
        scratch_shapes=[pltpu.VMEM((planes, nb, blk, 2, nocc), BF16), pltpu.SemaphoreType.DMA((planes, nb))],
        compiler_params=params(((planes, nb, blk, 4 * nocc), 2), ((planes, nb, blk, 2 * nocc), 2)),
        name="pack",
    )(where, trial)


def occupied_kernel(ids, meta, occupied, values, keep, send, table):
    batches, sig = ids.shape
    blk, nocc = occupied.shape[0] // (table.shape[0] - 1), occupied.shape[2]
    nlocal = table.shape[0] - 1
    pick = selectors(blk)
    for j in range(nlocal):
        both = occupied[j * blk : (j + 1) * blk].reshape(2 * blk, nocc)
        for c in range(2):
            split = jnp.dot(pick[c], both, preferred_element_type=F32)
            table[j, :, c * nocc : (c + 1) * nocc] = split.astype(BF16)
    table[nlocal] = jnp.zeros(table.shape[1:], BF16)

    def block(b, s):
        local = ids[b, s] - meta[0]
        return table[jnp.where((local >= 0) & (local < nlocal), local, nlocal)]

    for b in range(batches):
        total = jnp.zeros(keep.shape[1:], F32)
        for s in range(0, sig, 2):
            two = jnp.concatenate([block(b, s), block(b, s + 1)], axis=0)
            total += jnp.dot(values[b, :, s * blk : (s + 2) * blk], two, preferred_element_type=F32)
        keep[b] = total
        send[b] = total.astype(BF16)


def occupied_part(occupied, colloc, blocks, meta, blk):
    batches, npts, _ = colloc.shape
    nocc = occupied.shape[2]
    shape = (batches, npts, 2 * nocc)
    return pl.pallas_call(
        occupied_kernel,
        out_shape=(jax.ShapeDtypeStruct(shape, F32), jax.ShapeDtypeStruct(shape, BF16)),
        in_specs=[SMEM, SMEM, VMEM, VMEM],
        out_specs=(VMEM, VMEM),
        scratch_shapes=[pltpu.VMEM((occupied.shape[0] // blk + 1, blk, 2 * nocc), BF16)],
        compiler_params=params((colloc.shape, 2), (occupied.shape, 4), (shape, 12), (shape, 12)),
        name="occupied",
    )(blocks, meta, occupied, colloc)


def potential_kernel(sizes, ids, meta, *refs):
    tmasks, xmasks, omasks, fmasks, nlocal, rank, first = sizes
    panels, refs = refs[: len(tmasks)], refs[len(tmasks) :]
    values, refs = refs[: len(xmasks)], refs[len(xmasks) :]
    occ, refs = refs[: len(omasks)], refs[len(omasks) :]
    kern, refs = refs[0], refs[1:]
    out, table, x, left, m, tsems, xsems = refs
    nb, blk, width = panels[0].shape
    count, npts = x.shape[1], x.shape[2]
    sig = ids.shape[2]
    copies = []
    for i, (over, side) in enumerate(tmasks):
        at = (meta[3] ^ over) * nlocal + (meta[4] ^ side) * nb
        copies.append(pltpu.make_async_copy(panels[i], table.at[pl.ds(at, nb)], tsems.at[i]))
    loads = []
    todo = []
    at = 0
    for i, piece in enumerate(values):
        loads.append(pltpu.make_async_copy(piece, x.at[pl.ds(at, piece.shape[0])], xsems.at[i]))
        for j, mask in enumerate(xmasks[i]):
            todo += [(i, at + j, mask, b) for b in range(count)]
        at += piece.shape[0]
    for c in copies + loads:
        c.start()
    where = {mask: (i, j) for i, masks in enumerate(omasks) for j, mask in enumerate(masks)}
    dims = (((1,), (1,)), ((), ()))

    def turn_of(mask, b):
        piece, row = where[mask]
        og = occ[piece][row, b]
        half = width // 2
        return jnp.concatenate([og, jnp.concatenate([-og[:, half:], og[:, :half]], axis=1)], axis=0)

    for c in copies:
        c.wait()
    seen = -1
    for i, (piece, row, mask, b) in enumerate(todo):
        if piece != seen:
            loads[piece].wait()
            seen = piece
        f = fmasks.index(mask)
        dens = jnp.zeros((npts, width), F32)
        for s in range(0, sig, 2):
            two = [table[ids[f, first + b, s + t]] for t in range(2)]
            dens += jnp.dot(
                x[row, b, :, s * blk : (s + 2) * blk], jnp.concatenate(two, axis=0), preferred_element_type=F32
            )
        left[i] = dens.astype(BF16)
    for i, (_, _, mask, b) in enumerate(todo):
        rho = lax.dot_general(left[i], turn_of(mask, first + b), dims, preferred_element_type=F32)
        weight = kern[fmasks.index(mask), first + b]
        m[i] = (rho * jnp.concatenate([weight, weight], axis=1)).astype(BF16)
    for i, (_, _, mask, b) in enumerate(todo):
        e = jnp.dot(m[i], turn_of(mask, first + b), preferred_element_type=F32)
        out[meta[5] ^ (mask // rank), b] = e.astype(BF16)


def potential(panels, values, occ, kern, ids, fmasks, meta, nlocal, rank, chunk):
    tmasks = tuple(m for _, m in panels)
    xmasks = tuple(tuple(m) for _, m in values)
    omasks = tuple(tuple(m) for _, m in occ)
    count, npts, span = values[0][0].shape[1:]
    nb, blk, width = panels[0][0].shape
    nsrc = sum(len(m) for m in xmasks)
    sizes = (tmasks, xmasks, omasks, tuple(fmasks), nlocal, rank, chunk * count)
    table = (len(panels) * nb, blk, width)
    x = (nsrc, count, npts, span)
    left = (nsrc * count, npts, width)
    m = (nsrc * count, npts, 2 * npts)
    return pl.pallas_call(
        functools.partial(potential_kernel, sizes),
        out_shape=jax.ShapeDtypeStruct((nsrc, count, npts, width), BF16),
        in_specs=[SMEM, SMEM] + [VMEM] * len(panels) + [ANY] * len(values) + [VMEM] * (len(occ) + 1),
        out_specs=VMEM,
        scratch_shapes=[
            pltpu.VMEM(table, BF16),
            pltpu.VMEM(x, BF16),
            pltpu.VMEM(left, BF16),
            pltpu.VMEM(m, BF16),
            pltpu.SemaphoreType.DMA((len(panels),)),
            pltpu.SemaphoreType.DMA((len(values),)),
        ],
        compiler_params=params((table, 4), (x, 2), (left, 8), (m, 2), (kern.shape, 4)),
        name="potential",
    )(ids, meta, *[a for a, _ in panels], *[a for a, _ in values], *[a for a, _ in occ], kern)


def list_kernel(sizes, ids, meta, facts, place):
    entries, nchunk, rank, nown = sizes
    sig = ids.shape[2]
    nlist = nchunk * rank
    sizes = []
    for t in range(nlist):
        n = jnp.int32(0)
        for f, b, mask, chunk, _, _ in entries:
            if chunk * rank + mask % rank == t:
                for s in range(sig):
                    own = ids[f, b, s] - meta[2]
                    n = n + ((own >= 0) & (own < nown)).astype(jnp.int32)
        sizes.append(n)
    n = jnp.int32(0)
    for t in range(nlist):
        facts[5, t] = n
        place[t] = n
        end = n + sizes[t]
        for k in range(3):
            for f, one in enumerate((0, 0, 0, -1, 0)):
                facts[f, end + k] = jnp.int32(one)
        n = lax.div(end + 3, 4) * 4
    facts[5, nlist] = n
    for f, b, mask, chunk, row, inner in entries:
        for s in range(sig):
            own = ids[f, b, s] - meta[2]

            @pl.when((own >= 0) & (own < nown))
            def _(mask=mask, t=chunk * rank + mask % rank, row=row, inner=inner, s=s, own=own):
                to = place[t]
                place[t] = to + 1
                what = (own, meta[5] ^ (mask // rank), jnp.int32(inner), jnp.int32(row), jnp.int32(s))
                for f, one in enumerate(what):
                    facts[f, to] = one


def entries_of(xmasks, fmasks, nchunk, count):
    out = []
    at = 0
    groups = len(xmasks) // nchunk
    for i, masks in enumerate(xmasks):
        chunk = i // groups
        for j, mask in enumerate(masks):
            out += [(fmasks.index(mask), chunk * count + b, mask, chunk, at + j, b) for b in range(count)]
        at += len(masks)
    return tuple(out)


def pair_list(xmasks, ids, fmasks, meta, rank, nown, nchunk, count, group):
    nsrc, _, sig = ids.shape
    most = -(-(nchunk * (nsrc * count * sig + 3 * rank) + 4) // group) * group
    sizes = (entries_of(xmasks, fmasks, nchunk, count), nchunk, rank, nown)
    return pl.pallas_call(
        functools.partial(list_kernel, sizes),
        out_shape=jax.ShapeDtypeStruct((8, most), jnp.int32),
        in_specs=[SMEM, SMEM],
        out_specs=SMEM,
        scratch_shapes=[pltpu.SMEM((nchunk * rank,), jnp.int32)],
        compiler_params=params(),
        name="pairs",
    )(ids, meta)


def gather_kernel(group, nlist, facts, *refs):
    values, (columns, x, rows, xsems, osems) = refs[:-5], refs[-5:]
    blk = rows.shape[1]
    copies = []
    at = 0
    for i, piece in enumerate(values):
        copies.append(pltpu.make_async_copy(piece, x.at[pl.ds(at, piece.shape[0])], xsems.at[i]))
        at += piece.shape[0]
    for c in copies:
        c.start()
    for c in copies:
        c.wait()
    n = facts[5, nlist]

    def one(i, carry):
        for t in range(4):
            row = facts[3, 4 * i + t]
            start = pl.multiple_of(facts[4, 4 * i + t] * blk, blk)
            column = x[jnp.maximum(row, 0), facts[2, 4 * i + t], :, pl.ds(start, blk)]
            rows[4 * i + t] = jnp.where(row >= 0, column, jnp.zeros_like(column)).T
        return carry

    lax.fori_loop(0, lax.div(n, 4), one, 0)
    outs = [
        pltpu.make_async_copy(rows.at[pl.ds(i * group, group)], columns.at[pl.ds(i * group, group)], osems.at[i])
        for i in range(columns.shape[0] // group)
    ]
    for act in ("start", "wait"):
        for i, c in enumerate(outs):

            @pl.when(i * group < n)
            def _(c=c, act=act):
                getattr(c, act)()


def gather(values, facts, blk, group, nlist):
    flat = [a for pieces in values for a, _ in pieces]
    count, npts, span = flat[0].shape[1:]
    most = facts.shape[1]
    return pl.pallas_call(
        functools.partial(gather_kernel, group, nlist),
        out_shape=jax.ShapeDtypeStruct((most, blk, npts), BF16),
        in_specs=[SMEM] + [ANY] * len(flat),
        out_specs=ANY,
        scratch_shapes=[
            pltpu.VMEM((sum(a.shape[0] for a in flat), count, npts, span), BF16),
            pltpu.VMEM((most, blk, npts), BF16),
            pltpu.SemaphoreType.DMA((len(flat),)),
            pltpu.SemaphoreType.DMA((most // group,)),
        ],
        compiler_params=params(((most, blk, npts), 2), ((sum(a.shape[0] for a in flat), count, npts, span), 2)),
        name="gather",
    )(facts, *flat)


def project_kernel(sizes, facts, meta, columns, *refs):
    nchunk, emasks, rank, group, nown, again = sizes
    ne = len(emasks)
    potentials, refs = refs[:ne], refs[ne + again :]
    out, x, staged, total, xsems, osems = refs
    blk = x.shape[1]
    offsets = sorted({mask // rank for _, masks in emasks for mask in masks})
    n = facts[5, nchunk * rank]
    xcopies = [
        pltpu.make_async_copy(columns.at[pl.ds(i * group, group)], x.at[pl.ds(i * group, group)], xsems.at[i])
        for i in range(columns.shape[0] // group)
    ]
    for i, c in enumerate(xcopies):

        @pl.when(i * group < n)
        def _(c=c):
            c.start()

    total[...] = jnp.zeros_like(total)
    for i, c in enumerate(xcopies):

        @pl.when(i * group < n)
        def _(c=c):
            c.wait()

    for t in range(nchunk * rank):
        mine = [
            (i, j, offsets.index(mask // rank))
            for i, (chunk, masks) in enumerate(emasks)
            for j, mask in enumerate(masks)
            if chunk * rank + mask % rank == t
        ]

        def one(p, carry, mine=mine):
            for at in range(4):
                own, source, b = [facts[f, 4 * p + at] for f in range(3)]
                for i, j, k in mine:
                    total[k, own] += jnp.dot(x[4 * p + at], potentials[i][j, source, b], preferred_element_type=F32)
            return carry

        lax.fori_loop(lax.div(facts[5, t], 4), lax.div(facts[5, t + 1], 4), one, 0)
    nocc = out.shape[2]
    copies = [
        pltpu.make_async_copy(staged.at[k], out.at[meta[5] ^ off], osems.at[k]) for k, off in enumerate(offsets)
    ]
    for k in range(len(offsets)):
        for o in range(nown):
            for c in range(2):
                staged[k, pl.ds(o * 2 * blk + c, blk, stride=2), :] = total[k, o, :, c * nocc : (c + 1) * nocc]
        copies[k].start()
    for c in copies:
        c.wait()


def project(potentials, facts, columns, meta, before, rank, nown, group):
    emasks = tuple((chunk, tuple(m)) for chunk, _, m in potentials)
    nchunk = 1 + max(chunk for chunk, _, _ in potentials)
    nv, _, _, width = potentials[0][1].shape[1:]
    blk = columns.shape[1]
    ne = len(potentials)
    again = before is not None
    nk = len({mask // rank for _, masks in emasks for mask in masks})
    args = [facts, meta, columns, *[a for _, a, _ in potentials]] + ([before] if again else [])
    staged = (nk, nown * blk * 2, width // 2)
    total = (nk, nown, blk, width)
    arrays = [(a.shape, 2) for _, a, _ in potentials]
    return pl.pallas_call(
        functools.partial(project_kernel, (nchunk, emasks, rank, group, nown, int(again))),
        out_shape=jax.ShapeDtypeStruct((nv, nown * blk * 2, width // 2), F32),
        in_specs=[SMEM] * 2 + [ANY] + [VMEM] * ne + [ANY] * int(again),
        out_specs=ANY,
        input_output_aliases={3 + ne: 0} if again else {},
        scratch_shapes=[
            pltpu.VMEM(columns.shape, BF16),
            pltpu.VMEM(staged, F32),
            pltpu.VMEM(total, F32),
            pltpu.SemaphoreType.DMA((columns.shape[0] // group,)),
            pltpu.SemaphoreType.DMA((nk,)),
        ],
        compiler_params=params((columns.shape, 2), (staged, 4), (total, 4), *arrays),
        name="project",
    )(*args)


def swap(array, axis, bit):
    size = lax.axis_size(axis)
    return lax.ppermute(array, axis, [(i, i ^ bit) for i in range(size)])


def across(part, bits):
    pieces = [(part, [0])]
    for bit in bits:
        for a, masks in pieces[:]:
            pieces.append((swap(a, "grid", bit), [m ^ bit for m in masks]))
    return pieces


def within(pieces, bits):
    for bit in bits:
        pieces = pieces + [(swap(a, "grid", bit), [m ^ bit for m in masks]) for a, masks in pieces]
    return pieces


def on_device(trial, occupied, colloc, blocks, coords, weights):
    n_ao, n_grid = lax.axis_size("ao"), lax.axis_size("grid")
    batches, npts, span = colloc.shape
    sig = blocks.shape[1]
    blk = span // sig
    nvec, nocc = trial.shape[1], trial.shape[3]
    nv = nvec // n_ao
    rank = n_grid // nv
    nlocal = trial.shape[0] // blk
    nown = nlocal * n_ao // n_grid
    parts = min(rank, nlocal & -nlocal)
    nb = nlocal // parts
    count = batches // 2
    ao, grid = lax.axis_index("ao"), lax.axis_index("grid")
    vector, side = grid // rank, grid % parts
    meta = jnp.stack([ao * nlocal, ao * 0, grid * nown, ao, side, vector]).astype(jnp.int32)
    high_bits = [rank << b for b in range(nv.bit_length() - 1)]
    low_bits = [1 << b for b in range(rank.bit_length() - 1)]
    part_bits = [1 << b for b in range(parts.bit_length() - 1)]

    panels = []
    far_first = list(reversed(range(n_ao)))
    for planes in (far_first[:1], far_first[1:]):
        where = jnp.stack([side * nb] + [(ao ^ over) * nv + vector for over in planes]).astype(jnp.int32)
        rows = pack(trial, where, len(planes), nb, blk)
        if not panels:
            rows, coords, weights = lax.optimization_barrier((rows, coords, weights))
        for over, one in zip(planes, rows, strict=True):
            panels.append((swap(one, "ao", over) if over else one, (over, 0)))

    near = []
    for chunk in range(2):
        part = colloc[None, chunk * count : (chunk + 1) * count]
        near.append(across(part, high_bits[::-1] if chunk else high_bits))
    far = [within(pieces, low_bits) for pieces in near]

    held, send = occupied_part(occupied, colloc, blocks, meta, blk)
    for s in range(n_ao.bit_length() - 1):
        got = swap(send, "ao", 1 << s)
        held = held + got.astype(F32)
        send = held.astype(BF16)
        whole = send[None]
    occ = across(whole, high_bits)

    numbers = jnp.pad(blocks.astype(F32), ((0, 0), (0, npts - sig)))
    extra = jnp.concatenate([numbers[:, None], coords, weights[:, None]], axis=1)
    extra = within(across(extra[None], high_bits), low_bits)
    fmasks = [m for _, masks in extra for m in masks]
    extra = jnp.concatenate([a for a, _ in extra], axis=0)
    ids = extra[:, :, 0, :sig].astype(jnp.int32)
    exact = extra[:nv, :, 1:]
    kern = kernel_matrix(exact[:, :, :3], exact[:, :, 3])
    group = 4 * sig
    xmasks = [m for pieces in far for _, m in pieces]
    facts = pair_list(xmasks, ids, fmasks, meta, rank, nown, 2, count, group)

    for bit in part_bits:
        panels = panels + [(swap(a, "grid", bit), (over, m ^ bit)) for a, (over, m) in panels]
    columns = gather(far, facts, blk, group, 2 * rank)
    early, late = [], []
    for chunk in range(2):
        e = potential(panels, near[chunk], occ, kern, ids, fmasks, meta, nlocal, rank, chunk)
        pieces = across(e[None], high_bits[::-1] if chunk else high_bits)
        early += [(chunk, a, m) for a, m in within(pieces[:-1], low_bits)]
        late += [(chunk, a, m) for a, m in within(pieces[-1:], low_bits)]
    total = project(early, facts, columns, meta, None, rank, nown, group)
    total = project(late, facts, columns, meta, total, rank, nown, group)
    return total.reshape(nv, nown * blk, 2, nocc)


def solution(mesh):
    in_specs = (
        P("ao", None, None, None),
        P("ao", None, None),
        P("grid", None, None),
        P("grid", None),
        P("grid", None, None),
        P("grid", None),
    )
    out_specs = P("ao", "grid", None, None)

    return jax.shard_map(on_device, mesh=mesh, in_specs=in_specs, out_specs=out_specs, check_vma=False)
```

```python
import functools
import math

import jax
import jax.numpy as jnp
from jax import lax
from jax.experimental import pallas as pl
from jax.experimental.pallas import tpu as pltpu
from jax.sharding import PartitionSpec as P

F32 = jnp.float32
BF16 = jnp.bfloat16
MIB = 1024 * 1024


def params(*arrays):
    total = sum(math.prod(shape) * size for shape, size in arrays)
    return pltpu.CompilerParams(vmem_limit_bytes=min(60 * MIB, total + 6 * MIB))


SMEM = pl.BlockSpec(memory_space=pltpu.SMEM)
VMEM = pl.BlockSpec(memory_space=pltpu.VMEM)
ANY = pl.BlockSpec(memory_space=pl.ANY)


def kernel_matrix(points, quad):
    differ = points[..., :, None, :] - points[..., :, :, None]
    square = jnp.sum(differ * differ, axis=-3)
    return quad[..., :, None] * quad[..., None, :] / jnp.sqrt(square + 0.25)


def selectors(blk):
    ao = lax.broadcasted_iota(jnp.int32, (blk, 2 * blk), 0)
    col = lax.broadcasted_iota(jnp.int32, (blk, 2 * blk), 1)
    return [(col == 2 * ao + c).astype(F32).astype(BF16) for c in range(2)]


def pack_kernel(where, trial, *refs):
    outs, (rows, sem) = refs[:-2], refs[-2:]
    nb, blk, width = outs[0].shape
    nocc = width // 2
    copies = []
    for i in range(len(outs)):
        for j in range(nb):
            at = (where[0] + j) * blk
            copies.append(
                pltpu.make_async_copy(trial.at[pl.ds(at, blk), where[1 + i]], rows.at[i, j], sem.at[i, j])
            )
    for c in copies:
        c.start()
    pick = jnp.concatenate(selectors(blk), axis=0)
    for i, out in enumerate(outs):
        for j in range(0, nb, 2):
            ahead = range(j, min(j + 2, nb))
            for k in ahead:
                copies[i * nb + k].wait()
            both = jnp.concatenate([rows[i, k].reshape(2 * blk, nocc) for k in ahead], axis=1)
            split = jnp.dot(pick, both, preferred_element_type=F32).astype(BF16)
            for k in ahead:
                for c in range(2):
                    piece = split[c * blk : (c + 1) * blk, (k - j) * nocc : (k - j + 1) * nocc]
                    out[k, :, c * nocc : (c + 1) * nocc] = piece


def pack(trial, where, planes, nb, blk):
    nocc = trial.shape[3]
    return pl.pallas_call(
        pack_kernel,
        out_shape=(jax.ShapeDtypeStruct((nb, blk, 2 * nocc), BF16),) * planes,
        in_specs=[SMEM, ANY],
        out_specs=(VMEM,) * planes,
        scratch_shapes=[pltpu.VMEM((planes, nb, blk, 2, nocc), BF16), pltpu.SemaphoreType.DMA((planes, nb))],
        compiler_params=pltpu.CompilerParams(vmem_limit_bytes=52 * MIB),
        name="pack",
    )(where, trial)


def occupied_kernel(ids, meta, occupied, values, keep, send, table):
    batches, sig = ids.shape
    blk, nocc = occupied.shape[0] // (table.shape[0] - 1), occupied.shape[2]
    nlocal = table.shape[0] - 1
    pick = selectors(blk)
    for j in range(nlocal):
        both = occupied[j * blk : (j + 1) * blk].reshape(2 * blk, nocc)
        for c in range(2):
            split = jnp.dot(pick[c], both, preferred_element_type=F32)
            table[j, :, c * nocc : (c + 1) * nocc] = split.astype(BF16)
    table[nlocal] = jnp.zeros(table.shape[1:], BF16)

    def block(b, s):
        local = ids[b, s] - meta[0]
        return table[jnp.where((local >= 0) & (local < nlocal), local, nlocal)]

    for b in range(batches):
        total = jnp.zeros(keep.shape[1:], F32)
        for s in range(0, sig, 2):
            two = jnp.concatenate([block(b, s), block(b, s + 1)], axis=0)
            total += jnp.dot(values[b, :, s * blk : (s + 2) * blk], two, preferred_element_type=F32)
        keep[b] = total
        send[b] = total.astype(BF16)


def occupied_part(occupied, colloc, blocks, meta, blk):
    batches, npts, _ = colloc.shape
    nocc = occupied.shape[2]
    shape = (batches, npts, 2 * nocc)
    return pl.pallas_call(
        occupied_kernel,
        out_shape=(jax.ShapeDtypeStruct(shape, F32), jax.ShapeDtypeStruct(shape, BF16)),
        in_specs=[SMEM, SMEM, VMEM, VMEM],
        out_specs=(VMEM, VMEM),
        scratch_shapes=[pltpu.VMEM((occupied.shape[0] // blk + 1, blk, 2 * nocc), BF16)],
        compiler_params=params((colloc.shape, 2), (occupied.shape, 4), (shape, 12), (shape, 12)),
        name="occupied",
    )(blocks, meta, occupied, colloc)


def potential_kernel(sizes, ids, meta, *refs):
    tmasks, xmasks, omasks, fmasks, nlocal, rank, first = sizes
    panels, refs = refs[: len(tmasks)], refs[len(tmasks) :]
    values, refs = refs[: len(xmasks)], refs[len(xmasks) :]
    occ, refs = refs[: len(omasks)], refs[len(omasks) :]
    kern, refs = refs[0], refs[1:]
    out, table, x, left, m, tsems, xsems = refs
    nb, blk, width = panels[0].shape
    count, npts = x.shape[1], x.shape[2]
    sig = ids.shape[2]
    copies = []
    for i, (over, side) in enumerate(tmasks):
        at = (meta[3] ^ over) * nlocal + (meta[4] ^ side) * nb
        copies.append(pltpu.make_async_copy(panels[i], table.at[pl.ds(at, nb)], tsems.at[i]))
    loads = []
    todo = []
    at = 0
    for i, piece in enumerate(values):
        loads.append(pltpu.make_async_copy(piece, x.at[pl.ds(at, piece.shape[0])], xsems.at[i]))
        for j, mask in enumerate(xmasks[i]):
            todo += [(i, at + j, mask, b) for b in range(count)]
        at += piece.shape[0]
    for c in copies + loads:
        c.start()
    where = {mask: (i, j) for i, masks in enumerate(omasks) for j, mask in enumerate(masks)}
    dims = (((1,), (1,)), ((), ()))

    def turn_of(mask, b):
        piece, row = where[mask]
        og = occ[piece][row, b]
        half = width // 2
        return jnp.concatenate([og, jnp.concatenate([-og[:, half:], og[:, :half]], axis=1)], axis=0)

    for c in copies:
        c.wait()
    seen = -1
    for i, (piece, row, mask, b) in enumerate(todo):
        if piece != seen:
            loads[piece].wait()
            seen = piece
        f = fmasks.index(mask)
        dens = jnp.zeros((npts, width), F32)
        for s in range(0, sig, 2):
            two = [table[ids[f, first + b, s + t]] for t in range(2)]
            dens += jnp.dot(
                x[row, b, :, s * blk : (s + 2) * blk], jnp.concatenate(two, axis=0), preferred_element_type=F32
            )
        left[i] = dens.astype(BF16)
    for i, (_, _, mask, b) in enumerate(todo):
        rho = lax.dot_general(left[i], turn_of(mask, first + b), dims, preferred_element_type=F32)
        weight = kern[fmasks.index(mask), first + b]
        m[i] = (rho * jnp.concatenate([weight, weight], axis=1)).astype(BF16)
    for i, (_, _, mask, b) in enumerate(todo):
        e = jnp.dot(m[i], turn_of(mask, first + b), preferred_element_type=F32)
        out[meta[5] ^ (mask // rank), b] = e.astype(BF16)


def potential(panels, values, occ, kern, ids, fmasks, meta, nlocal, rank, chunk):
    tmasks = tuple(m for _, m in panels)
    xmasks = tuple(tuple(m) for _, m in values)
    omasks = tuple(tuple(m) for _, m in occ)
    count, npts, span = values[0][0].shape[1:]
    nb, blk, width = panels[0][0].shape
    nsrc = sum(len(m) for m in xmasks)
    sizes = (tmasks, xmasks, omasks, tuple(fmasks), nlocal, rank, chunk * count)
    table = (len(panels) * nb, blk, width)
    x = (nsrc, count, npts, span)
    left = (nsrc * count, npts, width)
    m = (nsrc * count, npts, 2 * npts)
    return pl.pallas_call(
        functools.partial(potential_kernel, sizes),
        out_shape=jax.ShapeDtypeStruct((nsrc, count, npts, width), BF16),
        in_specs=[SMEM, SMEM] + [VMEM] * len(panels) + [ANY] * len(values) + [VMEM] * (len(occ) + 1),
        out_specs=VMEM,
        scratch_shapes=[
            pltpu.VMEM(table, BF16),
            pltpu.VMEM(x, BF16),
            pltpu.VMEM(left, BF16),
            pltpu.VMEM(m, BF16),
            pltpu.SemaphoreType.DMA((len(panels),)),
            pltpu.SemaphoreType.DMA((len(values),)),
        ],
        compiler_params=params((table, 4), (x, 2), (left, 8), (m, 2), (kern.shape, 4)),
        name="potential",
    )(ids, meta, *[a for a, _ in panels], *[a for a, _ in values], *[a for a, _ in occ], kern)


def list_kernel(sizes, ids, meta, facts, place):
    entries, nchunk, rank, nown = sizes
    sig = ids.shape[2]
    nlist = nchunk * rank
    sizes = []
    for t in range(nlist):
        n = jnp.int32(0)
        for f, b, mask, chunk, _, _ in entries:
            if chunk * rank + mask % rank == t:
                for s in range(sig):
                    own = ids[f, b, s] - meta[2]
                    n = n + ((own >= 0) & (own < nown)).astype(jnp.int32)
        sizes.append(n)
    n = jnp.int32(0)
    for t in range(nlist):
        facts[5, t] = n
        place[t] = n
        end = n + sizes[t]
        for k in range(3):
            for f, one in enumerate((0, 0, 0, -1, 0)):
                facts[f, end + k] = jnp.int32(one)
        n = lax.div(end + 3, 4) * 4
    facts[5, nlist] = n
    for f, b, mask, chunk, row, inner in entries:
        for s in range(sig):
            own = ids[f, b, s] - meta[2]

            @pl.when((own >= 0) & (own < nown))
            def _(mask=mask, t=chunk * rank + mask % rank, row=row, inner=inner, s=s, own=own):
                to = place[t]
                place[t] = to + 1
                what = (own, meta[5] ^ (mask // rank), jnp.int32(inner), jnp.int32(row), jnp.int32(s))
                for f, one in enumerate(what):
                    facts[f, to] = one


def entries_of(xmasks, fmasks, nchunk, count):
    out = []
    at = 0
    groups = len(xmasks) // nchunk
    for i, masks in enumerate(xmasks):
        chunk = i // groups
        for j, mask in enumerate(masks):
            out += [(fmasks.index(mask), chunk * count + b, mask, chunk, at + j, b) for b in range(count)]
        at += len(masks)
    return tuple(out)


def pair_list(xmasks, ids, fmasks, meta, rank, nown, nchunk, count, group):
    nsrc, _, sig = ids.shape
    most = -(-(nchunk * (nsrc * count * sig + 3 * rank) + 4) // group) * group
    sizes = (entries_of(xmasks, fmasks, nchunk, count), nchunk, rank, nown)
    return pl.pallas_call(
        functools.partial(list_kernel, sizes),
        out_shape=jax.ShapeDtypeStruct((8, most), jnp.int32),
        in_specs=[SMEM, SMEM],
        out_specs=SMEM,
        scratch_shapes=[pltpu.SMEM((nchunk * rank,), jnp.int32)],
        compiler_params=params(),
        name="pairs",
    )(ids, meta)


def gather_kernel(group, nlist, facts, *refs):
    values, (columns, x, rows, xsems, osems) = refs[:-5], refs[-5:]
    blk = rows.shape[1]
    copies = []
    at = 0
    for i, piece in enumerate(values):
        copies.append(pltpu.make_async_copy(piece, x.at[pl.ds(at, piece.shape[0])], xsems.at[i]))
        at += piece.shape[0]
    for c in copies:
        c.start()
    for c in copies:
        c.wait()
    n = facts[5, nlist]

    def one(i, carry):
        for t in range(4):
            row = facts[3, 4 * i + t]
            start = pl.multiple_of(facts[4, 4 * i + t] * blk, blk)
            column = x[jnp.maximum(row, 0), facts[2, 4 * i + t], :, pl.ds(start, blk)]
            rows[4 * i + t] = jnp.where(row >= 0, column, jnp.zeros_like(column)).T
        return carry

    lax.fori_loop(0, lax.div(n, 4), one, 0)
    outs = [
        pltpu.make_async_copy(rows.at[pl.ds(i * group, group)], columns.at[pl.ds(i * group, group)], osems.at[i])
        for i in range(columns.shape[0] // group)
    ]
    for act in ("start", "wait"):
        for i, c in enumerate(outs):

            @pl.when(i * group < n)
            def _(c=c, act=act):
                getattr(c, act)()


def gather(values, facts, blk, group, nlist):
    flat = [a for pieces in values for a, _ in pieces]
    count, npts, span = flat[0].shape[1:]
    most = facts.shape[1]
    return pl.pallas_call(
        functools.partial(gather_kernel, group, nlist),
        out_shape=jax.ShapeDtypeStruct((most, blk, npts), BF16),
        in_specs=[SMEM] + [ANY] * len(flat),
        out_specs=ANY,
        scratch_shapes=[
            pltpu.VMEM((sum(a.shape[0] for a in flat), count, npts, span), BF16),
            pltpu.VMEM((most, blk, npts), BF16),
            pltpu.SemaphoreType.DMA((len(flat),)),
            pltpu.SemaphoreType.DMA((most // group,)),
        ],
        compiler_params=params(((most, blk, npts), 2), ((sum(a.shape[0] for a in flat), count, npts, span), 2)),
        name="gather",
    )(facts, *flat)


def project_kernel(sizes, facts, meta, columns, *refs):
    nchunk, emasks, rank, group, nown, again = sizes
    ne = len(emasks)
    potentials, refs = refs[:ne], refs[ne + again :]
    out, x, staged, total, xsems, osems = refs
    blk = x.shape[1]
    offsets = sorted({mask // rank for _, masks in emasks for mask in masks})
    n = facts[5, nchunk * rank]
    xcopies = [
        pltpu.make_async_copy(columns.at[pl.ds(i * group, group)], x.at[pl.ds(i * group, group)], xsems.at[i])
        for i in range(columns.shape[0] // group)
    ]
    for i, c in enumerate(xcopies):

        @pl.when(i * group < n)
        def _(c=c):
            c.start()

    total[...] = jnp.zeros_like(total)
    for i, c in enumerate(xcopies):

        @pl.when(i * group < n)
        def _(c=c):
            c.wait()

    for t in range(nchunk * rank):
        mine = [
            (i, j, offsets.index(mask // rank))
            for i, (chunk, masks) in enumerate(emasks)
            for j, mask in enumerate(masks)
            if chunk * rank + mask % rank == t
        ]

        def one(p, carry, mine=mine):
            for at in range(4):
                own, source, b = [facts[f, 4 * p + at] for f in range(3)]
                for i, j, k in mine:
                    total[k, own] += jnp.dot(x[4 * p + at], potentials[i][j, source, b], preferred_element_type=F32)
            return carry

        lax.fori_loop(lax.div(facts[5, t], 4), lax.div(facts[5, t + 1], 4), one, 0)
    nocc = out.shape[2]
    copies = [
        pltpu.make_async_copy(staged.at[k], out.at[meta[5] ^ off], osems.at[k]) for k, off in enumerate(offsets)
    ]
    for k in range(len(offsets)):
        for o in range(nown):
            for c in range(2):
                staged[k, pl.ds(o * 2 * blk + c, blk, stride=2), :] = total[k, o, :, c * nocc : (c + 1) * nocc]
        copies[k].start()
    for c in copies:
        c.wait()


def project(potentials, facts, columns, meta, before, rank, nown, group):
    emasks = tuple((chunk, tuple(m)) for chunk, _, m in potentials)
    nchunk = 1 + max(chunk for chunk, _, _ in potentials)
    nv, _, _, width = potentials[0][1].shape[1:]
    blk = columns.shape[1]
    ne = len(potentials)
    again = before is not None
    nk = len({mask // rank for _, masks in emasks for mask in masks})
    args = [facts, meta, columns, *[a for _, a, _ in potentials]] + ([before] if again else [])
    staged = (nk, nown * blk * 2, width // 2)
    total = (nk, nown, blk, width)
    arrays = [(a.shape, 2) for _, a, _ in potentials]
    return pl.pallas_call(
        functools.partial(project_kernel, (nchunk, emasks, rank, group, nown, int(again))),
        out_shape=jax.ShapeDtypeStruct((nv, nown * blk * 2, width // 2), F32),
        in_specs=[SMEM] * 2 + [ANY] + [VMEM] * ne + [ANY] * int(again),
        out_specs=ANY,
        input_output_aliases={3 + ne: 0} if again else {},
        scratch_shapes=[
            pltpu.VMEM(columns.shape, BF16),
            pltpu.VMEM(staged, F32),
            pltpu.VMEM(total, F32),
            pltpu.SemaphoreType.DMA((columns.shape[0] // group,)),
            pltpu.SemaphoreType.DMA((nk,)),
        ],
        compiler_params=params((columns.shape, 2), (staged, 4), (total, 4), *arrays),
        name="project",
    )(*args)


def swap(array, axis, bit):
    size = lax.axis_size(axis)
    return lax.ppermute(array, axis, [(i, i ^ bit) for i in range(size)])


def across(part, bits):
    pieces = [(part, [0])]
    for bit in bits:
        for a, masks in pieces[:]:
            pieces.append((swap(a, "grid", bit), [m ^ bit for m in masks]))
    return pieces


def within(pieces, bits):
    for bit in bits:
        pieces = pieces + [(swap(a, "grid", bit), [m ^ bit for m in masks]) for a, masks in pieces]
    return pieces


def on_device(trial, occupied, colloc, blocks, coords, weights):
    n_ao, n_grid = lax.axis_size("ao"), lax.axis_size("grid")
    batches, npts, span = colloc.shape
    sig = blocks.shape[1]
    blk = span // sig
    nvec, nocc = trial.shape[1], trial.shape[3]
    nv = nvec // n_ao
    rank = n_grid // nv
    nlocal = trial.shape[0] // blk
    nown = nlocal * n_ao // n_grid
    parts = min(rank, nlocal & -nlocal)
    nb = nlocal // parts
    count = batches // 2
    ao, grid = lax.axis_index("ao"), lax.axis_index("grid")
    vector, side = grid // rank, grid % parts
    meta = jnp.stack([ao * nlocal, ao * 0, grid * nown, ao, side, vector]).astype(jnp.int32)
    high_bits = [rank << b for b in range(nv.bit_length() - 1)]
    low_bits = [1 << b for b in range(rank.bit_length() - 1)]
    part_bits = [1 << b for b in range(parts.bit_length() - 1)]

    panels = []
    far_first = list(reversed(range(n_ao)))
    for planes in (far_first[:1], far_first[1:]):
        where = jnp.stack([side * nb] + [(ao ^ over) * nv + vector for over in planes]).astype(jnp.int32)
        rows = pack(trial, where, len(planes), nb, blk)
        if not panels:
            rows, coords, weights = lax.optimization_barrier((rows, coords, weights))
        for over, one in zip(planes, rows, strict=True):
            panels.append((swap(one, "ao", over) if over else one, (over, 0)))

    near = []
    for chunk in range(2):
        part = colloc[None, chunk * count : (chunk + 1) * count]
        near.append(across(part, high_bits[::-1] if chunk else high_bits))
    far = [within(pieces, low_bits) for pieces in near]

    held, send = occupied_part(occupied, colloc, blocks, meta, blk)
    for s in range(n_ao.bit_length() - 1):
        got = swap(send, "ao", 1 << s)
        held = held + got.astype(F32)
        send = held.astype(BF16)
        whole = send[None]
    occ = across(whole, high_bits)

    numbers = jnp.pad(blocks.astype(F32), ((0, 0), (0, npts - sig)))
    extra = jnp.concatenate([numbers[:, None], coords, weights[:, None]], axis=1)
    extra = within(across(extra[None], high_bits), low_bits)
    fmasks = [m for _, masks in extra for m in masks]
    extra = jnp.concatenate([a for a, _ in extra], axis=0)
    ids = extra[:, :, 0, :sig].astype(jnp.int32)
    exact = extra[:nv, :, 1:]
    kern = kernel_matrix(exact[:, :, :3], exact[:, :, 3])
    group = 4 * sig
    xmasks = [m for pieces in far for _, m in pieces]
    facts = pair_list(xmasks, ids, fmasks, meta, rank, nown, 2, count, group)

    for bit in part_bits:
        panels = panels + [(swap(a, "grid", bit), (over, m ^ bit)) for a, (over, m) in panels]
    columns = gather(far, facts, blk, group, 2 * rank)
    early, late = [], []
    for chunk in range(2):
        e = potential(panels, near[chunk], occ, kern, ids, fmasks, meta, nlocal, rank, chunk)
        pieces = across(e[None], high_bits[::-1] if chunk else high_bits)
        early += [(chunk, a, m) for a, m in within(pieces[:-1], low_bits)]
        late += [(chunk, a, m) for a, m in within(pieces[-1:], low_bits)]
    total = project(early, facts, columns, meta, None, rank, nown, group)
    total = project(late, facts, columns, meta, total, rank, nown, group)
    return total.reshape(nv, nown * blk, 2, nocc)


def solution(mesh):
    in_specs = (
        P("ao", None, None, None),
        P("ao", None, None),
        P("grid", None, None),
        P("grid", None),
        P("grid", None, None),
        P("grid", None),
    )
    out_specs = P("ao", "grid", None, None)

    return jax.shard_map(on_device, mesh=mesh, in_specs=in_specs, out_specs=out_specs, check_vma=False)
```

```python
import functools
import math

import jax
import jax.numpy as jnp
from jax import lax
from jax.experimental import pallas as pl
from jax.experimental.pallas import tpu as pltpu
from jax.sharding import PartitionSpec as P

F32 = jnp.float32
BF16 = jnp.bfloat16
MIB = 1024 * 1024


def params(*arrays):
    total = sum(math.prod(shape) * size for shape, size in arrays)
    return pltpu.CompilerParams(vmem_limit_bytes=min(60 * MIB, total + 6 * MIB))


SMEM = pl.BlockSpec(memory_space=pltpu.SMEM)
VMEM = pl.BlockSpec(memory_space=pltpu.VMEM)
ANY = pl.BlockSpec(memory_space=pl.ANY)


def kernel_matrix(points, quad):
    differ = points[..., :, None, :] - points[..., :, :, None]
    square = jnp.sum(differ * differ, axis=-3)
    return quad[..., :, None] * quad[..., None, :] / jnp.sqrt(square + 0.25)


def selectors(blk):
    ao = lax.broadcasted_iota(jnp.int32, (blk, 2 * blk), 0)
    col = lax.broadcasted_iota(jnp.int32, (blk, 2 * blk), 1)
    return [(col == 2 * ao + c).astype(F32).astype(BF16) for c in range(2)]


def pack_kernel(where, trial, *refs):
    outs, (rows, sem) = refs[:-2], refs[-2:]
    nb, blk, width = outs[0].shape
    nocc = width // 2
    copies = []
    for i in range(len(outs)):
        for j in range(nb):
            at = (where[0] + j) * blk
            copies.append(
                pltpu.make_async_copy(trial.at[pl.ds(at, blk), where[1 + i]], rows.at[i, j], sem.at[i, j])
            )
    for c in copies:
        c.start()
    pick = jnp.concatenate(selectors(blk), axis=0)
    for i, out in enumerate(outs):
        for j in range(0, nb, 2):
            ahead = range(j, min(j + 2, nb))
            for k in ahead:
                copies[i * nb + k].wait()
            both = jnp.concatenate([rows[i, k].reshape(2 * blk, nocc) for k in ahead], axis=1)
            split = jnp.dot(pick, both, preferred_element_type=F32).astype(BF16)
            for k in ahead:
                for c in range(2):
                    piece = split[c * blk : (c + 1) * blk, (k - j) * nocc : (k - j + 1) * nocc]
                    out[k, :, c * nocc : (c + 1) * nocc] = piece


def pack(trial, where, planes, nb, blk):
    nocc = trial.shape[3]
    return pl.pallas_call(
        pack_kernel,
        out_shape=(jax.ShapeDtypeStruct((nb, blk, 2 * nocc), BF16),) * planes,
        in_specs=[SMEM, ANY],
        out_specs=(VMEM,) * planes,
        scratch_shapes=[pltpu.VMEM((planes, nb, blk, 2, nocc), BF16), pltpu.SemaphoreType.DMA((planes, nb))],
        compiler_params=pltpu.CompilerParams(vmem_limit_bytes=52 * MIB),
        name="pack",
    )(where, trial)


def occupied_kernel(ids, meta, occupied, values, keep, send, table):
    batches, sig = ids.shape
    blk, nocc = occupied.shape[0] // (table.shape[0] - 1), occupied.shape[2]
    nlocal = table.shape[0] - 1
    pick = selectors(blk)
    for j in range(nlocal):
        both = occupied[j * blk : (j + 1) * blk].reshape(2 * blk, nocc)
        for c in range(2):
            split = jnp.dot(pick[c], both, preferred_element_type=F32)
            table[j, :, c * nocc : (c + 1) * nocc] = split.astype(BF16)
    table[nlocal] = jnp.zeros(table.shape[1:], BF16)

    def block(b, s):
        local = ids[b, s] - meta[0]
        return table[jnp.where((local >= 0) & (local < nlocal), local, nlocal)]

    for b in range(batches):
        total = jnp.zeros(keep.shape[1:], F32)
        half, inner = divmod(b, keep.shape[0])
        for s in range(0, sig, 2):
            two = jnp.concatenate([block(b, s), block(b, s + 1)], axis=0)
            total += jnp.dot(values[b, :, s * blk : (s + 2) * blk], two, preferred_element_type=F32)

        @pl.when(meta[1] == half)
        def _(total=total, inner=inner):
            keep[inner] = total

        @pl.when(meta[1] != half)
        def _(total=total, inner=inner):
            send[inner] = total.astype(BF16)


def occupied_part(occupied, colloc, blocks, meta, blk):
    batches, npts, _ = colloc.shape
    nocc = occupied.shape[2]
    shape = (batches // 2, npts, 2 * nocc)
    return pl.pallas_call(
        occupied_kernel,
        out_shape=(jax.ShapeDtypeStruct(shape, F32), jax.ShapeDtypeStruct(shape, BF16)),
        in_specs=[SMEM, SMEM, VMEM, VMEM],
        out_specs=(VMEM, VMEM),
        scratch_shapes=[pltpu.VMEM((occupied.shape[0] // blk + 1, blk, 2 * nocc), BF16)],
        compiler_params=params((colloc.shape, 2), (occupied.shape, 4), (shape, 12), (shape, 12)),
        name="occupied",
    )(blocks, meta, occupied, colloc)


def potential_kernel(sizes, ids, meta, *refs):
    tmasks, xmasks, omasks, fmasks, nlocal, rank, first = sizes
    panels, refs = refs[: len(tmasks)], refs[len(tmasks) :]
    values, refs = refs[: len(xmasks)], refs[len(xmasks) :]
    occ, refs = refs[: len(omasks)], refs[len(omasks) :]
    kern, refs = refs[0], refs[1:]
    out, table, x, left, m, tsems, xsems = refs
    nb, blk, width = panels[0].shape
    count, npts = x.shape[1], x.shape[2]
    sig = ids.shape[2]
    copies = []
    for i, (over, side) in enumerate(tmasks):
        at = (meta[3] ^ over) * nlocal + (meta[4] ^ side) * nb
        copies.append(pltpu.make_async_copy(panels[i], table.at[pl.ds(at, nb)], tsems.at[i]))
    loads = []
    todo = []
    at = 0
    for i, piece in enumerate(values):
        loads.append(pltpu.make_async_copy(piece, x.at[pl.ds(at, piece.shape[0])], xsems.at[i]))
        for j, mask in enumerate(xmasks[i]):
            todo += [(i, at + j, mask, b) for b in range(count)]
        at += piece.shape[0]
    for c in copies + loads:
        c.start()
    where = {mask: (i, j) for i, masks in enumerate(omasks) for j, mask in enumerate(masks)}
    dims = (((1,), (1,)), ((), ()))

    def turn_of(mask, b):
        piece, row = where[mask]
        og = occ[piece][row, meta[1] ^ (b // count), b % count]
        half = width // 2
        return jnp.concatenate([og, jnp.concatenate([-og[:, half:], og[:, :half]], axis=1)], axis=0)

    for c in copies:
        c.wait()
    seen = -1
    for i, (piece, row, mask, b) in enumerate(todo):
        if piece != seen:
            loads[piece].wait()
            seen = piece
        f = fmasks.index(mask)
        dens = jnp.zeros((npts, width), F32)
        for s in range(0, sig, 2):
            two = [table[ids[f, first + b, s + t]] for t in range(2)]
            dens += jnp.dot(
                x[row, b, :, s * blk : (s + 2) * blk], jnp.concatenate(two, axis=0), preferred_element_type=F32
            )
        left[i] = dens.astype(BF16)
    for i, (_, _, mask, b) in enumerate(todo):
        rho = lax.dot_general(left[i], turn_of(mask, first + b), dims, preferred_element_type=F32)
        weight = kern[fmasks.index(mask), first + b]
        m[i] = (rho * jnp.concatenate([weight, weight], axis=1)).astype(BF16)
    for i, (_, _, mask, b) in enumerate(todo):
        e = jnp.dot(m[i], turn_of(mask, first + b), preferred_element_type=F32)
        out[meta[5] ^ (mask // rank), b] = e.astype(BF16)


def potential(panels, values, occ, kern, ids, fmasks, meta, nlocal, rank, chunk):
    tmasks = tuple(m for _, m in panels)
    xmasks = tuple(tuple(m) for _, m in values)
    omasks = tuple(tuple(m) for _, m in occ)
    count, npts, span = values[0][0].shape[1:]
    nb, blk, width = panels[0][0].shape
    nsrc = sum(len(m) for m in xmasks)
    sizes = (tmasks, xmasks, omasks, tuple(fmasks), nlocal, rank, chunk * count)
    table = (len(panels) * nb, blk, width)
    x = (nsrc, count, npts, span)
    left = (nsrc * count, npts, width)
    m = (nsrc * count, npts, 2 * npts)
    return pl.pallas_call(
        functools.partial(potential_kernel, sizes),
        out_shape=jax.ShapeDtypeStruct((nsrc, count, npts, width), BF16),
        in_specs=[SMEM, SMEM] + [VMEM] * len(panels) + [ANY] * len(values) + [VMEM] * (len(occ) + 1),
        out_specs=VMEM,
        scratch_shapes=[
            pltpu.VMEM(table, BF16),
            pltpu.VMEM(x, BF16),
            pltpu.VMEM(left, BF16),
            pltpu.VMEM(m, BF16),
            pltpu.SemaphoreType.DMA((len(panels),)),
            pltpu.SemaphoreType.DMA((len(values),)),
        ],
        compiler_params=params((table, 4), (x, 2), (left, 8), (m, 2), (kern.shape, 4)),
        name="potential",
    )(ids, meta, *[a for a, _ in panels], *[a for a, _ in values], *[a for a, _ in occ], kern)


def list_kernel(sizes, ids, meta, facts, place):
    entries, nchunk, rank, nown = sizes
    sig = ids.shape[2]
    nlist = nchunk * rank
    sizes = []
    for t in range(nlist):
        n = jnp.int32(0)
        for f, b, mask, chunk, _, _ in entries:
            if chunk * rank + mask % rank == t:
                for s in range(sig):
                    own = ids[f, b, s] - meta[2]
                    n = n + ((own >= 0) & (own < nown)).astype(jnp.int32)
        sizes.append(n)
    n = jnp.int32(0)
    for t in range(nlist):
        facts[5, t] = n
        place[t] = n
        end = n + sizes[t]
        for k in range(3):
            for f, one in enumerate((0, 0, 0, -1, 0)):
                facts[f, end + k] = jnp.int32(one)
        n = lax.div(end + 3, 4) * 4
    facts[5, nlist] = n
    for f, b, mask, chunk, row, inner in entries:
        for s in range(sig):
            own = ids[f, b, s] - meta[2]

            @pl.when((own >= 0) & (own < nown))
            def _(mask=mask, t=chunk * rank + mask % rank, row=row, inner=inner, s=s, own=own):
                to = place[t]
                place[t] = to + 1
                what = (own, meta[5] ^ (mask // rank), jnp.int32(inner), jnp.int32(row), jnp.int32(s))
                for f, one in enumerate(what):
                    facts[f, to] = one


def entries_of(xmasks, fmasks, nchunk, count):
    out = []
    at = 0
    groups = len(xmasks) // nchunk
    for i, masks in enumerate(xmasks):
        chunk = i // groups
        for j, mask in enumerate(masks):
            out += [(fmasks.index(mask), chunk * count + b, mask, chunk, at + j, b) for b in range(count)]
        at += len(masks)
    return tuple(out)


def pair_list(xmasks, ids, fmasks, meta, rank, nown, nchunk, count, group):
    nsrc, _, sig = ids.shape
    most = -(-(nchunk * (nsrc * count * sig + 3 * rank) + 4) // group) * group
    sizes = (entries_of(xmasks, fmasks, nchunk, count), nchunk, rank, nown)
    return pl.pallas_call(
        functools.partial(list_kernel, sizes),
        out_shape=jax.ShapeDtypeStruct((8, most), jnp.int32),
        in_specs=[SMEM, SMEM],
        out_specs=SMEM,
        scratch_shapes=[pltpu.SMEM((nchunk * rank,), jnp.int32)],
        compiler_params=params(),
        name="pairs",
    )(ids, meta)


def gather_kernel(group, nlist, facts, *refs):
    values, (columns, x, rows, xsems, osems) = refs[:-5], refs[-5:]
    blk = rows.shape[1]
    copies = []
    at = 0
    for i, piece in enumerate(values):
        copies.append(pltpu.make_async_copy(piece, x.at[pl.ds(at, piece.shape[0])], xsems.at[i]))
        at += piece.shape[0]
    for c in copies:
        c.start()
    for c in copies:
        c.wait()
    n = facts[5, nlist]

    def one(i, carry):
        for t in range(4):
            row = facts[3, 4 * i + t]
            start = pl.multiple_of(facts[4, 4 * i + t] * blk, blk)
            column = x[jnp.maximum(row, 0), facts[2, 4 * i + t], :, pl.ds(start, blk)]
            rows[4 * i + t] = jnp.where(row >= 0, column, jnp.zeros_like(column)).T
        return carry

    lax.fori_loop(0, lax.div(n, 4), one, 0)
    outs = [
        pltpu.make_async_copy(rows.at[pl.ds(i * group, group)], columns.at[pl.ds(i * group, group)], osems.at[i])
        for i in range(columns.shape[0] // group)
    ]
    for act in ("start", "wait"):
        for i, c in enumerate(outs):

            @pl.when(i * group < n)
            def _(c=c, act=act):
                getattr(c, act)()


def gather(values, facts, blk, group, nlist):
    flat = [a for pieces in values for a, _ in pieces]
    count, npts, span = flat[0].shape[1:]
    most = facts.shape[1]
    return pl.pallas_call(
        functools.partial(gather_kernel, group, nlist),
        out_shape=jax.ShapeDtypeStruct((most, blk, npts), BF16),
        in_specs=[SMEM] + [ANY] * len(flat),
        out_specs=ANY,
        scratch_shapes=[
            pltpu.VMEM((sum(a.shape[0] for a in flat), count, npts, span), BF16),
            pltpu.VMEM((most, blk, npts), BF16),
            pltpu.SemaphoreType.DMA((len(flat),)),
            pltpu.SemaphoreType.DMA((most // group,)),
        ],
        compiler_params=params(((most, blk, npts), 2), ((sum(a.shape[0] for a in flat), count, npts, span), 2)),
        name="gather",
    )(facts, *flat)


def project_kernel(sizes, facts, meta, columns, *refs):
    nchunk, emasks, rank, group, nown, again = sizes
    ne = len(emasks)
    potentials, refs = refs[:ne], refs[ne + again :]
    out, x, staged, total, xsems, osems = refs
    blk = x.shape[1]
    offsets = sorted({mask // rank for _, masks in emasks for mask in masks})
    n = facts[5, nchunk * rank]
    xcopies = [
        pltpu.make_async_copy(columns.at[pl.ds(i * group, group)], x.at[pl.ds(i * group, group)], xsems.at[i])
        for i in range(columns.shape[0] // group)
    ]
    for i, c in enumerate(xcopies):

        @pl.when(i * group < n)
        def _(c=c):
            c.start()

    total[...] = jnp.zeros_like(total)
    for i, c in enumerate(xcopies):

        @pl.when(i * group < n)
        def _(c=c):
            c.wait()

    for t in range(nchunk * rank):
        mine = [
            (i, j, offsets.index(mask // rank))
            for i, (chunk, masks) in enumerate(emasks)
            for j, mask in enumerate(masks)
            if chunk * rank + mask % rank == t
        ]

        def one(p, carry, mine=mine):
            for at in range(4):
                own, source, b = [facts[f, 4 * p + at] for f in range(3)]
                for i, j, k in mine:
                    total[k, own] += jnp.dot(x[4 * p + at], potentials[i][j, source, b], preferred_element_type=F32)
            return carry

        lax.fori_loop(lax.div(facts[5, t], 4), lax.div(facts[5, t + 1], 4), one, 0)
    nocc = out.shape[2]
    copies = [
        pltpu.make_async_copy(staged.at[k], out.at[meta[5] ^ off], osems.at[k]) for k, off in enumerate(offsets)
    ]
    for k in range(len(offsets)):
        for o in range(nown):
            for c in range(2):
                staged[k, pl.ds(o * 2 * blk + c, blk, stride=2), :] = total[k, o, :, c * nocc : (c + 1) * nocc]
        copies[k].start()
    for c in copies:
        c.wait()


def project(potentials, facts, columns, meta, before, rank, nown, group):
    emasks = tuple((chunk, tuple(m)) for chunk, _, m in potentials)
    nchunk = 1 + max(chunk for chunk, _, _ in potentials)
    nv, _, _, width = potentials[0][1].shape[1:]
    blk = columns.shape[1]
    ne = len(potentials)
    again = before is not None
    nk = len({mask // rank for _, masks in emasks for mask in masks})
    args = [facts, meta, columns, *[a for _, a, _ in potentials]] + ([before] if again else [])
    staged = (nk, nown * blk * 2, width // 2)
    total = (nk, nown, blk, width)
    arrays = [(a.shape, 2) for _, a, _ in potentials]
    return pl.pallas_call(
        functools.partial(project_kernel, (nchunk, emasks, rank, group, nown, int(again))),
        out_shape=jax.ShapeDtypeStruct((nv, nown * blk * 2, width // 2), F32),
        in_specs=[SMEM] * 2 + [ANY] + [VMEM] * ne + [ANY] * int(again),
        out_specs=ANY,
        input_output_aliases={3 + ne: 0} if again else {},
        scratch_shapes=[
            pltpu.VMEM(columns.shape, BF16),
            pltpu.VMEM(staged, F32),
            pltpu.VMEM(total, F32),
            pltpu.SemaphoreType.DMA((columns.shape[0] // group,)),
            pltpu.SemaphoreType.DMA((nk,)),
        ],
        compiler_params=params((columns.shape, 2), (staged, 4), (total, 4), *arrays),
        name="project",
    )(*args)


def swap(array, axis, bit):
    size = lax.axis_size(axis)
    return lax.ppermute(array, axis, [(i, i ^ bit) for i in range(size)])


def across(part, bits):
    pieces = [(part, [0])]
    for bit in bits:
        for a, masks in pieces[:]:
            pieces.append((swap(a, "grid", bit), [m ^ bit for m in masks]))
    return pieces


def within(pieces, bits):
    for bit in bits:
        pieces = pieces + [(swap(a, "grid", bit), [m ^ bit for m in masks]) for a, masks in pieces]
    return pieces


def on_device(trial, occupied, colloc, blocks, coords, weights):
    n_ao, n_grid = lax.axis_size("ao"), lax.axis_size("grid")
    batches, npts, span = colloc.shape
    sig = blocks.shape[1]
    blk = span // sig
    nvec, nocc = trial.shape[1], trial.shape[3]
    nv = nvec // n_ao
    rank = n_grid // nv
    nlocal = trial.shape[0] // blk
    nown = nlocal * n_ao // n_grid
    parts = min(rank, nlocal & -nlocal)
    nb = nlocal // parts
    count = batches // 2
    ao, grid = lax.axis_index("ao"), lax.axis_index("grid")
    vector, side = grid // rank, grid % parts
    meta = jnp.stack([ao * nlocal, ao & 1, grid * nown, ao, side, vector]).astype(jnp.int32)
    high_bits = [rank << b for b in range(nv.bit_length() - 1)]
    low_bits = [1 << b for b in range(rank.bit_length() - 1)]
    part_bits = [1 << b for b in range(parts.bit_length() - 1)]

    panels = []
    far_first = list(reversed(range(n_ao)))
    for planes in (far_first[:1], far_first[1:]):
        where = jnp.stack([side * nb] + [(ao ^ over) * nv + vector for over in planes]).astype(jnp.int32)
        rows = pack(trial, where, len(planes), nb, blk)
        if not panels:
            rows, coords, weights = lax.optimization_barrier((rows, coords, weights))
        for over, one in zip(planes, rows, strict=True):
            panels.append((swap(one, "ao", over) if over else one, (over, 0)))

    near = []
    for chunk in range(2):
        part = colloc[None, chunk * count : (chunk + 1) * count]
        near.append(across(part, high_bits[::-1] if chunk else high_bits))
    far = [within(pieces, low_bits) for pieces in near]

    held, send = occupied_part(occupied, colloc, blocks, meta, blk)
    for s in range(n_ao.bit_length() - 1):
        got = swap(send, "ao", 1 << s)
        held = held + got.astype(F32)
        send = held.astype(BF16)
    other = swap(send, "ao", 1)
    whole = jnp.stack([send, other])[None]
    occ = across(whole, high_bits)

    numbers = jnp.pad(blocks.astype(F32), ((0, 0), (0, npts - sig)))
    extra = jnp.concatenate([numbers[:, None], coords, weights[:, None]], axis=1)
    extra = within(across(extra[None], high_bits), low_bits)
    fmasks = [m for _, masks in extra for m in masks]
    extra = jnp.concatenate([a for a, _ in extra], axis=0)
    ids = extra[:, :, 0, :sig].astype(jnp.int32)
    exact = extra[:nv, :, 1:]
    kern = kernel_matrix(exact[:, :, :3], exact[:, :, 3])
    group = 4 * sig
    xmasks = [m for pieces in far for _, m in pieces]
    facts = pair_list(xmasks, ids, fmasks, meta, rank, nown, 2, count, group)

    for bit in part_bits:
        panels = panels + [(swap(a, "grid", bit), (over, m ^ bit)) for a, (over, m) in panels]
    columns = gather(far, facts, blk, group, 2 * rank)
    early, late = [], []
    for chunk in range(2):
        e = potential(panels, near[chunk], occ, kern, ids, fmasks, meta, nlocal, rank, chunk)
        pieces = across(e[None], high_bits[::-1] if chunk else high_bits)
        early += [(chunk, a, m) for a, m in within(pieces[:-1], low_bits)]
        late += [(chunk, a, m) for a, m in within(pieces[-1:], low_bits)]
    total = project(early, facts, columns, meta, None, rank, nown, group)
    total = project(late, facts, columns, meta, total, rank, nown, group)
    return total.reshape(nv, nown * blk, 2, nocc)


def solution(mesh):
    in_specs = (
        P("ao", None, None, None),
        P("ao", None, None),
        P("grid", None, None),
        P("grid", None),
        P("grid", None, None),
        P("grid", None),
    )
    out_specs = P("ao", "grid", None, None)

    return jax.shard_map(on_device, mesh=mesh, in_specs=in_specs, out_specs=out_specs, check_vma=False)
```

```python
import functools
import math

import jax
import jax.numpy as jnp
from jax import lax
from jax.experimental import pallas as pl
from jax.experimental.pallas import tpu as pltpu
from jax.sharding import PartitionSpec as P

F32 = jnp.float32
BF16 = jnp.bfloat16
MIB = 1024 * 1024


def params(*arrays):
    total = sum(math.prod(shape) * size for shape, size in arrays)
    return pltpu.CompilerParams(vmem_limit_bytes=min(60 * MIB, total + 6 * MIB))


SMEM = pl.BlockSpec(memory_space=pltpu.SMEM)
VMEM = pl.BlockSpec(memory_space=pltpu.VMEM)
ANY = pl.BlockSpec(memory_space=pl.ANY)


def kernel_matrix(points, quad):
    differ = points[..., :, None, :] - points[..., :, :, None]
    square = jnp.sum(differ * differ, axis=-3)
    return quad[..., :, None] * quad[..., None, :] / jnp.sqrt(square + 0.25)


def selectors(blk):
    ao = lax.broadcasted_iota(jnp.int32, (blk, 2 * blk), 0)
    col = lax.broadcasted_iota(jnp.int32, (blk, 2 * blk), 1)
    return [(col == 2 * ao + c).astype(F32).astype(BF16) for c in range(2)]


def pack_kernel(where, trial, *refs):
    outs, (rows, sem) = refs[:-2], refs[-2:]
    nb, blk, width = outs[0].shape
    nocc = width // 2
    copies = []
    for i in range(len(outs)):
        for j in range(nb):
            at = (where[0] + j) * blk
            copies.append(
                pltpu.make_async_copy(trial.at[pl.ds(at, blk), where[1 + i]], rows.at[i, j], sem.at[i, j])
            )
    for c in copies:
        c.start()
    pick = jnp.concatenate(selectors(blk), axis=0)
    for i, out in enumerate(outs):
        for j in range(0, nb, 2):
            ahead = range(j, min(j + 2, nb))
            for k in ahead:
                copies[i * nb + k].wait()
            both = jnp.concatenate([rows[i, k].reshape(2 * blk, nocc) for k in ahead], axis=1)
            split = jnp.dot(pick, both, preferred_element_type=F32).astype(BF16)
            for k in ahead:
                for c in range(2):
                    piece = split[c * blk : (c + 1) * blk, (k - j) * nocc : (k - j + 1) * nocc]
                    out[k, :, c * nocc : (c + 1) * nocc] = piece


def pack(trial, where, planes, nb, blk):
    nocc = trial.shape[3]
    return pl.pallas_call(
        pack_kernel,
        out_shape=(jax.ShapeDtypeStruct((nb, blk, 2 * nocc), BF16),) * planes,
        in_specs=[SMEM, ANY],
        out_specs=(VMEM,) * planes,
        scratch_shapes=[pltpu.VMEM((planes, nb, blk, 2, nocc), BF16), pltpu.SemaphoreType.DMA((planes, nb))],
        compiler_params=pltpu.CompilerParams(vmem_limit_bytes=52 * MIB),
        name="pack",
    )(where, trial)


def occupied_kernel(ids, meta, occupied, values, keep, send, table):
    batches, sig = ids.shape
    blk, nocc = occupied.shape[0] // (table.shape[0] - 1), occupied.shape[2]
    nlocal = table.shape[0] - 1
    pick = selectors(blk)
    for j in range(nlocal):
        both = occupied[j * blk : (j + 1) * blk].reshape(2 * blk, nocc)
        for c in range(2):
            split = jnp.dot(pick[c], both, preferred_element_type=F32)
            table[j, :, c * nocc : (c + 1) * nocc] = split.astype(BF16)
    table[nlocal] = jnp.zeros(table.shape[1:], BF16)

    def block(b, s):
        local = ids[b, s] - meta[0]
        return table[jnp.where((local >= 0) & (local < nlocal), local, nlocal)]

    for b in range(batches):
        total = jnp.zeros(keep.shape[1:], F32)
        half, inner = divmod(b, keep.shape[0])
        for s in range(0, sig, 2):
            two = jnp.concatenate([block(b, s), block(b, s + 1)], axis=0)
            total += jnp.dot(values[b, :, s * blk : (s + 2) * blk], two, preferred_element_type=F32)

        @pl.when(meta[1] == half)
        def _(total=total, inner=inner):
            keep[inner] = total

        @pl.when(meta[1] != half)
        def _(total=total, inner=inner):
            send[inner] = total.astype(BF16)


def occupied_part(occupied, colloc, blocks, meta, blk):
    batches, npts, _ = colloc.shape
    nocc = occupied.shape[2]
    shape = (batches // 2, npts, 2 * nocc)
    return pl.pallas_call(
        occupied_kernel,
        out_shape=(jax.ShapeDtypeStruct(shape, F32), jax.ShapeDtypeStruct(shape, BF16)),
        in_specs=[SMEM, SMEM, VMEM, VMEM],
        out_specs=(VMEM, VMEM),
        scratch_shapes=[pltpu.VMEM((occupied.shape[0] // blk + 1, blk, 2 * nocc), BF16)],
        compiler_params=params((colloc.shape, 2), (occupied.shape, 4), (shape, 12), (shape, 12)),
        name="occupied",
    )(blocks, meta, occupied, colloc)


def potential_kernel(sizes, ids, meta, *refs):
    tmasks, xmasks, omasks, fmasks, nlocal, rank, nchunk = sizes
    panels, refs = refs[: len(tmasks)], refs[len(tmasks) :]
    values, refs = refs[: len(xmasks)], refs[len(xmasks) :]
    occ, refs = refs[: len(omasks)], refs[len(omasks) :]
    kern, refs = refs[0], refs[1:]
    outs, (table, x, left, m, tsems, xsems) = refs[:nchunk], refs[nchunk:]
    groups = len(values) // nchunk
    nb, blk, width = panels[0].shape
    count, npts = x.shape[1], x.shape[2]
    sig = ids.shape[2]
    copies = []
    for i, (over, side) in enumerate(tmasks):
        at = (meta[3] ^ over) * nlocal + (meta[4] ^ side) * nb
        copies.append(pltpu.make_async_copy(panels[i], table.at[pl.ds(at, nb)], tsems.at[i]))
    loads = []
    todo = []
    at = 0
    for i, piece in enumerate(values):
        loads.append(pltpu.make_async_copy(piece, x.at[pl.ds(at, piece.shape[0])], xsems.at[i]))
        for j, mask in enumerate(xmasks[i]):
            todo += [(i, i // groups, at + j, mask, b) for b in range(count)]
        at += piece.shape[0]
    for c in copies + loads:
        c.start()
    where = {mask: (i, j) for i, masks in enumerate(omasks) for j, mask in enumerate(masks)}
    dims = (((1,), (1,)), ((), ()))

    def turn_of(mask, b):
        piece, row = where[mask]
        og = occ[piece][row, meta[1] ^ (b // count), b % count]
        half = width // 2
        return jnp.concatenate([og, jnp.concatenate([-og[:, half:], og[:, :half]], axis=1)], axis=0)

    for c in copies:
        c.wait()
    seen = -1
    for i, (piece, chunk, row, mask, b) in enumerate(todo):
        if piece != seen:
            loads[piece].wait()
            seen = piece
        f = fmasks.index(mask)
        dens = jnp.zeros((npts, width), F32)
        for s in range(0, sig, 2):
            two = [table[ids[f, chunk * count + b, s + t]] for t in range(2)]
            dens += jnp.dot(
                x[row, b, :, s * blk : (s + 2) * blk], jnp.concatenate(two, axis=0), preferred_element_type=F32
            )
        left[i] = dens.astype(BF16)
    for i, (_, chunk, _, mask, b) in enumerate(todo):
        rho = lax.dot_general(left[i], turn_of(mask, chunk * count + b), dims, preferred_element_type=F32)
        weight = kern[fmasks.index(mask), chunk * count + b]
        m[i] = (rho * jnp.concatenate([weight, weight], axis=1)).astype(BF16)
    for i, (_, chunk, _, mask, b) in enumerate(todo):
        e = jnp.dot(m[i], turn_of(mask, chunk * count + b), preferred_element_type=F32)
        outs[chunk][meta[5] ^ (mask // rank), b] = e.astype(BF16)


def potential(panels, chunks, occ, kern, ids, fmasks, meta, nlocal, rank):
    tmasks = tuple(m for _, m in panels)
    nchunk = len(chunks)
    values = [piece for pieces in chunks for piece in pieces]
    xmasks = tuple(tuple(m) for _, m in values)
    omasks = tuple(tuple(m) for _, m in occ)
    count, npts, span = values[0][0].shape[1:]
    nb, blk, width = panels[0][0].shape
    nsrc = sum(len(m) for m in xmasks)
    sizes = (tmasks, xmasks, omasks, tuple(fmasks), nlocal, rank, nchunk)
    table = (len(panels) * nb, blk, width)
    x = (nsrc, count, npts, span)
    left = (nsrc * count, npts, width)
    m = (nsrc * count, npts, 2 * npts)
    return pl.pallas_call(
        functools.partial(potential_kernel, sizes),
        out_shape=(jax.ShapeDtypeStruct((nsrc // nchunk, count, npts, width), BF16),) * nchunk,
        in_specs=[SMEM, SMEM] + [VMEM] * len(panels) + [ANY] * len(values) + [VMEM] * (len(occ) + 1),
        out_specs=(VMEM,) * nchunk,
        scratch_shapes=[
            pltpu.VMEM(table, BF16),
            pltpu.VMEM(x, BF16),
            pltpu.VMEM(left, BF16),
            pltpu.VMEM(m, BF16),
            pltpu.SemaphoreType.DMA((len(panels),)),
            pltpu.SemaphoreType.DMA((len(values),)),
        ],
        compiler_params=params((table, 4), (x, 2), (left, 8), (m, 2), (kern.shape, 4)),
        name="potential",
    )(ids, meta, *[a for a, _ in panels], *[a for a, _ in values], *[a for a, _ in occ], kern)


def list_kernel(sizes, ids, meta, facts, place):
    entries, nchunk, rank, nown = sizes
    sig = ids.shape[2]
    nlist = nchunk * rank
    sizes = []
    for t in range(nlist):
        n = jnp.int32(0)
        for f, b, mask, chunk, _, _ in entries:
            if chunk * rank + mask % rank == t:
                for s in range(sig):
                    own = ids[f, b, s] - meta[2]
                    n = n + ((own >= 0) & (own < nown)).astype(jnp.int32)
        sizes.append(n)
    n = jnp.int32(0)
    for t in range(nlist):
        facts[5, t] = n
        place[t] = n
        end = n + sizes[t]
        for k in range(3):
            for f, one in enumerate((0, 0, 0, -1, 0)):
                facts[f, end + k] = jnp.int32(one)
        n = lax.div(end + 3, 4) * 4
    facts[5, nlist] = n
    for f, b, mask, chunk, row, inner in entries:
        for s in range(sig):
            own = ids[f, b, s] - meta[2]

            @pl.when((own >= 0) & (own < nown))
            def _(mask=mask, t=chunk * rank + mask % rank, row=row, inner=inner, s=s, own=own):
                to = place[t]
                place[t] = to + 1
                what = (own, meta[5] ^ (mask // rank), jnp.int32(inner), jnp.int32(row), jnp.int32(s))
                for f, one in enumerate(what):
                    facts[f, to] = one


def entries_of(xmasks, fmasks, nchunk, count):
    out = []
    at = 0
    groups = len(xmasks) // nchunk
    for i, masks in enumerate(xmasks):
        chunk = i // groups
        for j, mask in enumerate(masks):
            out += [(fmasks.index(mask), chunk * count + b, mask, chunk, at + j, b) for b in range(count)]
        at += len(masks)
    return tuple(out)


def pair_list(xmasks, ids, fmasks, meta, rank, nown, nchunk, count, group):
    nsrc, _, sig = ids.shape
    most = -(-(nchunk * (nsrc * count * sig + 3 * rank) + 4) // group) * group
    sizes = (entries_of(xmasks, fmasks, nchunk, count), nchunk, rank, nown)
    return pl.pallas_call(
        functools.partial(list_kernel, sizes),
        out_shape=jax.ShapeDtypeStruct((8, most), jnp.int32),
        in_specs=[SMEM, SMEM],
        out_specs=SMEM,
        scratch_shapes=[pltpu.SMEM((nchunk * rank,), jnp.int32)],
        compiler_params=params(),
        name="pairs",
    )(ids, meta)


def gather_kernel(group, nlist, facts, *refs):
    values, (columns, x, rows, xsems, osems) = refs[:-5], refs[-5:]
    blk = rows.shape[1]
    copies = []
    at = 0
    for i, piece in enumerate(values):
        copies.append(pltpu.make_async_copy(piece, x.at[pl.ds(at, piece.shape[0])], xsems.at[i]))
        at += piece.shape[0]
    for c in copies:
        c.start()
    for c in copies:
        c.wait()
    n = facts[5, nlist]

    def one(i, carry):
        for t in range(4):
            row = facts[3, 4 * i + t]
            start = pl.multiple_of(facts[4, 4 * i + t] * blk, blk)
            column = x[jnp.maximum(row, 0), facts[2, 4 * i + t], :, pl.ds(start, blk)]
            rows[4 * i + t] = jnp.where(row >= 0, column, jnp.zeros_like(column)).T
        return carry

    lax.fori_loop(0, lax.div(n, 4), one, 0)
    outs = [
        pltpu.make_async_copy(rows.at[pl.ds(i * group, group)], columns.at[pl.ds(i * group, group)], osems.at[i])
        for i in range(columns.shape[0] // group)
    ]
    for act in ("start", "wait"):
        for i, c in enumerate(outs):

            @pl.when(i * group < n)
            def _(c=c, act=act):
                getattr(c, act)()


def gather(values, facts, blk, group, nlist):
    flat = [a for pieces in values for a, _ in pieces]
    count, npts, span = flat[0].shape[1:]
    most = facts.shape[1]
    return pl.pallas_call(
        functools.partial(gather_kernel, group, nlist),
        out_shape=jax.ShapeDtypeStruct((most, blk, npts), BF16),
        in_specs=[SMEM] + [ANY] * len(flat),
        out_specs=ANY,
        scratch_shapes=[
            pltpu.VMEM((sum(a.shape[0] for a in flat), count, npts, span), BF16),
            pltpu.VMEM((most, blk, npts), BF16),
            pltpu.SemaphoreType.DMA((len(flat),)),
            pltpu.SemaphoreType.DMA((most // group,)),
        ],
        compiler_params=params(((most, blk, npts), 2), ((sum(a.shape[0] for a in flat), count, npts, span), 2)),
        name="gather",
    )(facts, *flat)


def project_kernel(sizes, facts, meta, columns, *refs):
    nchunk, emasks, rank, group, nown, again = sizes
    ne = len(emasks)
    potentials, refs = refs[:ne], refs[ne + again :]
    out, x, staged, total, xsems, osems = refs
    blk = x.shape[1]
    offsets = sorted({mask // rank for _, masks in emasks for mask in masks})
    n = facts[5, nchunk * rank]
    xcopies = [
        pltpu.make_async_copy(columns.at[pl.ds(i * group, group)], x.at[pl.ds(i * group, group)], xsems.at[i])
        for i in range(columns.shape[0] // group)
    ]
    for i, c in enumerate(xcopies):

        @pl.when(i * group < n)
        def _(c=c):
            c.start()

    total[...] = jnp.zeros_like(total)
    for i, c in enumerate(xcopies):

        @pl.when(i * group < n)
        def _(c=c):
            c.wait()

    for t in range(nchunk * rank):
        mine = [
            (i, j, offsets.index(mask // rank))
            for i, (chunk, masks) in enumerate(emasks)
            for j, mask in enumerate(masks)
            if chunk * rank + mask % rank == t
        ]

        def one(p, carry, mine=mine):
            for at in range(4):
                own, source, b = [facts[f, 4 * p + at] for f in range(3)]
                for i, j, k in mine:
                    total[k, own] += jnp.dot(x[4 * p + at], potentials[i][j, source, b], preferred_element_type=F32)
            return carry

        lax.fori_loop(lax.div(facts[5, t], 4), lax.div(facts[5, t + 1], 4), one, 0)
    nocc = out.shape[2]
    copies = [
        pltpu.make_async_copy(staged.at[k], out.at[meta[5] ^ off], osems.at[k]) for k, off in enumerate(offsets)
    ]
    for k in range(len(offsets)):
        for o in range(nown):
            for c in range(2):
                staged[k, pl.ds(o * 2 * blk + c, blk, stride=2), :] = total[k, o, :, c * nocc : (c + 1) * nocc]
        copies[k].start()
    for c in copies:
        c.wait()


def project(potentials, facts, columns, meta, before, rank, nown, group):
    emasks = tuple((chunk, tuple(m)) for chunk, _, m in potentials)
    nchunk = 1 + max(chunk for chunk, _, _ in potentials)
    nv, _, _, width = potentials[0][1].shape[1:]
    blk = columns.shape[1]
    ne = len(potentials)
    again = before is not None
    nk = len({mask // rank for _, masks in emasks for mask in masks})
    args = [facts, meta, columns, *[a for _, a, _ in potentials]] + ([before] if again else [])
    staged = (nk, nown * blk * 2, width // 2)
    total = (nk, nown, blk, width)
    arrays = [(a.shape, 2) for _, a, _ in potentials]
    return pl.pallas_call(
        functools.partial(project_kernel, (nchunk, emasks, rank, group, nown, int(again))),
        out_shape=jax.ShapeDtypeStruct((nv, nown * blk * 2, width // 2), F32),
        in_specs=[SMEM] * 2 + [ANY] + [VMEM] * ne + [ANY] * int(again),
        out_specs=ANY,
        input_output_aliases={3 + ne: 0} if again else {},
        scratch_shapes=[
            pltpu.VMEM(columns.shape, BF16),
            pltpu.VMEM(staged, F32),
            pltpu.VMEM(total, F32),
            pltpu.SemaphoreType.DMA((columns.shape[0] // group,)),
            pltpu.SemaphoreType.DMA((nk,)),
        ],
        compiler_params=params((columns.shape, 2), (staged, 4), (total, 4), *arrays),
        name="project",
    )(*args)


def swap(array, axis, bit):
    size = lax.axis_size(axis)
    return lax.ppermute(array, axis, [(i, i ^ bit) for i in range(size)])


def across(part, bits):
    pieces = [(part, [0])]
    for bit in bits:
        for a, masks in pieces[:]:
            pieces.append((swap(a, "grid", bit), [m ^ bit for m in masks]))
    return pieces


def within(pieces, bits):
    for bit in bits:
        pieces = pieces + [(swap(a, "grid", bit), [m ^ bit for m in masks]) for a, masks in pieces]
    return pieces


def on_device(trial, occupied, colloc, blocks, coords, weights):
    n_ao, n_grid = lax.axis_size("ao"), lax.axis_size("grid")
    batches, npts, span = colloc.shape
    sig = blocks.shape[1]
    blk = span // sig
    nvec, nocc = trial.shape[1], trial.shape[3]
    nv = nvec // n_ao
    rank = n_grid // nv
    nlocal = trial.shape[0] // blk
    nown = nlocal * n_ao // n_grid
    parts = min(rank, nlocal & -nlocal)
    nb = nlocal // parts
    count = batches // 2
    ao, grid = lax.axis_index("ao"), lax.axis_index("grid")
    vector, side = grid // rank, grid % parts
    meta = jnp.stack([ao * nlocal, ao & 1, grid * nown, ao, side, vector]).astype(jnp.int32)
    high_bits = [rank << b for b in range(nv.bit_length() - 1)]
    low_bits = [1 << b for b in range(rank.bit_length() - 1)]
    part_bits = [1 << b for b in range(parts.bit_length() - 1)]

    panels = []
    far_first = list(reversed(range(n_ao)))
    for planes in (far_first[:1], far_first[1:]):
        where = jnp.stack([side * nb] + [(ao ^ over) * nv + vector for over in planes]).astype(jnp.int32)
        rows = pack(trial, where, len(planes), nb, blk)
        if not panels:
            rows, coords, weights, occupied = lax.optimization_barrier((rows, coords, weights, occupied))
        for over, one in zip(planes, rows, strict=True):
            panels.append((swap(one, "ao", over) if over else one, (over, 0)))

    near = []
    for chunk in range(2):
        part = colloc[None, chunk * count : (chunk + 1) * count]
        near.append(across(part, high_bits[::-1] if chunk else high_bits))
    far = [within(pieces, low_bits) for pieces in near]

    held, send = occupied_part(occupied, colloc, blocks, meta, blk)
    for s in range(n_ao.bit_length() - 1):
        got = swap(send, "ao", 1 << s)
        held = held + got.astype(F32)
        send = held.astype(BF16)
    other = swap(send, "ao", 1)
    whole = jnp.stack([send, other])[None]
    occ = across(whole, high_bits)

    numbers = jnp.pad(blocks.astype(F32), ((0, 0), (0, npts - sig)))
    extra = jnp.concatenate([numbers[:, None], coords, weights[:, None]], axis=1)
    extra = within(across(extra[None], high_bits), low_bits)
    fmasks = [m for _, masks in extra for m in masks]
    extra = jnp.concatenate([a for a, _ in extra], axis=0)
    ids = extra[:, :, 0, :sig].astype(jnp.int32)
    exact = extra[:nv, :, 1:]
    kern = kernel_matrix(exact[:, :, :3], exact[:, :, 3])
    group = 4 * sig
    xmasks = [m for pieces in far for _, m in pieces]
    facts = pair_list(xmasks, ids, fmasks, meta, rank, nown, 2, count, group)

    for bit in part_bits:
        panels = panels + [(swap(a, "grid", bit), (over, m ^ bit)) for a, (over, m) in panels]
    columns = gather(far, facts, blk, group, 2 * rank)
    parts = potential(panels, near, occ, kern, ids, fmasks, meta, nlocal, rank)
    early, late = [], []
    for chunk in range(2):
        pieces = across(parts[chunk][None], high_bits[::-1] if chunk else high_bits)
        early += [(chunk, a, m) for a, m in within(pieces[:-1], low_bits)]
        late += [(chunk, a, m) for a, m in within(pieces[-1:], low_bits)]
    total = project(early, facts, columns, meta, None, rank, nown, group)
    total = project(late, facts, columns, meta, total, rank, nown, group)
    return total.reshape(nv, nown * blk, 2, nocc)


def solution(mesh):
    in_specs = (
        P("ao", None, None, None),
        P("ao", None, None),
        P("grid", None, None),
        P("grid", None),
        P("grid", None, None),
        P("grid", None),
    )
    out_specs = P("ao", "grid", None, None)

    return jax.shard_map(on_device, mesh=mesh, in_specs=in_specs, out_specs=out_specs, check_vma=False)
```

```python
import functools
import math

import jax
import jax.numpy as jnp
from jax import lax
from jax.experimental import pallas as pl
from jax.experimental.pallas import tpu as pltpu
from jax.sharding import PartitionSpec as P

F32 = jnp.float32
BF16 = jnp.bfloat16
MIB = 1024 * 1024


def params(*arrays):
    total = sum(math.prod(shape) * size for shape, size in arrays)
    return pltpu.CompilerParams(vmem_limit_bytes=min(60 * MIB, total + 6 * MIB))


SMEM = pl.BlockSpec(memory_space=pltpu.SMEM)
VMEM = pl.BlockSpec(memory_space=pltpu.VMEM)
ANY = pl.BlockSpec(memory_space=pl.ANY)


def kernel_matrix(points, quad):
    differ = points[..., :, None, :] - points[..., :, :, None]
    square = jnp.sum(differ * differ, axis=-3)
    return quad[..., :, None] * quad[..., None, :] / jnp.sqrt(square + 0.25)


def selectors(blk):
    ao = lax.broadcasted_iota(jnp.int32, (blk, 2 * blk), 0)
    col = lax.broadcasted_iota(jnp.int32, (blk, 2 * blk), 1)
    return [(col == 2 * ao + c).astype(F32).astype(BF16) for c in range(2)]


def pack_kernel(where, trial, *refs):
    outs, (rows, sem) = refs[:-2], refs[-2:]
    nb, blk, width = outs[0].shape
    nocc = width // 2
    copies = []
    for i in range(len(outs)):
        for j in range(nb):
            at = (where[0] + j) * blk
            copies.append(
                pltpu.make_async_copy(trial.at[pl.ds(at, blk), where[1 + i]], rows.at[i, j], sem.at[i, j])
            )
    for c in copies:
        c.start()
    pick = jnp.concatenate(selectors(blk), axis=0)
    for i, out in enumerate(outs):
        for j in range(0, nb, 2):
            ahead = range(j, min(j + 2, nb))
            for k in ahead:
                copies[i * nb + k].wait()
            both = jnp.concatenate([rows[i, k].reshape(2 * blk, nocc) for k in ahead], axis=1)
            split = jnp.dot(pick, both, preferred_element_type=F32).astype(BF16)
            for k in ahead:
                for c in range(2):
                    piece = split[c * blk : (c + 1) * blk, (k - j) * nocc : (k - j + 1) * nocc]
                    out[k, :, c * nocc : (c + 1) * nocc] = piece


def pack(trial, where, planes, nb, blk):
    nocc = trial.shape[3]
    return pl.pallas_call(
        pack_kernel,
        out_shape=(jax.ShapeDtypeStruct((nb, blk, 2 * nocc), BF16),) * planes,
        in_specs=[SMEM, ANY],
        out_specs=(VMEM,) * planes,
        scratch_shapes=[pltpu.VMEM((planes, nb, blk, 2, nocc), BF16), pltpu.SemaphoreType.DMA((planes, nb))],
        compiler_params=pltpu.CompilerParams(vmem_limit_bytes=52 * MIB),
        name="pack",
    )(where, trial)


def occupied_kernel(ids, meta, occupied, values, keep, send, table):
    batches, sig = ids.shape
    blk, nocc = occupied.shape[0] // (table.shape[0] - 1), occupied.shape[2]
    nlocal = table.shape[0] - 1
    pick = selectors(blk)
    for j in range(nlocal):
        both = occupied[j * blk : (j + 1) * blk].reshape(2 * blk, nocc)
        for c in range(2):
            split = jnp.dot(pick[c], both, preferred_element_type=F32)
            table[j, :, c * nocc : (c + 1) * nocc] = split.astype(BF16)
    table[nlocal] = jnp.zeros(table.shape[1:], BF16)

    def block(b, s):
        local = ids[b, s] - meta[0]
        return table[jnp.where((local >= 0) & (local < nlocal), local, nlocal)]

    for b in range(batches):
        total = jnp.zeros(keep.shape[1:], F32)
        half, inner = divmod(b, keep.shape[0])
        for s in range(0, sig, 2):
            two = jnp.concatenate([block(b, s), block(b, s + 1)], axis=0)
            total += jnp.dot(values[b, :, s * blk : (s + 2) * blk], two, preferred_element_type=F32)

        @pl.when(meta[1] == half)
        def _(total=total, inner=inner):
            keep[inner] = total

        @pl.when(meta[1] != half)
        def _(total=total, inner=inner):
            send[inner] = total.astype(BF16)


def occupied_part(occupied, colloc, blocks, meta, blk):
    batches, npts, _ = colloc.shape
    nocc = occupied.shape[2]
    shape = (batches // 2, npts, 2 * nocc)
    return pl.pallas_call(
        occupied_kernel,
        out_shape=(jax.ShapeDtypeStruct(shape, F32), jax.ShapeDtypeStruct(shape, BF16)),
        in_specs=[SMEM, SMEM, VMEM, VMEM],
        out_specs=(VMEM, VMEM),
        scratch_shapes=[pltpu.VMEM((occupied.shape[0] // blk + 1, blk, 2 * nocc), BF16)],
        compiler_params=params((colloc.shape, 2), (occupied.shape, 4), (shape, 12), (shape, 12)),
        name="occupied",
    )(blocks, meta, occupied, colloc)


def potential_kernel(sizes, ids, meta, *refs):
    tmasks, xmasks, omasks, fmasks, nlocal, rank, nchunk = sizes
    panels, refs = refs[: len(tmasks)], refs[len(tmasks) :]
    values, refs = refs[: len(xmasks)], refs[len(xmasks) :]
    occ, refs = refs[: len(omasks)], refs[len(omasks) :]
    kern, refs = refs[0], refs[1:]
    outs, (table, x, left, m, tsems, xsems) = refs[:nchunk], refs[nchunk:]
    groups = len(values) // nchunk
    nb, blk, width = panels[0].shape
    count, npts = x.shape[1], x.shape[2]
    sig = ids.shape[2]
    copies = []
    for i, (over, side) in enumerate(tmasks):
        at = (meta[3] ^ over) * nlocal + (meta[4] ^ side) * nb
        copies.append(pltpu.make_async_copy(panels[i], table.at[pl.ds(at, nb)], tsems.at[i]))
    loads = []
    todo = []
    at = 0
    for i, piece in enumerate(values):
        loads.append(pltpu.make_async_copy(piece, x.at[pl.ds(at, piece.shape[0])], xsems.at[i]))
        for j, mask in enumerate(xmasks[i]):
            todo += [(i, i // groups, at + j, mask, b) for b in range(count)]
        at += piece.shape[0]
    for c in copies + loads:
        c.start()
    where = {mask: (i, j) for i, masks in enumerate(omasks) for j, mask in enumerate(masks)}
    dims = (((1,), (1,)), ((), ()))

    def turn_of(mask, b):
        piece, row = where[mask]
        og = occ[piece][row, meta[1] ^ (b // count), b % count]
        half = width // 2
        return jnp.concatenate([og, jnp.concatenate([-og[:, half:], og[:, :half]], axis=1)], axis=0)

    for c in copies:
        c.wait()
    seen = -1
    for i, (piece, chunk, row, mask, b) in enumerate(todo):
        if piece != seen:
            loads[piece].wait()
            seen = piece
        f = fmasks.index(mask)
        dens = jnp.zeros((npts, width), F32)
        for s in range(0, sig, 2):
            two = [table[ids[f, chunk * count + b, s + t]] for t in range(2)]
            dens += jnp.dot(
                x[row, b, :, s * blk : (s + 2) * blk], jnp.concatenate(two, axis=0), preferred_element_type=F32
            )
        left[i] = dens.astype(BF16)
    for i, (_, chunk, _, mask, b) in enumerate(todo):
        rho = lax.dot_general(left[i], turn_of(mask, chunk * count + b), dims, preferred_element_type=F32)
        weight = kern[fmasks.index(mask), chunk * count + b]
        m[i] = (rho * jnp.concatenate([weight, weight], axis=1)).astype(BF16)
    for i, (_, chunk, _, mask, b) in enumerate(todo):
        e = jnp.dot(m[i], turn_of(mask, chunk * count + b), preferred_element_type=F32)
        outs[chunk][meta[5] ^ (mask // rank), b] = e.astype(BF16)


def potential(panels, chunks, occ, kern, ids, fmasks, meta, nlocal, rank):
    tmasks = tuple(m for _, m in panels)
    nchunk = len(chunks)
    values = [piece for pieces in chunks for piece in pieces]
    xmasks = tuple(tuple(m) for _, m in values)
    omasks = tuple(tuple(m) for _, m in occ)
    count, npts, span = values[0][0].shape[1:]
    nb, blk, width = panels[0][0].shape
    nsrc = sum(len(m) for m in xmasks)
    sizes = (tmasks, xmasks, omasks, tuple(fmasks), nlocal, rank, nchunk)
    table = (len(panels) * nb, blk, width)
    x = (nsrc, count, npts, span)
    left = (nsrc * count, npts, width)
    m = (nsrc * count, npts, 2 * npts)
    return pl.pallas_call(
        functools.partial(potential_kernel, sizes),
        out_shape=(jax.ShapeDtypeStruct((nsrc // nchunk, count, npts, width), BF16),) * nchunk,
        in_specs=[SMEM, SMEM] + [VMEM] * len(panels) + [ANY] * len(values) + [VMEM] * (len(occ) + 1),
        out_specs=(VMEM,) * nchunk,
        scratch_shapes=[
            pltpu.VMEM(table, BF16),
            pltpu.VMEM(x, BF16),
            pltpu.VMEM(left, BF16),
            pltpu.VMEM(m, BF16),
            pltpu.SemaphoreType.DMA((len(panels),)),
            pltpu.SemaphoreType.DMA((len(values),)),
        ],
        compiler_params=params((table, 4), (x, 2), (left, 8), (m, 2), (kern.shape, 4)),
        name="potential",
    )(ids, meta, *[a for a, _ in panels], *[a for a, _ in values], *[a for a, _ in occ], kern)


def list_kernel(sizes, ids, meta, facts, place):
    entries, nchunk, rank, nown = sizes
    sig = ids.shape[2]
    nlist = nchunk * rank
    sizes = []
    for t in range(nlist):
        n = jnp.int32(0)
        for f, b, mask, chunk, _, _ in entries:
            if chunk * rank + mask % rank == t:
                for s in range(sig):
                    own = ids[f, b, s] - meta[2]
                    n = n + ((own >= 0) & (own < nown)).astype(jnp.int32)
        sizes.append(n)
    n = jnp.int32(0)
    for t in range(nlist):
        facts[5, t] = n
        place[t] = n
        end = n + sizes[t]
        for k in range(3):
            for f, one in enumerate((0, 0, 0, -1, 0)):
                facts[f, end + k] = jnp.int32(one)
        n = lax.div(end + 3, 4) * 4
    facts[5, nlist] = n
    for f, b, mask, chunk, row, inner in entries:
        for s in range(sig):
            own = ids[f, b, s] - meta[2]

            @pl.when((own >= 0) & (own < nown))
            def _(mask=mask, t=chunk * rank + mask % rank, row=row, inner=inner, s=s, own=own):
                to = place[t]
                place[t] = to + 1
                what = (own, meta[5] ^ (mask // rank), jnp.int32(inner), jnp.int32(row), jnp.int32(s))
                for f, one in enumerate(what):
                    facts[f, to] = one


def entries_of(xmasks, fmasks, nchunk, count):
    out = []
    at = 0
    groups = len(xmasks) // nchunk
    for i, masks in enumerate(xmasks):
        chunk = i // groups
        for j, mask in enumerate(masks):
            out += [(fmasks.index(mask), chunk * count + b, mask, chunk, at + j, b) for b in range(count)]
        at += len(masks)
    return tuple(out)


def pair_list(xmasks, ids, fmasks, meta, rank, nown, nchunk, count, group):
    nsrc, _, sig = ids.shape
    most = -(-(nchunk * (nsrc * count * sig + 3 * rank) + 4) // group) * group
    sizes = (entries_of(xmasks, fmasks, nchunk, count), nchunk, rank, nown)
    return pl.pallas_call(
        functools.partial(list_kernel, sizes),
        out_shape=jax.ShapeDtypeStruct((8, most), jnp.int32),
        in_specs=[SMEM, SMEM],
        out_specs=SMEM,
        scratch_shapes=[pltpu.SMEM((nchunk * rank,), jnp.int32)],
        compiler_params=params(),
        name="pairs",
    )(ids, meta)


def gather_kernel(nlist, facts, *refs):
    values, (columns, x, xsems) = refs[:-3], refs[-3:]
    blk = columns.shape[1]
    copies = []
    at = 0
    for i, piece in enumerate(values):
        copies.append(pltpu.make_async_copy(piece, x.at[pl.ds(at, piece.shape[0])], xsems.at[i]))
        at += piece.shape[0]
    for c in copies:
        c.start()
    for c in copies:
        c.wait()

    def one(i, carry):
        for t in range(4):
            row = facts[3, 4 * i + t]
            start = pl.multiple_of(facts[4, 4 * i + t] * blk, blk)
            column = x[jnp.maximum(row, 0), facts[2, 4 * i + t], :, pl.ds(start, blk)]
            columns[4 * i + t] = jnp.where(row >= 0, column, jnp.zeros_like(column)).T
        return carry

    lax.fori_loop(0, lax.div(facts[5, nlist], 4), one, 0)


def gather(values, facts, blk, nlist):
    flat = [a for pieces in values for a, _ in pieces]
    count, npts, span = flat[0].shape[1:]
    most = facts.shape[1]
    x = (sum(a.shape[0] for a in flat), count, npts, span)
    large = most * blk * npts * 2 > 16 * MIB
    return pl.pallas_call(
        functools.partial(gather_kernel, nlist),
        out_shape=jax.ShapeDtypeStruct((most, blk, npts), BF16),
        in_specs=[SMEM] + [ANY] * len(flat),
        out_specs=VMEM,
        scratch_shapes=[pltpu.VMEM(x, BF16), pltpu.SemaphoreType.DMA((len(flat),))],
        compiler_params=params((x, 2), ((most if large else 0, blk, npts), 2)),
        name="gather",
    )(facts, *flat)


def project_kernel(sizes, facts, meta, columns, *refs):
    nchunk, emasks, rank, nown, again = sizes
    ne = len(emasks)
    potentials, refs = refs[:ne], refs[ne + again :]
    out, staged, total, osems = refs
    blk = columns.shape[1]
    offsets = sorted({mask // rank for _, masks in emasks for mask in masks})
    total[...] = jnp.zeros_like(total)
    for t in range(nchunk * rank):
        mine = [
            (i, j, offsets.index(mask // rank))
            for i, (chunk, masks) in enumerate(emasks)
            for j, mask in enumerate(masks)
            if chunk * rank + mask % rank == t
        ]

        def one(p, carry, mine=mine):
            for at in range(4):
                own, source, b = [facts[f, 4 * p + at] for f in range(3)]
                for i, j, k in mine:
                    total[k, own] += jnp.dot(columns[4 * p + at], potentials[i][j, source, b], preferred_element_type=F32)
            return carry

        lax.fori_loop(lax.div(facts[5, t], 4), lax.div(facts[5, t + 1], 4), one, 0)
    nocc = out.shape[2]
    copies = [
        pltpu.make_async_copy(staged.at[k], out.at[meta[5] ^ off], osems.at[k]) for k, off in enumerate(offsets)
    ]
    for k in range(len(offsets)):
        for o in range(nown):
            for c in range(2):
                staged[k, pl.ds(o * 2 * blk + c, blk, stride=2), :] = total[k, o, :, c * nocc : (c + 1) * nocc]
        copies[k].start()
    for c in copies:
        c.wait()


def project(potentials, facts, columns, meta, before, rank, nown):
    emasks = tuple((chunk, tuple(m)) for chunk, _, m in potentials)
    nchunk = 1 + max(chunk for chunk, _, _ in potentials)
    nv, _, _, width = potentials[0][1].shape[1:]
    blk = columns.shape[1]
    ne = len(potentials)
    again = before is not None
    nk = len({mask // rank for _, masks in emasks for mask in masks})
    args = [facts, meta, columns, *[a for _, a, _ in potentials]] + ([before] if again else [])
    staged = (nk, nown * blk * 2, width // 2)
    total = (nk, nown, blk, width)
    arrays = [(a.shape, 2) for _, a, _ in potentials]
    return pl.pallas_call(
        functools.partial(project_kernel, (nchunk, emasks, rank, nown, int(again))),
        out_shape=jax.ShapeDtypeStruct((nv, nown * blk * 2, width // 2), F32),
        in_specs=[SMEM] * 2 + [VMEM] * (1 + ne) + [ANY] * int(again),
        out_specs=ANY,
        input_output_aliases={3 + ne: 0} if again else {},
        scratch_shapes=[
            pltpu.VMEM(staged, F32),
            pltpu.VMEM(total, F32),
            pltpu.SemaphoreType.DMA((nk,)),
        ],
        compiler_params=params((columns.shape, 2), (staged, 4), (total, 4), *arrays),
        name="project",
    )(*args)


def swap(array, axis, bit):
    size = lax.axis_size(axis)
    return lax.ppermute(array, axis, [(i, i ^ bit) for i in range(size)])


def across(part, bits):
    pieces = [(part, [0])]
    for bit in bits:
        for a, masks in pieces[:]:
            pieces.append((swap(a, "grid", bit), [m ^ bit for m in masks]))
    return pieces


def within(pieces, bits):
    for bit in bits:
        pieces = pieces + [(swap(a, "grid", bit), [m ^ bit for m in masks]) for a, masks in pieces]
    return pieces


def on_device(trial, occupied, colloc, blocks, coords, weights):
    n_ao, n_grid = lax.axis_size("ao"), lax.axis_size("grid")
    batches, npts, span = colloc.shape
    sig = blocks.shape[1]
    blk = span // sig
    nvec, nocc = trial.shape[1], trial.shape[3]
    nv = nvec // n_ao
    rank = n_grid // nv
    nlocal = trial.shape[0] // blk
    nown = nlocal * n_ao // n_grid
    parts = min(rank, nlocal & -nlocal)
    nb = nlocal // parts
    count = batches // 2
    ao, grid = lax.axis_index("ao"), lax.axis_index("grid")
    vector, side = grid // rank, grid % parts
    meta = jnp.stack([ao * nlocal, ao & 1, grid * nown, ao, side, vector]).astype(jnp.int32)
    high_bits = [rank << b for b in range(nv.bit_length() - 1)]
    low_bits = [1 << b for b in range(rank.bit_length() - 1)]
    part_bits = [1 << b for b in range(parts.bit_length() - 1)]

    panels = []
    far_first = list(reversed(range(n_ao)))
    for planes in (far_first[:1], far_first[1:]):
        where = jnp.stack([side * nb] + [(ao ^ over) * nv + vector for over in planes]).astype(jnp.int32)
        rows = pack(trial, where, len(planes), nb, blk)
        if not panels:
            rows, coords, weights, occupied = lax.optimization_barrier((rows, coords, weights, occupied))
        for over, one in zip(planes, rows, strict=True):
            panels.append((swap(one, "ao", over) if over else one, (over, 0)))

    near = []
    for chunk in range(2):
        part = colloc[None, chunk * count : (chunk + 1) * count]
        near.append(across(part, high_bits[::-1] if chunk else high_bits))
    far = [within(pieces, low_bits) for pieces in near]

    held, send = occupied_part(occupied, colloc, blocks, meta, blk)
    for s in range(n_ao.bit_length() - 1):
        got = swap(send, "ao", 1 << s)
        held = held + got.astype(F32)
        send = held.astype(BF16)
    other = swap(send, "ao", 1)
    whole = jnp.stack([send, other])[None]
    occ = across(whole, high_bits)

    numbers = jnp.pad(blocks.astype(F32), ((0, 0), (0, npts - sig)))
    extra = jnp.concatenate([numbers[:, None], coords, weights[:, None]], axis=1)
    extra = within(across(extra[None], high_bits), low_bits)
    fmasks = [m for _, masks in extra for m in masks]
    extra = jnp.concatenate([a for a, _ in extra], axis=0)
    ids = extra[:, :, 0, :sig].astype(jnp.int32)
    exact = extra[:nv, :, 1:]
    kern = kernel_matrix(exact[:, :, :3], exact[:, :, 3])
    group = 4 * sig
    xmasks = [m for pieces in far for _, m in pieces]
    facts = pair_list(xmasks, ids, fmasks, meta, rank, nown, 2, count, group)

    for bit in part_bits:
        panels = panels + [(swap(a, "grid", bit), (over, m ^ bit)) for a, (over, m) in panels]
    parts = potential(panels, near, occ, kern, ids, fmasks, meta, nlocal, rank)
    stages = [[], [], []]
    for chunk in range(2):
        pieces = across(parts[chunk][None], high_bits[::-1] if chunk else high_bits)
        for stage, some in enumerate((pieces[:1], pieces[1:-1], pieces[-1:])):
            stages[stage] += [(chunk, a, m) for a, m in within(some, low_bits)]
    columns = gather(far, facts, blk, 2 * rank)
    total = None
    for some in stages:
        if some:
            total = project(some, facts, columns, meta, total, rank, nown)
    return total.reshape(nv, nown * blk, 2, nocc)


def solution(mesh):
    in_specs = (
        P("ao", None, None, None),
        P("ao", None, None),
        P("grid", None, None),
        P("grid", None),
        P("grid", None, None),
        P("grid", None),
    )
    out_specs = P("ao", "grid", None, None)

    return jax.shard_map(on_device, mesh=mesh, in_specs=in_specs, out_specs=out_specs, check_vma=False)
```

```python
import functools
import math

import jax
import jax.numpy as jnp
from jax import lax
from jax.experimental import pallas as pl
from jax.experimental.pallas import tpu as pltpu
from jax.sharding import PartitionSpec as P

F32 = jnp.float32
BF16 = jnp.bfloat16
MIB = 1024 * 1024


def params(*arrays):
    total = sum(math.prod(shape) * size for shape, size in arrays)
    return pltpu.CompilerParams(vmem_limit_bytes=min(60 * MIB, total + 6 * MIB))


SMEM = pl.BlockSpec(memory_space=pltpu.SMEM)
VMEM = pl.BlockSpec(memory_space=pltpu.VMEM)
ANY = pl.BlockSpec(memory_space=pl.ANY)


def kernel_matrix(points, quad):
    differ = points[..., :, None, :] - points[..., :, :, None]
    square = jnp.sum(differ * differ, axis=-3)
    return quad[..., :, None] * quad[..., None, :] / jnp.sqrt(square + 0.25)


def selectors(blk):
    ao = lax.broadcasted_iota(jnp.int32, (blk, 2 * blk), 0)
    col = lax.broadcasted_iota(jnp.int32, (blk, 2 * blk), 1)
    return [(col == 2 * ao + c).astype(F32).astype(BF16) for c in range(2)]


def pack_kernel(where, trial, *refs):
    outs, (rows, sem) = refs[:-2], refs[-2:]
    nb, blk, width = outs[0].shape
    nocc = width // 2
    copies = []
    for i in range(len(outs)):
        for j in range(nb):
            at = (where[0] + j) * blk
            copies.append(
                pltpu.make_async_copy(trial.at[pl.ds(at, blk), where[1 + i]], rows.at[i, j], sem.at[i, j])
            )
    for c in copies:
        c.start()
    pick = jnp.concatenate(selectors(blk), axis=0)
    for i, out in enumerate(outs):
        for j in range(0, nb, 2):
            ahead = range(j, min(j + 2, nb))
            for k in ahead:
                copies[i * nb + k].wait()
            both = jnp.concatenate([rows[i, k].reshape(2 * blk, nocc) for k in ahead], axis=1)
            split = jnp.dot(pick, both, preferred_element_type=F32).astype(BF16)
            for k in ahead:
                for c in range(2):
                    piece = split[c * blk : (c + 1) * blk, (k - j) * nocc : (k - j + 1) * nocc]
                    out[k, :, c * nocc : (c + 1) * nocc] = piece


def pack(trial, where, planes, nb, blk):
    nocc = trial.shape[3]
    return pl.pallas_call(
        pack_kernel,
        out_shape=(jax.ShapeDtypeStruct((nb, blk, 2 * nocc), BF16),) * planes,
        in_specs=[SMEM, ANY],
        out_specs=(VMEM,) * planes,
        scratch_shapes=[pltpu.VMEM((planes, nb, blk, 2, nocc), BF16), pltpu.SemaphoreType.DMA((planes, nb))],
        compiler_params=pltpu.CompilerParams(vmem_limit_bytes=52 * MIB),
        name="pack",
    )(where, trial)


def occupied_kernel(ids, meta, occupied, values, keep, send, table):
    batches, sig = ids.shape
    blk, nocc = occupied.shape[0] // (table.shape[0] - 1), occupied.shape[2]
    nlocal = table.shape[0] - 1
    pick = jnp.concatenate(selectors(blk), axis=0)
    for j in range(0, nlocal, 2):
        ahead = range(j, min(j + 2, nlocal))
        both = jnp.concatenate([occupied[k * blk : (k + 1) * blk].reshape(2 * blk, nocc) for k in ahead], axis=1)
        split = jnp.dot(pick, both, preferred_element_type=F32).astype(BF16)
        for k in ahead:
            for c in range(2):
                piece = split[c * blk : (c + 1) * blk, (k - j) * nocc : (k - j + 1) * nocc]
                table[k, :, c * nocc : (c + 1) * nocc] = piece
    table[nlocal] = jnp.zeros(table.shape[1:], BF16)

    def block(b, s):
        local = ids[b, s] - meta[0]
        return table[jnp.where((local >= 0) & (local < nlocal), local, nlocal)]

    for b in range(batches):
        total = jnp.zeros(keep.shape[1:], F32)
        half, inner = divmod(b, keep.shape[0])
        for s in range(0, sig, 2):
            two = jnp.concatenate([block(b, s), block(b, s + 1)], axis=0)
            total += jnp.dot(values[b, :, s * blk : (s + 2) * blk], two, preferred_element_type=F32)

        @pl.when(meta[1] == half)
        def _(total=total, inner=inner):
            keep[inner] = total

        @pl.when(meta[1] != half)
        def _(total=total, inner=inner):
            send[inner] = total.astype(BF16)


def occupied_part(occupied, colloc, blocks, meta, blk):
    batches, npts, _ = colloc.shape
    nocc = occupied.shape[2]
    shape = (batches // 2, npts, 2 * nocc)
    return pl.pallas_call(
        occupied_kernel,
        out_shape=(jax.ShapeDtypeStruct(shape, F32), jax.ShapeDtypeStruct(shape, BF16)),
        in_specs=[SMEM, SMEM, VMEM, VMEM],
        out_specs=(VMEM, VMEM),
        scratch_shapes=[pltpu.VMEM((occupied.shape[0] // blk + 1, blk, 2 * nocc), BF16)],
        compiler_params=params((colloc.shape, 2), (occupied.shape, 4), (shape, 12), (shape, 12)),
        name="occupied",
    )(blocks, meta, occupied, colloc)


def potential_kernel(sizes, ids, meta, *refs):
    tmasks, xmasks, omasks, fmasks, nlocal, rank, nchunk = sizes
    panels, refs = refs[: len(tmasks)], refs[len(tmasks) :]
    values, refs = refs[: len(xmasks)], refs[len(xmasks) :]
    occ, refs = refs[: len(omasks)], refs[len(omasks) :]
    kern, refs = refs[0], refs[1:]
    outs, (table, x, left, m, tsems, xsems) = refs[:nchunk], refs[nchunk:]
    groups = len(values) // nchunk
    nb, blk, width = panels[0].shape
    count, npts = x.shape[1], x.shape[2]
    sig = ids.shape[2]
    copies = []
    for i, (over, side) in enumerate(tmasks):
        at = (meta[3] ^ over) * nlocal + (meta[4] ^ side) * nb
        copies.append(pltpu.make_async_copy(panels[i], table.at[pl.ds(at, nb)], tsems.at[i]))
    loads = []
    todo = []
    at = 0
    for i, piece in enumerate(values):
        loads.append(pltpu.make_async_copy(piece, x.at[pl.ds(at, piece.shape[0])], xsems.at[i]))
        for j, mask in enumerate(xmasks[i]):
            todo += [(i, i // groups, at + j, mask, b) for b in range(count)]
        at += piece.shape[0]
    for c in copies + loads:
        c.start()
    where = {mask: (i, j) for i, masks in enumerate(omasks) for j, mask in enumerate(masks)}
    dims = (((1,), (1,)), ((), ()))

    def turn_of(mask, b):
        piece, row = where[mask]
        og = occ[piece][row, meta[1] ^ (b // count), b % count]
        half = width // 2
        return jnp.concatenate([og, jnp.concatenate([-og[:, half:], og[:, :half]], axis=1)], axis=0)

    for c in copies:
        c.wait()
    seen = -1
    for i, (piece, chunk, row, mask, b) in enumerate(todo):
        if piece != seen:
            loads[piece].wait()
            seen = piece
        f = fmasks.index(mask)
        dens = jnp.zeros((npts, width), F32)
        for s in range(0, sig, 2):
            two = [table[ids[f, chunk * count + b, s + t]] for t in range(2)]
            dens += jnp.dot(
                x[row, b, :, s * blk : (s + 2) * blk], jnp.concatenate(two, axis=0), preferred_element_type=F32
            )
        left[i] = dens.astype(BF16)
    for i, (_, chunk, _, mask, b) in enumerate(todo):
        rho = lax.dot_general(left[i], turn_of(mask, chunk * count + b), dims, preferred_element_type=F32)
        weight = kern[fmasks.index(mask), chunk * count + b]
        m[i] = (rho * jnp.concatenate([weight, weight], axis=1)).astype(BF16)
    for i, (_, chunk, _, mask, b) in enumerate(todo):
        e = jnp.dot(m[i], turn_of(mask, chunk * count + b), preferred_element_type=F32)
        outs[chunk][meta[5] ^ (mask // rank), b] = e.astype(BF16)


def potential(panels, chunks, occ, kern, ids, fmasks, meta, nlocal, rank):
    tmasks = tuple(m for _, m in panels)
    nchunk = len(chunks)
    values = [piece for pieces in chunks for piece in pieces]
    xmasks = tuple(tuple(m) for _, m in values)
    omasks = tuple(tuple(m) for _, m in occ)
    count, npts, span = values[0][0].shape[1:]
    nb, blk, width = panels[0][0].shape
    nsrc = sum(len(m) for m in xmasks)
    sizes = (tmasks, xmasks, omasks, tuple(fmasks), nlocal, rank, nchunk)
    table = (len(panels) * nb, blk, width)
    x = (nsrc, count, npts, span)
    left = (nsrc * count, npts, width)
    m = (nsrc * count, npts, 2 * npts)
    return pl.pallas_call(
        functools.partial(potential_kernel, sizes),
        out_shape=(jax.ShapeDtypeStruct((nsrc // nchunk, count, npts, width), BF16),) * nchunk,
        in_specs=[SMEM, SMEM] + [VMEM] * len(panels) + [ANY] * len(values) + [VMEM] * (len(occ) + 1),
        out_specs=(VMEM,) * nchunk,
        scratch_shapes=[
            pltpu.VMEM(table, BF16),
            pltpu.VMEM(x, BF16),
            pltpu.VMEM(left, BF16),
            pltpu.VMEM(m, BF16),
            pltpu.SemaphoreType.DMA((len(panels),)),
            pltpu.SemaphoreType.DMA((len(values),)),
        ],
        compiler_params=params((table, 4), (x, 2), (left, 8), (m, 2), (kern.shape, 4)),
        name="potential",
    )(ids, meta, *[a for a, _ in panels], *[a for a, _ in values], *[a for a, _ in occ], kern)


def list_kernel(sizes, ids, meta, facts, place):
    entries, nchunk, rank, nown = sizes
    sig = ids.shape[2]
    nlist = nchunk * rank
    sizes = []
    for t in range(nlist):
        n = jnp.int32(0)
        for f, b, mask, chunk, _, _ in entries:
            if chunk * rank + mask % rank == t:
                for s in range(sig):
                    own = ids[f, b, s] - meta[2]
                    n = n + ((own >= 0) & (own < nown)).astype(jnp.int32)
        sizes.append(n)
    n = jnp.int32(0)
    for t in range(nlist):
        facts[5, t] = n
        place[t] = n
        end = n + sizes[t]
        for k in range(3):
            for f, one in enumerate((0, 0, 0, -1, 0)):
                facts[f, end + k] = jnp.int32(one)
        n = lax.div(end + 3, 4) * 4
    facts[5, nlist] = n
    for f, b, mask, chunk, row, inner in entries:
        for s in range(sig):
            own = ids[f, b, s] - meta[2]

            @pl.when((own >= 0) & (own < nown))
            def _(mask=mask, t=chunk * rank + mask % rank, row=row, inner=inner, s=s, own=own):
                to = place[t]
                place[t] = to + 1
                what = (own, meta[5] ^ (mask // rank), jnp.int32(inner), jnp.int32(row), jnp.int32(s))
                for f, one in enumerate(what):
                    facts[f, to] = one


def entries_of(xmasks, fmasks, nchunk, count):
    out = []
    at = 0
    groups = len(xmasks) // nchunk
    for i, masks in enumerate(xmasks):
        chunk = i // groups
        for j, mask in enumerate(masks):
            out += [(fmasks.index(mask), chunk * count + b, mask, chunk, at + j, b) for b in range(count)]
        at += len(masks)
    return tuple(out)


def pair_list(xmasks, ids, fmasks, meta, rank, nown, nchunk, count, group):
    nsrc, _, sig = ids.shape
    most = -(-(nchunk * (nsrc * count * sig + 3 * rank) + 4) // group) * group
    sizes = (entries_of(xmasks, fmasks, nchunk, count), nchunk, rank, nown)
    return pl.pallas_call(
        functools.partial(list_kernel, sizes),
        out_shape=jax.ShapeDtypeStruct((8, most), jnp.int32),
        in_specs=[SMEM, SMEM],
        out_specs=SMEM,
        scratch_shapes=[pltpu.SMEM((nchunk * rank,), jnp.int32)],
        compiler_params=params(),
        name="pairs",
    )(ids, meta)


def gather_kernel(nlist, facts, *refs):
    values, (columns, x, xsems) = refs[:-3], refs[-3:]
    blk = columns.shape[1]
    copies = []
    at = 0
    for i, piece in enumerate(values):
        copies.append(pltpu.make_async_copy(piece, x.at[pl.ds(at, piece.shape[0])], xsems.at[i]))
        at += piece.shape[0]
    for c in copies:
        c.start()
    for c in copies:
        c.wait()

    def one(i, carry):
        for t in range(4):
            row = facts[3, 4 * i + t]
            start = pl.multiple_of(facts[4, 4 * i + t] * blk, blk)
            column = x[jnp.maximum(row, 0), facts[2, 4 * i + t], :, pl.ds(start, blk)]
            columns[4 * i + t] = jnp.where(row >= 0, column, jnp.zeros_like(column)).T
        return carry

    lax.fori_loop(0, lax.div(facts[5, nlist], 4), one, 0)


def gather(values, facts, blk, nlist):
    flat = [a for pieces in values for a, _ in pieces]
    count, npts, span = flat[0].shape[1:]
    most = facts.shape[1]
    x = (sum(a.shape[0] for a in flat), count, npts, span)
    large = most * blk * npts * 2 > 16 * MIB
    return pl.pallas_call(
        functools.partial(gather_kernel, nlist),
        out_shape=jax.ShapeDtypeStruct((most, blk, npts), BF16),
        in_specs=[SMEM] + [ANY] * len(flat),
        out_specs=VMEM,
        scratch_shapes=[pltpu.VMEM(x, BF16), pltpu.SemaphoreType.DMA((len(flat),))],
        compiler_params=params((x, 2), ((most if large else 0, blk, npts), 2)),
        name="gather",
    )(facts, *flat)


def project_kernel(sizes, facts, meta, columns, *refs):
    nchunk, emasks, rank, nown, again = sizes
    ne = len(emasks)
    potentials, refs = refs[:ne], refs[ne + again :]
    out, staged, total, osems = refs
    blk = columns.shape[1]
    offsets = sorted({mask // rank for _, masks in emasks for mask in masks})
    total[...] = jnp.zeros_like(total)
    for t in range(nchunk * rank):
        mine = [
            (i, j, offsets.index(mask // rank))
            for i, (chunk, masks) in enumerate(emasks)
            for j, mask in enumerate(masks)
            if chunk * rank + mask % rank == t
        ]

        def one(p, carry, mine=mine):
            for at in range(4):
                own, source, b = [facts[f, 4 * p + at] for f in range(3)]
                for i, j, k in mine:
                    total[k, own] += jnp.dot(columns[4 * p + at], potentials[i][j, source, b], preferred_element_type=F32)
            return carry

        lax.fori_loop(lax.div(facts[5, t], 4), lax.div(facts[5, t + 1], 4), one, 0)
    nocc = out.shape[2]
    copies = [
        pltpu.make_async_copy(staged.at[k], out.at[meta[5] ^ off], osems.at[k]) for k, off in enumerate(offsets)
    ]
    for k in range(len(offsets)):
        for o in range(nown):
            for c in range(2):
                staged[k, pl.ds(o * 2 * blk + c, blk, stride=2), :] = total[k, o, :, c * nocc : (c + 1) * nocc]
        copies[k].start()
    for c in copies:
        c.wait()


def project(potentials, facts, columns, meta, before, rank, nown):
    emasks = tuple((chunk, tuple(m)) for chunk, _, m in potentials)
    nchunk = 1 + max(chunk for chunk, _, _ in potentials)
    nv, _, _, width = potentials[0][1].shape[1:]
    blk = columns.shape[1]
    ne = len(potentials)
    again = before is not None
    nk = len({mask // rank for _, masks in emasks for mask in masks})
    args = [facts, meta, columns, *[a for _, a, _ in potentials]] + ([before] if again else [])
    staged = (nk, nown * blk * 2, width // 2)
    total = (nk, nown, blk, width)
    arrays = [(a.shape, 2) for _, a, _ in potentials]
    return pl.pallas_call(
        functools.partial(project_kernel, (nchunk, emasks, rank, nown, int(again))),
        out_shape=jax.ShapeDtypeStruct((nv, nown * blk * 2, width // 2), F32),
        in_specs=[SMEM] * 2 + [VMEM] * (1 + ne) + [ANY] * int(again),
        out_specs=ANY,
        input_output_aliases={3 + ne: 0} if again else {},
        scratch_shapes=[
            pltpu.VMEM(staged, F32),
            pltpu.VMEM(total, F32),
            pltpu.SemaphoreType.DMA((nk,)),
        ],
        compiler_params=params((columns.shape, 2), (staged, 4), (total, 4), *arrays),
        name="project",
    )(*args)


def swap(array, axis, bit):
    size = lax.axis_size(axis)
    return lax.ppermute(array, axis, [(i, i ^ bit) for i in range(size)])


def across(part, bits):
    pieces = [(part, [0])]
    for bit in bits:
        for a, masks in pieces[:]:
            pieces.append((swap(a, "grid", bit), [m ^ bit for m in masks]))
    return pieces


def within(pieces, bits):
    for bit in bits:
        pieces = pieces + [(swap(a, "grid", bit), [m ^ bit for m in masks]) for a, masks in pieces]
    return pieces


def on_device(trial, occupied, colloc, blocks, coords, weights):
    n_ao, n_grid = lax.axis_size("ao"), lax.axis_size("grid")
    batches, npts, span = colloc.shape
    sig = blocks.shape[1]
    blk = span // sig
    nvec, nocc = trial.shape[1], trial.shape[3]
    nv = nvec // n_ao
    rank = n_grid // nv
    nlocal = trial.shape[0] // blk
    nown = nlocal * n_ao // n_grid
    parts = min(rank, nlocal & -nlocal)
    nb = nlocal // parts
    count = batches // 2
    ao, grid = lax.axis_index("ao"), lax.axis_index("grid")
    vector, side = grid // rank, grid % parts
    meta = jnp.stack([ao * nlocal, ao & 1, grid * nown, ao, side, vector]).astype(jnp.int32)
    high_bits = [rank << b for b in range(nv.bit_length() - 1)]
    low_bits = [1 << b for b in range(rank.bit_length() - 1)]
    part_bits = [1 << b for b in range(parts.bit_length() - 1)]

    panels = []
    far_first = list(reversed(range(n_ao)))
    for planes in (far_first[:1], far_first[1:]):
        where = jnp.stack([side * nb] + [(ao ^ over) * nv + vector for over in planes]).astype(jnp.int32)
        rows = pack(trial, where, len(planes), nb, blk)
        if not panels:
            rows, coords, weights, occupied = lax.optimization_barrier((rows, coords, weights, occupied))
        for over, one in zip(planes, rows, strict=True):
            panels.append((swap(one, "ao", over) if over else one, (over, 0)))

    near = []
    for chunk in range(2):
        part = colloc[None, chunk * count : (chunk + 1) * count]
        near.append(across(part, high_bits[::-1] if chunk else high_bits))
    far = [within(pieces, low_bits) for pieces in near]

    held, send = occupied_part(occupied, colloc, blocks, meta, blk)
    for s in range(n_ao.bit_length() - 1):
        got = swap(send, "ao", 1 << s)
        held = held + got.astype(F32)
        send = held.astype(BF16)
    other = swap(send, "ao", 1)
    whole = jnp.stack([send, other])[None]
    occ = across(whole, high_bits)

    numbers = jnp.pad(blocks.astype(F32), ((0, 0), (0, npts - sig)))
    extra = jnp.concatenate([numbers[:, None], coords, weights[:, None]], axis=1)
    extra = within(across(extra[None], high_bits), low_bits)
    fmasks = [m for _, masks in extra for m in masks]
    extra = jnp.concatenate([a for a, _ in extra], axis=0)
    ids = extra[:, :, 0, :sig].astype(jnp.int32)
    exact = extra[:nv, :, 1:]
    kern = kernel_matrix(exact[:, :, :3], exact[:, :, 3])
    group = 4 * sig
    xmasks = [m for pieces in far for _, m in pieces]
    facts = pair_list(xmasks, ids, fmasks, meta, rank, nown, 2, count, group)

    for bit in part_bits:
        panels = panels + [(swap(a, "grid", bit), (over, m ^ bit)) for a, (over, m) in panels]
    parts = potential(panels, near, occ, kern, ids, fmasks, meta, nlocal, rank)
    stages = [[], [], []]
    for chunk in range(2):
        pieces = across(parts[chunk][None], high_bits[::-1] if chunk else high_bits)
        for stage, some in enumerate((pieces[:1], pieces[1:-1], pieces[-1:])):
            stages[stage] += [(chunk, a, m) for a, m in within(some, low_bits)]
    columns = gather(far, facts, blk, 2 * rank)
    total = None
    for some in stages:
        if some:
            total = project(some, facts, columns, meta, total, rank, nown)
    return total.reshape(nv, nown * blk, 2, nocc)


def solution(mesh):
    in_specs = (
        P("ao", None, None, None),
        P("ao", None, None),
        P("grid", None, None),
        P("grid", None),
        P("grid", None, None),
        P("grid", None),
    )
    out_specs = P("ao", "grid", None, None)

    return jax.shard_map(on_device, mesh=mesh, in_specs=in_specs, out_specs=out_specs, check_vma=False)
```

```python
import functools
import math

import jax
import jax.numpy as jnp
from jax import lax
from jax.experimental import pallas as pl
from jax.experimental.pallas import tpu as pltpu
from jax.sharding import PartitionSpec as P

F32 = jnp.float32
BF16 = jnp.bfloat16
MIB = 1024 * 1024


def params(*arrays):
    total = sum(math.prod(shape) * size for shape, size in arrays)
    return pltpu.CompilerParams(vmem_limit_bytes=min(60 * MIB, total + 6 * MIB))


SMEM = pl.BlockSpec(memory_space=pltpu.SMEM)
VMEM = pl.BlockSpec(memory_space=pltpu.VMEM)
ANY = pl.BlockSpec(memory_space=pl.ANY)


def kernel_matrix(points, quad):
    differ = points[..., :, None, :] - points[..., :, :, None]
    square = jnp.sum(differ * differ, axis=-3)
    return quad[..., :, None] * quad[..., None, :] / jnp.sqrt(square + 0.25)


def selectors(blk):
    ao = lax.broadcasted_iota(jnp.int32, (blk, 2 * blk), 0)
    col = lax.broadcasted_iota(jnp.int32, (blk, 2 * blk), 1)
    return [(col == 2 * ao + c).astype(F32).astype(BF16) for c in range(2)]


def pack_kernel(where, trial, *refs):
    outs, (rows, sem) = refs[:-2], refs[-2:]
    nb, blk, width = outs[0].shape
    nocc = width // 2
    copies = []
    for i in range(len(outs)):
        for j in range(nb):
            at = (where[0] + j) * blk
            copies.append(
                pltpu.make_async_copy(trial.at[pl.ds(at, blk), where[1 + i]], rows.at[i, j], sem.at[i, j])
            )
    for c in copies:
        c.start()
    pick = jnp.concatenate(selectors(blk), axis=0)
    for i, out in enumerate(outs):
        for j in range(0, nb, 2):
            ahead = range(j, min(j + 2, nb))
            for k in ahead:
                copies[i * nb + k].wait()
            both = jnp.concatenate([rows[i, k].reshape(2 * blk, nocc) for k in ahead], axis=1)
            split = jnp.dot(pick, both, preferred_element_type=F32).astype(BF16)
            for k in ahead:
                for c in range(2):
                    piece = split[c * blk : (c + 1) * blk, (k - j) * nocc : (k - j + 1) * nocc]
                    out[k, :, c * nocc : (c + 1) * nocc] = piece


def pack(trial, where, planes, nb, blk):
    nocc = trial.shape[3]
    return pl.pallas_call(
        pack_kernel,
        out_shape=(jax.ShapeDtypeStruct((nb, blk, 2 * nocc), BF16),) * planes,
        in_specs=[SMEM, ANY],
        out_specs=(VMEM,) * planes,
        scratch_shapes=[pltpu.VMEM((planes, nb, blk, 2, nocc), BF16), pltpu.SemaphoreType.DMA((planes, nb))],
        compiler_params=pltpu.CompilerParams(vmem_limit_bytes=52 * MIB),
        name="pack",
    )(where, trial)


def occupied_kernel(ids, meta, occupied, values, keep, send, table):
    batches, sig = ids.shape
    blk, nocc = occupied.shape[0] // (table.shape[0] - 1), occupied.shape[2]
    nlocal = table.shape[0] - 1
    pick = jnp.concatenate(selectors(blk), axis=0)
    for j in range(0, nlocal, 2):
        ahead = range(j, min(j + 2, nlocal))
        both = jnp.concatenate([occupied[k * blk : (k + 1) * blk].reshape(2 * blk, nocc) for k in ahead], axis=1)
        split = jnp.dot(pick, both, preferred_element_type=F32).astype(BF16)
        for k in ahead:
            for c in range(2):
                piece = split[c * blk : (c + 1) * blk, (k - j) * nocc : (k - j + 1) * nocc]
                table[k, :, c * nocc : (c + 1) * nocc] = piece
    table[nlocal] = jnp.zeros(table.shape[1:], BF16)

    def block(b, s):
        local = ids[b, s] - meta[0]
        return table[jnp.where((local >= 0) & (local < nlocal), local, nlocal)]

    for b in range(batches):
        total = jnp.zeros(keep.shape[1:], F32)
        half, inner = divmod(b, keep.shape[0])
        for s in range(0, sig, 2):
            two = jnp.concatenate([block(b, s), block(b, s + 1)], axis=0)
            total += jnp.dot(values[b, :, s * blk : (s + 2) * blk], two, preferred_element_type=F32)

        @pl.when(meta[1] == half)
        def _(total=total, inner=inner):
            keep[inner] = total

        @pl.when(meta[1] != half)
        def _(total=total, inner=inner):
            send[inner] = total.astype(BF16)


def occupied_part(occupied, colloc, blocks, meta, blk):
    batches, npts, _ = colloc.shape
    nocc = occupied.shape[2]
    shape = (batches // 2, npts, 2 * nocc)
    return pl.pallas_call(
        occupied_kernel,
        out_shape=(jax.ShapeDtypeStruct(shape, F32), jax.ShapeDtypeStruct(shape, BF16)),
        in_specs=[SMEM, SMEM, VMEM, VMEM],
        out_specs=(VMEM, VMEM),
        scratch_shapes=[pltpu.VMEM((occupied.shape[0] // blk + 1, blk, 2 * nocc), BF16)],
        compiler_params=params((colloc.shape, 2), (occupied.shape, 4), (shape, 12), (shape, 12)),
        name="occupied",
    )(blocks, meta, occupied, colloc)


def potential_kernel(sizes, ids, meta, *refs):
    tmasks, xmasks, omasks, fmasks, nlocal, rank, nchunk = sizes
    panels, refs = refs[: len(tmasks)], refs[len(tmasks) :]
    values, refs = refs[: len(xmasks)], refs[len(xmasks) :]
    occ, refs = refs[: len(omasks)], refs[len(omasks) :]
    kern, refs = refs[0], refs[1:]
    outs, (table, x, left, m, tsems, xsems) = refs[:nchunk], refs[nchunk:]
    groups = len(values) // nchunk
    blk, width = panels[0].shape[1:]
    nb = nlocal // (1 + max(side for _, side, _ in tmasks))
    count, npts = x.shape[1], x.shape[2]
    sig = ids.shape[2]
    copies = []
    for i, (over, side, off) in enumerate(tmasks):
        at = (meta[3] ^ over) * nlocal + (meta[4] ^ side) * nb + off
        size = panels[i].shape[0]
        copies.append(pltpu.make_async_copy(panels[i], table.at[pl.ds(at, size)], tsems.at[i]))
    loads = []
    todo = []
    at = 0
    for i, piece in enumerate(values):
        loads.append(pltpu.make_async_copy(piece, x.at[pl.ds(at, piece.shape[0])], xsems.at[i]))
        for j, mask in enumerate(xmasks[i]):
            todo += [(i, i // groups, at + j, mask, b) for b in range(count)]
        at += piece.shape[0]
    for c in copies + loads:
        c.start()
    where = {mask: (i, j) for i, masks in enumerate(omasks) for j, mask in enumerate(masks)}
    dims = (((1,), (1,)), ((), ()))

    def turn_of(mask, b):
        piece, row = where[mask]
        og = occ[piece][row, meta[1] ^ (b // count), b % count]
        half = width // 2
        return jnp.concatenate([og, jnp.concatenate([-og[:, half:], og[:, :half]], axis=1)], axis=0)

    for c in copies:
        c.wait()
    seen = -1
    for i, (piece, chunk, row, mask, b) in enumerate(todo):
        if piece != seen:
            loads[piece].wait()
            seen = piece
        f = fmasks.index(mask)
        dens = jnp.zeros((npts, width), F32)
        for s in range(0, sig, 2):
            two = [table[ids[f, chunk * count + b, s + t]] for t in range(2)]
            dens += jnp.dot(
                x[row, b, :, s * blk : (s + 2) * blk], jnp.concatenate(two, axis=0), preferred_element_type=F32
            )
        left[i] = dens.astype(BF16)
    for i, (_, chunk, _, mask, b) in enumerate(todo):
        rho = lax.dot_general(left[i], turn_of(mask, chunk * count + b), dims, preferred_element_type=F32)
        weight = kern[fmasks.index(mask), chunk * count + b]
        m[i] = (rho * jnp.concatenate([weight, weight], axis=1)).astype(BF16)
    for i, (_, chunk, _, mask, b) in enumerate(todo):
        e = jnp.dot(m[i], turn_of(mask, chunk * count + b), preferred_element_type=F32)
        outs[chunk][meta[5] ^ (mask // rank), b] = e.astype(BF16)


def potential(panels, chunks, occ, kern, ids, fmasks, meta, nlocal, rank):
    tmasks = tuple(m for _, m in panels)
    nchunk = len(chunks)
    values = [piece for pieces in chunks for piece in pieces]
    xmasks = tuple(tuple(m) for _, m in values)
    omasks = tuple(tuple(m) for _, m in occ)
    count, npts, span = values[0][0].shape[1:]
    blk, width = panels[0][0].shape[1:]
    nsrc = sum(len(m) for m in xmasks)
    sizes = (tmasks, xmasks, omasks, tuple(fmasks), nlocal, rank, nchunk)
    table = (sum(a.shape[0] for a, _ in panels), blk, width)
    x = (nsrc, count, npts, span)
    left = (nsrc * count, npts, width)
    m = (nsrc * count, npts, 2 * npts)
    return pl.pallas_call(
        functools.partial(potential_kernel, sizes),
        out_shape=(jax.ShapeDtypeStruct((nsrc // nchunk, count, npts, width), BF16),) * nchunk,
        in_specs=[SMEM, SMEM] + [VMEM] * len(panels) + [ANY] * len(values) + [VMEM] * (len(occ) + 1),
        out_specs=(VMEM,) * nchunk,
        scratch_shapes=[
            pltpu.VMEM(table, BF16),
            pltpu.VMEM(x, BF16),
            pltpu.VMEM(left, BF16),
            pltpu.VMEM(m, BF16),
            pltpu.SemaphoreType.DMA((len(panels),)),
            pltpu.SemaphoreType.DMA((len(values),)),
        ],
        compiler_params=params((table, 4), (x, 2), (left, 8), (m, 2), (kern.shape, 4)),
        name="potential",
    )(ids, meta, *[a for a, _ in panels], *[a for a, _ in values], *[a for a, _ in occ], kern)


def list_kernel(sizes, ids, meta, facts, place):
    entries, nchunk, rank, nown = sizes
    sig = ids.shape[2]
    nlist = nchunk * rank
    sizes = []
    for t in range(nlist):
        n = jnp.int32(0)
        for f, b, mask, chunk, _, _ in entries:
            if chunk * rank + mask % rank == t:
                for s in range(sig):
                    own = ids[f, b, s] - meta[2]
                    n = n + ((own >= 0) & (own < nown)).astype(jnp.int32)
        sizes.append(n)
    n = jnp.int32(0)
    for t in range(nlist):
        facts[5, t] = n
        place[t] = n
        end = n + sizes[t]
        for k in range(3):
            for f, one in enumerate((0, 0, 0, -1, 0)):
                facts[f, end + k] = jnp.int32(one)
        n = lax.div(end + 3, 4) * 4
    facts[5, nlist] = n
    for f, b, mask, chunk, row, inner in entries:
        for s in range(sig):
            own = ids[f, b, s] - meta[2]

            @pl.when((own >= 0) & (own < nown))
            def _(mask=mask, t=chunk * rank + mask % rank, row=row, inner=inner, s=s, own=own):
                to = place[t]
                place[t] = to + 1
                what = (own, meta[5] ^ (mask // rank), jnp.int32(inner), jnp.int32(row), jnp.int32(s))
                for f, one in enumerate(what):
                    facts[f, to] = one


def entries_of(xmasks, fmasks, nchunk, count):
    out = []
    at = 0
    groups = len(xmasks) // nchunk
    for i, masks in enumerate(xmasks):
        chunk = i // groups
        for j, mask in enumerate(masks):
            out += [(fmasks.index(mask), chunk * count + b, mask, chunk, at + j, b) for b in range(count)]
        at += len(masks)
    return tuple(out)


def pair_list(xmasks, ids, fmasks, meta, rank, nown, nchunk, count, group):
    nsrc, _, sig = ids.shape
    most = -(-(nchunk * (nsrc * count * sig + 3 * rank) + 4) // group) * group
    sizes = (entries_of(xmasks, fmasks, nchunk, count), nchunk, rank, nown)
    return pl.pallas_call(
        functools.partial(list_kernel, sizes),
        out_shape=jax.ShapeDtypeStruct((8, most), jnp.int32),
        in_specs=[SMEM, SMEM],
        out_specs=SMEM,
        scratch_shapes=[pltpu.SMEM((nchunk * rank,), jnp.int32)],
        compiler_params=params(),
        name="pairs",
    )(ids, meta)


def gather_kernel(nlist, facts, *refs):
    values, (columns, x, xsems) = refs[:-3], refs[-3:]
    blk = columns.shape[1]
    copies = []
    at = 0
    for i, piece in enumerate(values):
        copies.append(pltpu.make_async_copy(piece, x.at[pl.ds(at, piece.shape[0])], xsems.at[i]))
        at += piece.shape[0]
    for c in copies:
        c.start()
    for c in copies:
        c.wait()

    def one(i, carry):
        for t in range(4):
            row = facts[3, 4 * i + t]
            start = pl.multiple_of(facts[4, 4 * i + t] * blk, blk)
            column = x[jnp.maximum(row, 0), facts[2, 4 * i + t], :, pl.ds(start, blk)]
            columns[4 * i + t] = jnp.where(row >= 0, column, jnp.zeros_like(column)).T
        return carry

    lax.fori_loop(0, lax.div(facts[5, nlist], 4), one, 0)


def gather(values, facts, blk, nlist):
    flat = [a for pieces in values for a, _ in pieces]
    count, npts, span = flat[0].shape[1:]
    most = facts.shape[1]
    x = (sum(a.shape[0] for a in flat), count, npts, span)
    large = most * blk * npts * 2 > 16 * MIB
    return pl.pallas_call(
        functools.partial(gather_kernel, nlist),
        out_shape=jax.ShapeDtypeStruct((most, blk, npts), BF16),
        in_specs=[SMEM] + [ANY] * len(flat),
        out_specs=VMEM,
        scratch_shapes=[pltpu.VMEM(x, BF16), pltpu.SemaphoreType.DMA((len(flat),))],
        compiler_params=params((x, 2), ((most if large else 0, blk, npts), 2)),
        name="gather",
    )(facts, *flat)


def project_kernel(sizes, facts, meta, columns, *refs):
    nchunk, emasks, rank, nown, again = sizes
    ne = len(emasks)
    potentials, refs = refs[:ne], refs[ne + again :]
    out, staged, total, osems = refs
    blk = columns.shape[1]
    offsets = sorted({mask // rank for _, masks in emasks for mask in masks})
    total[...] = jnp.zeros_like(total)
    for t in range(nchunk * rank):
        mine = [
            (i, j, offsets.index(mask // rank))
            for i, (chunk, masks) in enumerate(emasks)
            for j, mask in enumerate(masks)
            if chunk * rank + mask % rank == t
        ]

        def one(p, carry, mine=mine):
            for at in range(4):
                own, source, b = [facts[f, 4 * p + at] for f in range(3)]
                for i, j, k in mine:
                    total[k, own] += jnp.dot(columns[4 * p + at], potentials[i][j, source, b], preferred_element_type=F32)
            return carry

        lax.fori_loop(lax.div(facts[5, t], 4), lax.div(facts[5, t + 1], 4), one, 0)
    nocc = out.shape[2]
    copies = [
        pltpu.make_async_copy(staged.at[k], out.at[meta[5] ^ off], osems.at[k]) for k, off in enumerate(offsets)
    ]
    for k in range(len(offsets)):
        for o in range(nown):
            for c in range(2):
                staged[k, pl.ds(o * 2 * blk + c, blk, stride=2), :] = total[k, o, :, c * nocc : (c + 1) * nocc]
        copies[k].start()
    for c in copies:
        c.wait()


def project(potentials, facts, columns, meta, before, rank, nown):
    emasks = tuple((chunk, tuple(m)) for chunk, _, m in potentials)
    nchunk = 1 + max(chunk for chunk, _, _ in potentials)
    nv, _, _, width = potentials[0][1].shape[1:]
    blk = columns.shape[1]
    ne = len(potentials)
    again = before is not None
    nk = len({mask // rank for _, masks in emasks for mask in masks})
    args = [facts, meta, columns, *[a for _, a, _ in potentials]] + ([before] if again else [])
    staged = (nk, nown * blk * 2, width // 2)
    total = (nk, nown, blk, width)
    arrays = [(a.shape, 2) for _, a, _ in potentials]
    return pl.pallas_call(
        functools.partial(project_kernel, (nchunk, emasks, rank, nown, int(again))),
        out_shape=jax.ShapeDtypeStruct((nv, nown * blk * 2, width // 2), F32),
        in_specs=[SMEM] * 2 + [VMEM] * (1 + ne) + [ANY] * int(again),
        out_specs=ANY,
        input_output_aliases={3 + ne: 0} if again else {},
        scratch_shapes=[
            pltpu.VMEM(staged, F32),
            pltpu.VMEM(total, F32),
            pltpu.SemaphoreType.DMA((nk,)),
        ],
        compiler_params=params((columns.shape, 2), (staged, 4), (total, 4), *arrays),
        name="project",
    )(*args)


def swap(array, axis, bit):
    size = lax.axis_size(axis)
    return lax.ppermute(array, axis, [(i, i ^ bit) for i in range(size)])


def across(part, bits):
    pieces = [(part, [0])]
    for bit in bits:
        for a, masks in pieces[:]:
            pieces.append((swap(a, "grid", bit), [m ^ bit for m in masks]))
    return pieces


def within(pieces, bits):
    for bit in bits:
        pieces = pieces + [(swap(a, "grid", bit), [m ^ bit for m in masks]) for a, masks in pieces]
    return pieces


def on_device(trial, occupied, colloc, blocks, coords, weights):
    n_ao, n_grid = lax.axis_size("ao"), lax.axis_size("grid")
    batches, npts, span = colloc.shape
    sig = blocks.shape[1]
    blk = span // sig
    nvec, nocc = trial.shape[1], trial.shape[3]
    nv = nvec // n_ao
    rank = n_grid // nv
    nlocal = trial.shape[0] // blk
    nown = nlocal * n_ao // n_grid
    parts = min(rank, nlocal & -nlocal)
    nb = nlocal // parts
    count = batches // 2
    ao, grid = lax.axis_index("ao"), lax.axis_index("grid")
    vector, side = grid // rank, grid % parts
    meta = jnp.stack([ao * nlocal, ao & 1, grid * nown, ao, side, vector]).astype(jnp.int32)
    high_bits = [rank << b for b in range(nv.bit_length() - 1)]
    low_bits = [1 << b for b in range(rank.bit_length() - 1)]
    part_bits = [1 << b for b in range(parts.bit_length() - 1)]

    panels = []
    far_first = list(reversed(range(n_ao)))
    early = max(1, nb // 4)
    jobs = [(far_first[:1], 0, early), (far_first[:1], early, nb - early), (far_first[1:], 0, nb)]
    for i, (planes, off, size) in enumerate(jobs):
        where = jnp.stack([side * nb + off] + [(ao ^ over) * nv + vector for over in planes]).astype(jnp.int32)
        rows = pack(trial, where, len(planes), size, blk)
        if i == 0:
            rows, coords, weights, occupied = lax.optimization_barrier((rows, coords, weights, occupied))
        for over, one in zip(planes, rows, strict=True):
            name = str(over) if i else "f"
            panels.append((swap(one, "ao", over) if over else one, (over, 0, off), name))

    near = []
    for chunk in range(2):
        part = colloc[None, chunk * count : (chunk + 1) * count]
        near.append(across(part, high_bits[::-1] if chunk else high_bits))
    far = [within(pieces, low_bits) for pieces in near]

    held, send = occupied_part(occupied, colloc, blocks, meta, blk)
    for s in range(n_ao.bit_length() - 1):
        got = swap(send, "ao", 1 << s)
        held = held + got.astype(F32)
        send = held.astype(BF16)
    other = swap(send, "ao", 1)
    whole = jnp.stack([send, other])[None]
    occ = across(whole, high_bits)

    numbers = jnp.pad(blocks.astype(F32), ((0, 0), (0, npts - sig)))
    extra = jnp.concatenate([numbers[:, None], coords, weights[:, None]], axis=1)
    extra = within(across(extra[None], high_bits), low_bits)
    fmasks = [m for _, masks in extra for m in masks]
    extra = jnp.concatenate([a for a, _ in extra], axis=0)
    ids = extra[:, :, 0, :sig].astype(jnp.int32)
    exact = extra[:nv, :, 1:]
    kern = kernel_matrix(exact[:, :, :3], exact[:, :, 3])
    group = 4 * sig
    xmasks = [m for pieces in far for _, m in pieces]
    facts = pair_list(xmasks, ids, fmasks, meta, rank, nown, 2, count, group)

    for bit in part_bits:
        panels = panels + [(swap(x, "grid", bit), (over, m ^ bit, off), name) for x, (over, m, off), name in panels]
    panels = [(x, what) for x, what, _ in panels]
    parts = potential(panels, near, occ, kern, ids, fmasks, meta, nlocal, rank)
    stages = [[], [], []]
    for chunk in range(2):
        pieces = across(parts[chunk][None], high_bits[::-1] if chunk else high_bits)
        for stage, some in enumerate((pieces[:1], pieces[1:-1], pieces[-1:])):
            stages[stage] += [(chunk, a, m) for a, m in within(some, low_bits)]
    columns = gather(far, facts, blk, 2 * rank)
    total = None
    for some in stages:
        if some:
            total = project(some, facts, columns, meta, total, rank, nown)
    return total.reshape(nv, nown * blk, 2, nocc)


def solution(mesh):
    in_specs = (
        P("ao", None, None, None),
        P("ao", None, None),
        P("grid", None, None),
        P("grid", None),
        P("grid", None, None),
        P("grid", None),
    )
    out_specs = P("ao", "grid", None, None)

    return jax.shard_map(on_device, mesh=mesh, in_specs=in_specs, out_specs=out_specs, check_vma=False)
```
